128 devices in a mesh: ctx: 8 (over z_lo, x), ch: 16 (over y, z_hi, core).
Axes of the slice: x: 4, y: 4, z: 4 (z_hi: 2, z_lo: 2; z = z_hi * 2 + z_lo), core: 2. Of those that a mesh axis runs over, the one named last changes fastest.
Arguments:
- features: bfloat16 [8192, 3, 8192], P('ctx', None, 'ch'), may hold values from -6 to 6
- short_filter: float32 [3, 3, 8192], P(None, None, 'ch'), may hold values from -3 to 3
- decay_rate: float32 [16, 8192], P(None, 'ch'), may hold values from 6.1035156e-06 to 0.0333333333
- residues: float32 [16, 8192], P(None, 'ch'), may hold values from -0.2581989 to 0.2581989
- out_weight: bfloat16 [8192, 8192], P('ch'), may hold values from -0.09375 to 0.09375
Outputs:
- mixed_out: bfloat16 [8192, 8192], P('ctx', 'ch')
The draws below stay inside these ranges and needn't reach their ends.
All inputs are finite; a program needn't handle non-finite values.
Results may differ from the reference program's by a relative error of at most 0.02.
Values may be sent and summed in bfloat16 or wider, within the bound.
No kernel may reach another device: no remote copies, remote signals or barrier semaphores. Data moves between devices by JAX's collectives and lax.ppermute only.
A program may use at most 128 MiB of HBM per device.

```python
import jax
import jax.numpy as jnp
from jax import lax

D = 8192
ORDER = 16
TOKENS = 8192
N_CH = 16


def rate_law(key):
    first_key = jax.random.fold_in(jax.random.fold_in(key, 11), 0)
    low_end = jnp.log(0.05 / TOKENS)
    high_end = jnp.log(1.0 / 30.0)
    uniform_part = jax.random.uniform(first_key, (ORDER, D), jnp.float32)
    log_rate = low_end + uniform_part * (high_end - low_end)
    return jnp.clip(jnp.exp(log_rate), 0.05 / TOKENS, 1.0 / 30.0)


def draw_decay_rate(key, part):
    return rate_law(key)


def draw_residues(key, part):
    rate_now = rate_law(key)
    normal_part = jnp.clip(jax.random.normal(jax.random.fold_in(key, 23), (ORDER, D), jnp.float32), -4.0, 4.0)
    scale_now = jnp.sqrt(jnp.maximum(2.0 * rate_now, 1.0 / TOKENS) / ORDER)
    return normal_part * scale_now


def raised(drawn, rng, source, target, parts, factor):
    def block_of(axis_at):
        return (jnp.arange(drawn.shape[axis_at]) // (drawn.shape[axis_at] // parts)).reshape((-1,) + (1,) * (drawn.ndim - 1 - axis_at))

    near = jax.random.permutation(rng, parts)[block_of(target)]
    other_side = (block_of(target) + parts // 2) % parts
    return jnp.where((block_of(source) == near) | (block_of(source) == other_side), factor * drawn, drawn)


def block_levels(stream_key, extent, pieces, least, largest):
    factor_of, own = 1.0, jax.random.fold_in(stream_key, 6)
    for dim, parts in pieces:
        steps = jnp.exp(jax.random.uniform(jax.random.fold_in(own, dim), (parts,), jnp.float32, least / len(pieces), largest / len(pieces)))
        factor_of = factor_of * jnp.repeat(steps, extent[dim] // parts).reshape([-1 if axis == dim else 1 for axis in range(len(extent))])
    return factor_of


def bell_draw(own_key, dims, scale, reach, shards=(), held_as=jnp.bfloat16):
    entries = scale * jax.random.normal(own_key, dims, jnp.float32)
    if shards:
        entries = entries * block_levels(own_key, dims, shards, -0.22, 0.18)
    return jnp.clip(entries, -reach, reach).astype(held_as)


def noise_with(stream_key, dims, spread, limit, cuts, heavy, kind=jnp.bfloat16):
    result = spread * jax.random.normal(stream_key, dims, jnp.float32)
    if cuts:
        result = result * block_levels(stream_key, dims, cuts, -0.22, 0.18)
    return jnp.clip(raised(result, jax.random.fold_in(stream_key, 3), *heavy), -limit, limit).astype(kind)


def setup_inputs(seed: int = 0) -> dict:
    key_list = jax.random.split(jax.random.key(seed), 6)
    return {
        "features": bell_draw(key_list[0], (TOKENS, 3, D), 1.0, 6.0, ((0, 8), (2, 16))),
        "short_filter": bell_draw(key_list[1], (3, 3, D), 0.6, 3.0, ((2, 16),), jnp.float32),
        "decay_rate": draw_decay_rate(jax.random.fold_in(key_list[5], 71), 0),
        "residues": draw_residues(jax.random.fold_in(key_list[5], 71), 0),
        "out_weight": noise_with(key_list[4], (D, D), D ** -0.5, 0.09375, ((0, 16),), (0, 1, 16, 2.0)),
    }


def reference(features, short_filter, decay_rate, residues, out_weight):
    inputs_f = features.astype(jnp.float32)
    padded = jnp.concatenate([jnp.zeros((2, 3, D), jnp.float32), inputs_f], axis=0)
    featured = short_filter[0][None] * padded[2:] + short_filter[1][None] * padded[1:TOKENS + 1] + short_filter[2][None] * padded[:TOKENS]
    product = (featured[:, 1] * featured[:, 2]).astype(jnp.bfloat16)
    chan_block = D // N_CH
    positions = jnp.arange(TOKENS).astype(jnp.float32)
    rate_blocks = decay_rate.reshape(ORDER, N_CH, chan_block).transpose(1, 0, 2)
    res_blocks = residues.reshape(ORDER, N_CH, chan_block).transpose(1, 0, 2)
    prod_blocks = product.astype(jnp.float32).reshape(TOKENS, N_CH, chan_block).transpose(1, 0, 2)
    fft_len = 2 * TOKENS

    def one_block(packed):
        rate_b, res_b, prod_b = packed
        filter_full = jnp.zeros((TOKENS, chan_block), jnp.float32)
        for mode in range(ORDER):
            filter_full = filter_full + res_b[mode][None] * jnp.exp(-rate_b[mode][None] * positions[:, None])
        z_freq = jnp.fft.rfft(prod_b, fft_len, axis=0)
        h_freq = jnp.fft.rfft(filter_full, fft_len, axis=0)
        return jnp.fft.irfft(z_freq * h_freq, fft_len, axis=0)[:TOKENS]

    conv_blocks = lax.map(one_block, (rate_blocks, res_blocks, prod_blocks))
    conv_out = conv_blocks.transpose(1, 0, 2).reshape(TOKENS, D)
    gated_out = (featured[:, 0] * conv_out).astype(jnp.bfloat16)
    return jnp.dot(gated_out, out_weight, preferred_element_type=jnp.float32).astype(jnp.bfloat16)
```

```python
import jax
import jax.numpy as jnp
from jax import lax
from jax.experimental import pallas as pl
from jax.experimental.pallas import tpu as pltpu
from jax.sharding import PartitionSpec as P

f32, bf16 = jnp.float32, jnp.bfloat16
LANES = 128
SUBS = 8


def row_scan(values, factor, rows):
    step = 1
    while step < SUBS:
        back = jnp.where(rows >= step, pltpu.roll(values, step, axis=0), 0.0)
        values = values + factor * back
        factor = factor * factor
        step *= 2
    return values


def state_kernel(key_ref, val_ref, halo_ref, sf_ref, rate_ref, p_ref, own_ref, start_ref, xs):
    n_modes = rate_ref.shape[0]
    steps = p_ref.shape[0]
    rows = lax.broadcasted_iota(jnp.int32, (SUBS, LANES), 0)
    for j in range(2):
        xs[j, pl.ds(8, SUBS * steps), :] = (key_ref, val_ref)[j][0].astype(f32)
        xs[j, pl.ds(6, 2), :] = halo_ref[j + 1].astype(f32)
    w = [[jnp.broadcast_to(sf_ref[k, j + 1][None], (SUBS, LANES)) for k in range(3)] for j in range(2)]
    decay = [jnp.exp(-jnp.broadcast_to(rate_ref[pl.ds(r, 1), :], (SUBS, LANES))) for r in range(n_modes)]

    def tap(j, at):
        return xs[j, pl.ds(8 + at, SUBS, stride=steps), :]

    def body(t, carry):
        k1, k2, v1, v2, state = carry
        k0, v0 = tap(0, t), tap(1, t)
        key = w[0][0] * k0 + w[0][1] * k1 + w[0][2] * k2
        val = w[1][0] * v0 + w[1][1] * v1 + w[1][2] * v2
        p = (key * val).astype(bf16).astype(f32)
        p_ref[t] = p
        state = tuple(a * s + p for a, s in zip(decay, state))
        return (k0, k1, v0, v1, state)

    zero = jnp.zeros((SUBS, LANES), f32)
    init = (tap(0, -1), tap(0, -2), tap(1, -1), tap(1, -2), (zero,) * n_modes)
    state = lax.fori_loop(0, steps, body, init, unroll=4)[4]
    for r in range(n_modes):
        rate = jnp.broadcast_to(rate_ref[pl.ds(r, 1), :], (SUBS, LANES))
        scanned = row_scan(state[r], jnp.exp(-rate * steps), rows)
        own_ref[pl.ds(r, 1), :] = scanned[SUBS - 1 :]
        start_ref[r] = jnp.where(rows >= 1, pltpu.roll(scanned, 1, axis=0), 0.0)


def gate_kernel(x_ref, halo_ref, sf_ref, rate_ref, res_ref, p_ref, start_ref, enter_ref, out_ref, xs, ys):
    n_modes = rate_ref.shape[0]
    steps = p_ref.shape[0]
    rows = lax.broadcasted_iota(jnp.int32, (SUBS, LANES), 0).astype(f32)
    xs[pl.ds(8, SUBS * steps), :] = x_ref[0].astype(f32)
    xs[pl.ds(6, 2), :] = halo_ref[0].astype(f32)
    w = [jnp.broadcast_to(sf_ref[k, 0][None], (SUBS, LANES)) for k in range(3)]
    decay, gain, state0 = [], [], []
    for r in range(n_modes):
        rate = jnp.broadcast_to(rate_ref[pl.ds(r, 1), :], (SUBS, LANES))
        enter = jnp.broadcast_to(enter_ref[pl.ds(r, 1), :], (SUBS, LANES))
        decay.append(jnp.exp(-rate))
        gain.append(jnp.broadcast_to(res_ref[pl.ds(r, 1), :], (SUBS, LANES)))
        state0.append(start_ref[r] + jnp.exp(-rate * steps * rows) * enter)

    def tap(at):
        return xs[pl.ds(8 + at, SUBS, stride=steps), :]

    def body(t, carry):
        x1, x2, state = carry
        x0 = tap(t)
        gate = w[0] * x0 + w[1] * x1 + w[2] * x2
        p = p_ref[t]
        state = tuple(a * s + p for a, s in zip(decay, state))
        parts = [c * s for c, s in zip(gain, state)]
        while len(parts) > 1:
            parts = [a + b for a, b in zip(parts[::2], parts[1::2])]
        ys[pl.ds(t, SUBS, stride=steps), :] = gate * parts[0]
        return (x0, x1, state)

    lax.fori_loop(0, steps, body, (tap(-1), tap(-2), tuple(state0)), unroll=4)
    out_ref[...] = ys[...].astype(bf16)


def states(x, halo, sf, rate):
    _, n_tok, width = x.shape
    modes = rate.shape[0]
    steps = n_tok // SUBS
    col = lambda g: (0, g)
    return pl.pallas_call(
        state_kernel,
        grid=(width // LANES,),
        in_specs=[
            pl.BlockSpec((1, n_tok, LANES), lambda g: (1, 0, g)),
            pl.BlockSpec((1, n_tok, LANES), lambda g: (2, 0, g)),
            pl.BlockSpec((3, 2, LANES), lambda g: (0, 0, g)),
            pl.BlockSpec((3, 3, LANES), lambda g: (0, 0, g)),
            pl.BlockSpec((modes, LANES), col),
        ],
        out_specs=[
            pl.BlockSpec((steps, SUBS, LANES), lambda g: (0, 0, g)),
            pl.BlockSpec((modes, LANES), col),
            pl.BlockSpec((modes, SUBS, LANES), lambda g: (0, 0, g)),
        ],
        out_shape=[
            jax.ShapeDtypeStruct((steps, SUBS, width), f32),
            jax.ShapeDtypeStruct((modes, width), f32),
            jax.ShapeDtypeStruct((modes, SUBS, width), f32),
        ],
        scratch_shapes=[pltpu.VMEM((2, n_tok + 8, LANES), f32)],
        compiler_params=pltpu.CompilerParams(vmem_limit_bytes=32 << 20),
        name="states",
    )(x, x, halo, sf, rate)


def gated(x, halo, sf, rate, res, p, start, enter):
    _, n_tok, width = x.shape
    modes = rate.shape[0]
    steps = n_tok // SUBS
    col = lambda g: (0, g)
    three = lambda g: (0, 0, g)
    return pl.pallas_call(
        gate_kernel,
        grid=(width // LANES,),
        in_specs=[
            pl.BlockSpec((1, n_tok, LANES), three),
            pl.BlockSpec((1, 2, LANES), three),
            pl.BlockSpec((3, 3, LANES), three),
            pl.BlockSpec((modes, LANES), col),
            pl.BlockSpec((modes, LANES), col),
            pl.BlockSpec((steps, SUBS, LANES), three),
            pl.BlockSpec((modes, SUBS, LANES), three),
            pl.BlockSpec((modes, LANES), col),
        ],
        out_specs=pl.BlockSpec((n_tok, LANES), col),
        out_shape=jax.ShapeDtypeStruct((n_tok, width), bf16),
        scratch_shapes=[pltpu.VMEM((n_tok + 8, LANES), f32), pltpu.VMEM((n_tok, LANES), f32)],
        compiler_params=pltpu.CompilerParams(vmem_limit_bytes=32 << 20),
        name="gated",
    )(x, halo, sf, rate, res, p, start, enter)


def passed_along(x, axis, by):
    length = lax.axis_size(axis)
    pairs = [(i, i + by) for i in range(length) if 0 <= i + by < length]
    return lax.ppermute(x, axis, pairs)


def entering_state(own, rate, n_tok):
    block = jnp.exp(-rate * n_tok)
    one, two, three = (passed_along(own, "ctx", k) for k in (1, 2, 3))
    last = one + block * (two + block * three)
    four = own + block * last
    return last + block * block * block * passed_along(four, "ctx", 4)


def per_device(features, short_filter, decay_rate, residues, out_weight):
    n_tok = features.shape[0]
    halo = passed_along(features[n_tok - 2 :], "ctx", 1).transpose(1, 0, 2)
    x = features.transpose(1, 0, 2)
    product, own, start = states(x, halo, short_filter, decay_rate)
    enter = entering_state(own, decay_rate, float(n_tok))
    gated_out = gated(x, halo, short_filter, decay_rate, residues, product, start, enter)
    partial_value = jnp.dot(gated_out, out_weight, preferred_element_type=f32)
    return lax.psum_scatter(partial_value.astype(bf16), "ch", scatter_dimension=1, tiled=True)


def solution(mesh):
    placed = (P("ctx", None, "ch"), P(None, None, "ch"), P(None, "ch"), P(None, "ch"), P("ch", None))
    return jax.shard_map(per_device, mesh=mesh, in_specs=placed, out_specs=P("ctx", "ch"), check_vma=False)
```

```python
import functools

import jax
import jax.numpy as jnp
from jax import lax
from jax.experimental import pallas as pl
from jax.experimental.pallas import tpu as pltpu
from jax.sharding import PartitionSpec as P

f32, bf16 = jnp.float32, jnp.bfloat16
LANES = 128
SUBS = 8


def row_scan(values, factor, rows):
    step = 1
    while step < SUBS:
        back = jnp.where(rows >= step, pltpu.roll(values, step, axis=0), 0.0)
        values = values + factor * back
        factor = factor * factor
        step *= 2
    return values


def state_kernel(key_ref, val_ref, halo_ref, sf_ref, rate_ref, p_ref, own_ref, start_ref, xs):
    n_modes = rate_ref.shape[0]
    steps = p_ref.shape[0]
    rows = lax.broadcasted_iota(jnp.int32, (SUBS, LANES), 0)
    for j in range(2):
        xs[j, pl.ds(8, SUBS * steps), :] = (key_ref, val_ref)[j][0].astype(f32)
        xs[j, pl.ds(6, 2), :] = halo_ref[j + 1].astype(f32)
    w = [[jnp.broadcast_to(sf_ref[k, j + 1][None], (SUBS, LANES)) for k in range(3)] for j in range(2)]
    decay = [jnp.exp(-jnp.broadcast_to(rate_ref[pl.ds(r, 1), :], (SUBS, LANES))) for r in range(n_modes)]

    def tap(j, at):
        return xs[j, pl.ds(8 + at, SUBS, stride=steps), :]

    def body(t, carry):
        k1, k2, v1, v2, state = carry
        k0, v0 = tap(0, t), tap(1, t)
        key = w[0][0] * k0 + w[0][1] * k1 + w[0][2] * k2
        val = w[1][0] * v0 + w[1][1] * v1 + w[1][2] * v2
        p = (key * val).astype(bf16).astype(f32)
        p_ref[t] = p
        state = tuple(a * s + p for a, s in zip(decay, state))
        return (k0, k1, v0, v1, state)

    zero = jnp.zeros((SUBS, LANES), f32)
    init = (tap(0, -1), tap(0, -2), tap(1, -1), tap(1, -2), (zero,) * n_modes)
    state = lax.fori_loop(0, steps, body, init, unroll=4)[4]
    for r in range(n_modes):
        rate = jnp.broadcast_to(rate_ref[pl.ds(r, 1), :], (SUBS, LANES))
        scanned = row_scan(state[r], jnp.exp(-rate * steps), rows)
        own_ref[pl.ds(r, 1), :] = scanned[SUBS - 1 :]
        start_ref[r] = jnp.where(rows >= 1, pltpu.roll(scanned, 1, axis=0), 0.0)


def gate_kernel(x_ref, halo_ref, sf_ref, rate_ref, res_ref, p_ref, start_ref, enter_ref, out_ref, xs, ys):
    n_modes = rate_ref.shape[0]
    steps = p_ref.shape[0]
    rows = lax.broadcasted_iota(jnp.int32, (SUBS, LANES), 0).astype(f32)
    xs[pl.ds(8, SUBS * steps), :] = x_ref[0].astype(f32)
    xs[pl.ds(6, 2), :] = halo_ref[0].astype(f32)
    w = [jnp.broadcast_to(sf_ref[k, 0][None], (SUBS, LANES)) for k in range(3)]
    decay, gain, state0 = [], [], []
    for r in range(n_modes):
        rate = jnp.broadcast_to(rate_ref[pl.ds(r, 1), :], (SUBS, LANES))
        enter = jnp.broadcast_to(enter_ref[pl.ds(r, 1), :], (SUBS, LANES))
        decay.append(jnp.exp(-rate))
        gain.append(jnp.broadcast_to(res_ref[pl.ds(r, 1), :], (SUBS, LANES)))
        state0.append(start_ref[r] + jnp.exp(-rate * steps * rows) * enter)

    def tap(at):
        return xs[pl.ds(8 + at, SUBS, stride=steps), :]

    def body(t, carry):
        x1, x2, state = carry
        x0 = tap(t)
        gate = w[0] * x0 + w[1] * x1 + w[2] * x2
        p = p_ref[t]
        state = tuple(a * s + p for a, s in zip(decay, state))
        parts = [c * s for c, s in zip(gain, state)]
        while len(parts) > 1:
            parts = [a + b for a, b in zip(parts[::2], parts[1::2])]
        ys[pl.ds(t, SUBS, stride=steps), :] = gate * parts[0]
        return (x0, x1, state)

    lax.fori_loop(0, steps, body, (tap(-1), tap(-2), tuple(state0)), unroll=4)
    out_ref[...] = ys[...].astype(bf16)


def states(x, halo, sf, rate):
    _, n_tok, width = x.shape
    modes = rate.shape[0]
    steps = n_tok // SUBS
    col = lambda g: (0, g)
    return pl.pallas_call(
        state_kernel,
        grid=(width // LANES,),
        in_specs=[
            pl.BlockSpec((1, n_tok, LANES), lambda g: (1, 0, g)),
            pl.BlockSpec((1, n_tok, LANES), lambda g: (2, 0, g)),
            pl.BlockSpec((3, 2, LANES), lambda g: (0, 0, g)),
            pl.BlockSpec((3, 3, LANES), lambda g: (0, 0, g)),
            pl.BlockSpec((modes, LANES), col),
        ],
        out_specs=[
            pl.BlockSpec((steps, SUBS, LANES), lambda g: (0, 0, g)),
            pl.BlockSpec((modes, LANES), col),
            pl.BlockSpec((modes, SUBS, LANES), lambda g: (0, 0, g)),
        ],
        out_shape=[
            jax.ShapeDtypeStruct((steps, SUBS, width), f32),
            jax.ShapeDtypeStruct((modes, width), f32),
            jax.ShapeDtypeStruct((modes, SUBS, width), f32),
        ],
        scratch_shapes=[pltpu.VMEM((2, n_tok + 8, LANES), f32)],
        compiler_params=pltpu.CompilerParams(vmem_limit_bytes=60 << 20),
        name="states",
    )(x, x, halo, sf, rate)


def gated(x, halo, sf, rate, res, p, start, enter):
    _, n_tok, width = x.shape
    modes = rate.shape[0]
    steps = n_tok // SUBS
    col = lambda g: (0, g)
    three = lambda g: (0, 0, g)
    return pl.pallas_call(
        gate_kernel,
        grid=(width // LANES,),
        in_specs=[
            pl.BlockSpec((1, n_tok, LANES), three),
            pl.BlockSpec((1, 2, LANES), three),
            pl.BlockSpec((3, 3, LANES), three),
            pl.BlockSpec((modes, LANES), col),
            pl.BlockSpec((modes, LANES), col),
            pl.BlockSpec((steps, SUBS, LANES), three),
            pl.BlockSpec((modes, SUBS, LANES), three),
            pl.BlockSpec((modes, LANES), col),
        ],
        out_specs=pl.BlockSpec((n_tok, LANES), col),
        out_shape=jax.ShapeDtypeStruct((n_tok, width), bf16),
        scratch_shapes=[pltpu.VMEM((n_tok + 8, LANES), f32), pltpu.VMEM((n_tok, LANES), f32)],
        compiler_params=pltpu.CompilerParams(vmem_limit_bytes=60 << 20),
        name="gated",
    )(x, halo, sf, rate, res, p, start, enter)


def spread(x, axis, target):
    pairs = [(i, target(i)) for i in range(lax.axis_size(axis))]
    return lax.ppermute(x, axis, [(i, j) for i, j in pairs if j is not None])


def to_core(x):
    return spread(x, "ch", lambda i: i ^ 1)


def to_far_z(x):
    return spread(x, "ch", lambda i: i ^ 2)


def to_y(x, by):
    return spread(x, "ch", lambda i: (i + 4 * by) % 16)


def to_x(x, by):
    return spread(x, "ctx", lambda i: i // 4 * 4 + (i + by) % 4)


def entering_state(own, rate, n_tok):
    at = lax.axis_index("ctx") % 4
    behind = [own] + [to_x(own, k) for k in (1, 2, 3)]
    near = jnp.zeros_like(own)
    whole = jnp.zeros_like(own)
    for k, state in enumerate(behind):
        if k:
            near = near + jnp.where(at >= k, jnp.exp(-rate * (n_tok * (k - 1))) * state, 0.0)
        ahead = ((3 - (at - k)) % 4).astype(f32)
        whole = whole + jnp.exp(-rate * (n_tok * ahead)) * state
    before = spread(whole, "ctx", lambda i: i + 4 if i < 4 else None)
    return near + jnp.exp(-rate * (n_tok * at.astype(f32))) * before


def project_kernel(first, n_tok, cols_ref, g_ref, gp_ref, w_ref, wp_ref, *out_refs):
    k = pl.program_id(0)
    rows = pl.ds(first, n_tok)
    acc = jnp.dot(g_ref[rows, :], w_ref[...], preferred_element_type=f32)
    acc = acc + jnp.dot(gp_ref[rows, :], wp_ref[...], preferred_element_type=f32)
    if len(out_refs) == 1:
        out_refs[0][0] = acc.astype(bf16)
        return
    for i, out_ref in enumerate(out_refs):

        @pl.when(k == i)
        def _():
            out_ref[...] = acc.astype(bf16)


def project(operands, first, n_tok, blocks, stacked=False):
    g, gp, w, wp = operands
    at = lax.axis_index("ch")
    y, z, core = at // 4, at // 2 % 2, at % 2
    cols = jnp.stack([(y + dy) % 4 * 4 + (z + dz) % 2 * 2 + core for dy, dz in blocks]).astype(jnp.int32)
    tok, depth = g.shape
    n = len(blocks)
    if stacked:
        out_specs = pl.BlockSpec((1, n_tok, depth), lambda k, c: (k, 0, 0))
        out_shape = jax.ShapeDtypeStruct((n, n_tok, depth), bf16)
    else:
        out_specs = [pl.BlockSpec((n_tok, depth), lambda k, c: (0, 0))] * n
        out_shape = [jax.ShapeDtypeStruct((n_tok, depth), bf16)] * n
    return pl.pallas_call(
        functools.partial(project_kernel, first, n_tok),
        grid_spec=pltpu.PrefetchScalarGridSpec(
            num_scalar_prefetch=1,
            grid=(n,),
            in_specs=[
                pl.BlockSpec((tok, depth), lambda k, c: (0, 0)),
                pl.BlockSpec((tok, depth), lambda k, c: (0, 0)),
                pl.BlockSpec((depth, depth), lambda k, c: (0, c[k])),
                pl.BlockSpec((depth, depth), lambda k, c: (0, c[k])),
            ],
            out_specs=out_specs,
        ),
        out_shape=out_shape,
        compiler_params=pltpu.CompilerParams(vmem_limit_bytes=60 << 20),
        name="project",
    )(cols, g, gp, w, wp)


def total(*parts):
    return sum(p.astype(f32) for p in parts).astype(bf16)


Z_TOK = 384


def per_device(features, short_filter, decay_rate, residues, out_weight):
    n_tok = features.shape[0]
    halo = spread(features[n_tok - 2 :], "ctx", lambda i: i + 1 if i < 7 else None).transpose(1, 0, 2)
    x = features.transpose(1, 0, 2)
    weight_pair = to_core(out_weight)
    product, own, start = states(x, halo, short_filter, decay_rate)
    enter = entering_state(own, decay_rate, float(n_tok))
    mine = gated(x, halo, short_filter, decay_rate, residues, product, start, enter)
    operands = (mine, to_core(mine), out_weight, weight_pair)
    n_y = n_tok - Z_TOK
    half = Z_TOK // 2

    p20, p21 = project(operands, 0, n_y, [(2, 0), (2, 1)])
    r20, r21 = to_y(p20, 1), to_y(p21, -1)
    far = to_far_z(project(operands, n_y, Z_TOK, [(0, 1), (1, 1), (2, 1), (3, 1)], True))
    p11, p30 = project(operands, 0, n_y, [(1, 1), (3, 0)])
    r11, r30 = to_y(p11, 1), to_y(p30, -1)
    p10, p31, p00, p01 = project(operands, 0, n_y, [(1, 0), (3, 1), (0, 0), (0, 1)])
    r10, r31 = to_y(total(p10, r20), 1), to_y(total(p31, r21), -1)
    zv = to_far_z(total(p01, r11, r31))

    near = project(operands, n_y, Z_TOK, [(0, 0), (1, 0), (2, 0), (3, 0)], True)
    q2 = total(near[2], far[2])
    s2a, s2b = to_y(q2[:half], 1), to_y(q2[half:], -1)
    q1 = jnp.concatenate([total(near[1, :half], far[1, :half], s2a), total(near[1, half:], far[1, half:])])
    q3 = jnp.concatenate([total(near[3, :half], far[3, :half]), total(near[3, half:], far[3, half:], s2b)])
    s1, s3 = to_y(q1, 1), to_y(q3, -1)
    return jnp.concatenate([total(p00, r10, r30, zv), total(near[0], far[0], s1, s3)])


def solution(mesh):
    placed = (P("ctx", None, "ch"), P(None, None, "ch"), P(None, "ch"), P(None, "ch"), P("ch", None))
    return jax.shard_map(per_device, mesh=mesh, in_specs=placed, out_specs=P("ctx", "ch"), check_vma=False)
```

```python
import functools

import jax
import jax.numpy as jnp
from jax import lax
from jax.experimental import pallas as pl
from jax.experimental.pallas import tpu as pltpu
from jax.sharding import PartitionSpec as P

f32, bf16 = jnp.float32, jnp.bfloat16
LANES = 128
SUBS = 8
PAD = 8


def row_scan(values, factor, rows):
    step = 1
    while step < SUBS:
        back = jnp.where(rows >= step, pltpu.roll(values, step, axis=0), 0.0)
        values = values + factor * back
        factor = factor * factor
        step *= 2
    return values


def fill(rows_ref, x_ref, halo, steps):
    for s in range(SUBS):
        at = s * (steps + PAD) + PAD
        rows_ref[pl.ds(at, steps), :] = x_ref[pl.ds(s * steps, steps), :].astype(f32)
        before = x_ref[pl.ds(s * steps - 16, 16), :].astype(f32)[14:] if s else halo.astype(f32)
        rows_ref[pl.ds(at - 2, 2), :] = before


def state_kernel(key_ref, val_ref, halo_ref, sf_ref, rate_ref, p_ref, own_ref, start_ref, xs):
    n_modes = rate_ref.shape[0]
    steps = p_ref.shape[0]
    rows = lax.broadcasted_iota(jnp.int32, (SUBS, LANES), 0)
    for j in range(2):
        fill(xs.at[j], (key_ref, val_ref)[j].at[0], halo_ref[j + 1], steps)
    w = [[jnp.broadcast_to(sf_ref[k, j + 1][None], (SUBS, LANES)) for k in range(3)] for j in range(2)]
    decay = [jnp.exp(-jnp.broadcast_to(rate_ref[pl.ds(r, 1), :], (SUBS, LANES))) for r in range(n_modes)]

    def tap(j, at):
        return xs[j, pl.ds(8 + at, SUBS, stride=steps + PAD), :]

    def body(t, carry):
        k1, k2, v1, v2, state = carry
        k0, v0 = tap(0, t), tap(1, t)
        key = w[0][0] * k0 + w[0][1] * k1 + w[0][2] * k2
        val = w[1][0] * v0 + w[1][1] * v1 + w[1][2] * v2
        p = (key * val).astype(bf16).astype(f32)
        p_ref[t] = p
        state = tuple(a * s + p for a, s in zip(decay, state))
        return (k0, k1, v0, v1, state)

    zero = jnp.zeros((SUBS, LANES), f32)
    init = (tap(0, -1), tap(0, -2), tap(1, -1), tap(1, -2), (zero,) * n_modes)
    state = lax.fori_loop(0, steps, body, init, unroll=8)[4]
    for r in range(n_modes):
        rate = jnp.broadcast_to(rate_ref[pl.ds(r, 1), :], (SUBS, LANES))
        scanned = row_scan(state[r], jnp.exp(-rate * steps), rows)
        own_ref[pl.ds(r, 1), :] = scanned[SUBS - 1 :]
        start_ref[r] = jnp.where(rows >= 1, pltpu.roll(scanned, 1, axis=0), 0.0)


def gate_kernel(x_ref, halo_ref, sf_ref, rate_ref, res_ref, p_ref, start_ref, enter_ref, out_ref, xs, ys):
    n_modes = rate_ref.shape[0]
    steps = p_ref.shape[0]
    rows = lax.broadcasted_iota(jnp.int32, (SUBS, LANES), 0).astype(f32)
    fill(xs, x_ref.at[0], halo_ref[0], steps)
    w = [jnp.broadcast_to(sf_ref[k, 0][None], (SUBS, LANES)) for k in range(3)]
    decay, gain, state0 = [], [], []
    for r in range(n_modes):
        rate = jnp.broadcast_to(rate_ref[pl.ds(r, 1), :], (SUBS, LANES))
        enter = jnp.broadcast_to(enter_ref[pl.ds(r, 1), :], (SUBS, LANES))
        decay.append(jnp.exp(-rate))
        gain.append(jnp.broadcast_to(res_ref[pl.ds(r, 1), :], (SUBS, LANES)))
        state0.append(start_ref[r] + jnp.exp(-rate * steps * rows) * enter)

    def tap(at):
        return xs[pl.ds(8 + at, SUBS, stride=steps + PAD), :]

    def body(t, carry):
        x1, x2, state = carry
        x0 = tap(t)
        gate = w[0] * x0 + w[1] * x1 + w[2] * x2
        p = p_ref[t]
        state = tuple(a * s + p for a, s in zip(decay, state))
        parts = [c * s for c, s in zip(gain, state)]
        while len(parts) > 1:
            parts = [a + b for a, b in zip(parts[::2], parts[1::2])]
        ys[pl.ds(t, SUBS, stride=steps + PAD), :] = gate * parts[0]
        return (x0, x1, state)

    lax.fori_loop(0, steps, body, (tap(-1), tap(-2), tuple(state0)), unroll=4)
    for s in range(SUBS):
        out_ref[pl.ds(s * steps, steps), :] = ys[pl.ds(s * (steps + PAD), steps), :].astype(bf16)


def states(x, halo, sf, rate):
    _, n_tok, width = x.shape
    modes = rate.shape[0]
    steps = n_tok // SUBS
    col = lambda g: (0, g)
    return pl.pallas_call(
        state_kernel,
        grid=(width // LANES,),
        in_specs=[
            pl.BlockSpec((1, n_tok, LANES), lambda g: (1, 0, g)),
            pl.BlockSpec((1, n_tok, LANES), lambda g: (2, 0, g)),
            pl.BlockSpec((3, 2, LANES), lambda g: (0, 0, g)),
            pl.BlockSpec((3, 3, LANES), lambda g: (0, 0, g)),
            pl.BlockSpec((modes, LANES), col),
        ],
        out_specs=[
            pl.BlockSpec((steps, SUBS, LANES), lambda g: (0, 0, g)),
            pl.BlockSpec((modes, LANES), col),
            pl.BlockSpec((modes, SUBS, LANES), lambda g: (0, 0, g)),
        ],
        out_shape=[
            jax.ShapeDtypeStruct((steps, SUBS, width), f32),
            jax.ShapeDtypeStruct((modes, width), f32),
            jax.ShapeDtypeStruct((modes, SUBS, width), f32),
        ],
        scratch_shapes=[pltpu.VMEM((2, n_tok + SUBS * PAD, LANES), f32)],
        compiler_params=pltpu.CompilerParams(vmem_limit_bytes=60 << 20),
        name="states",
    )(x, x, halo, sf, rate)


def gated(x, halo, sf, rate, res, p, start, enter):
    _, n_tok, width = x.shape
    modes = rate.shape[0]
    steps = n_tok // SUBS
    col = lambda g: (0, g)
    three = lambda g: (0, 0, g)
    return pl.pallas_call(
        gate_kernel,
        grid=(width // LANES,),
        in_specs=[
            pl.BlockSpec((1, n_tok, LANES), three),
            pl.BlockSpec((1, 2, LANES), three),
            pl.BlockSpec((3, 3, LANES), three),
            pl.BlockSpec((modes, LANES), col),
            pl.BlockSpec((modes, LANES), col),
            pl.BlockSpec((steps, SUBS, LANES), three),
            pl.BlockSpec((modes, SUBS, LANES), three),
            pl.BlockSpec((modes, LANES), col),
        ],
        out_specs=pl.BlockSpec((n_tok, LANES), col),
        out_shape=jax.ShapeDtypeStruct((n_tok, width), bf16),
        scratch_shapes=[pltpu.VMEM((n_tok + SUBS * PAD, LANES), f32), pltpu.VMEM((n_tok + SUBS * PAD, LANES), f32)],
        compiler_params=pltpu.CompilerParams(vmem_limit_bytes=60 << 20),
        name="gated",
    )(x, halo, sf, rate, res, p, start, enter)


def spread(x, axis, target):
    pairs = [(i, target(i)) for i in range(lax.axis_size(axis))]
    return lax.ppermute(x, axis, [(i, j) for i, j in pairs if j is not None])


def to_core(x):
    return spread(x, "ch", lambda i: i ^ 1)


def to_far_z(x):
    return spread(x, "ch", lambda i: i ^ 2)


def to_y(x, by):
    return spread(x, "ch", lambda i: (i + 4 * by) % 16)


def to_x(x, by):
    return spread(x, "ctx", lambda i: i // 4 * 4 + (i + by) % 4)


def entering_state(own, rate, n_tok):
    at = lax.axis_index("ctx") % 4
    behind = [own] + [to_x(own, k) for k in (1, 2, 3)]
    near = jnp.zeros_like(own)
    whole = jnp.zeros_like(own)
    for k, state in enumerate(behind):
        if k:
            near = near + jnp.where(at >= k, jnp.exp(-rate * (n_tok * (k - 1))) * state, 0.0)
        ahead = ((3 - (at - k)) % 4).astype(f32)
        whole = whole + jnp.exp(-rate * (n_tok * ahead)) * state
    before = spread(whole, "ctx", lambda i: i + 4 if i < 4 else None)
    return near + jnp.exp(-rate * (n_tok * at.astype(f32))) * before


def project_kernel(plan, cols_ref, g_ref, gp_ref, w_ref, wp_ref, *refs):
    out_refs, (weights, sems) = refs[:-2], refs[-2:]
    depth = g_ref.shape[1]
    copies = []
    for k, (col, _) in enumerate(plan):
        at = pl.ds(pl.multiple_of(cols_ref[col] * depth, depth), depth)
        pair = []
        for j, source in enumerate((w_ref, wp_ref)):
            copy = pltpu.make_async_copy(source.at[:, at], weights.at[k, j], sems.at[k, j])
            copy.start()
            pair.append(copy)
        copies.append(pair)
    for k, (_, pieces) in enumerate(plan):
        for copy in copies[k]:
            copy.wait()
        for first, count, out, slot in pieces:
            rows = pl.ds(first, count)
            acc = jnp.dot(g_ref[rows, :], weights[k, 0], preferred_element_type=f32)
            acc = acc + jnp.dot(gp_ref[rows, :], weights[k, 1], preferred_element_type=f32)
            out_refs[out][slot] = acc.astype(bf16)


def project(operands, plan, counts):
    cols, g, gp, w, wp = operands
    depth = g.shape[1]
    slots = [0] * len(counts)
    laid = []
    for (dy, dz), pieces in plan:
        mine = []
        for first, out in pieces:
            mine.append((first, counts[out], out, slots[out]))
            slots[out] += 1
        laid.append((2 * dy + dz, mine))
    vmem = pl.BlockSpec(memory_space=pltpu.VMEM)
    hbm = pl.BlockSpec(memory_space=pltpu.HBM)
    return pl.pallas_call(
        functools.partial(project_kernel, laid),
        in_specs=[pl.BlockSpec(memory_space=pltpu.SMEM), vmem, vmem, hbm, hbm],
        out_specs=[vmem] * len(counts),
        out_shape=[jax.ShapeDtypeStruct((n, count, depth), bf16) for n, count in zip(slots, counts)],
        scratch_shapes=[
            pltpu.VMEM((len(plan), 2, depth, depth), bf16),
            pltpu.SemaphoreType.DMA((len(plan), 2)),
        ],
        compiler_params=pltpu.CompilerParams(vmem_limit_bytes=50 << 20),
        name="project",
    )(cols, g, gp, w, wp)


def total(*parts):
    return sum(p.astype(f32) for p in parts).astype(bf16)


Z_TOK = 384


def per_device(features, short_filter, decay_rate, residues, out_weight):
    n_tok = features.shape[0]
    halo = spread(features[n_tok - 2 :], "ctx", lambda i: i + 1 if i < 7 else None).transpose(1, 0, 2)
    x = features.transpose(1, 0, 2)
    weight_pair = to_core(out_weight)
    me = lax.axis_index("ch")
    steps = jnp.arange(8, dtype=jnp.int32)
    cols = (me // 4 + steps // 2) % 4 * 4 + (me // 2 + steps) % 2 * 2 + me % 2
    product, own, start = states(x, halo, short_filter, decay_rate)
    enter = entering_state(own, decay_rate, float(n_tok))
    mine = gated(x, halo, short_filter, decay_rate, residues, product, start, enter)
    operands = (cols, mine, to_core(mine), out_weight, weight_pair)
    n_y = n_tok - Z_TOK
    a, b, z = 0, n_y // 2, n_y

    up2, down2, far = project(
        operands,
        [((2, 0), [(a, 0), (b, 1)]), ((2, 1), [(a, 0), (b, 1), (z, 2)]), ((3, 1), [(z, 2)]), ((1, 1), [(z, 2)]), ((0, 1), [(z, 2)])],
        [b, b, Z_TOK],
    )
    up2, down2, far = to_y(up2, 1), to_y(down2, -1), to_far_z(far)
    up, down, up_more, down_more, keep_a, keep_b, near = project(
        operands,
        [((1, 0), [(b, 0), (a, 2)]), ((1, 1), [(b, 0), (a, 2)]), ((3, 0), [(a, 1), (b, 3)]), ((3, 1), [(a, 1), (b, 3)])]
        + [((0, 0), [(a, 4), (b, 5)]), ((0, 1), [(a, 4), (b, 5)])],
        [b, b, b, b, b, b],
    ) + project(operands, [((2, 0), [(z, 0)]), ((3, 0), [(z, 0)]), ((1, 0), [(z, 0)]), ((0, 0), [(z, 0)])], [Z_TOK])
    up, down = to_y(up, 1), to_y(down, -1)
    up_more, down_more = to_y(total(up_more, up2), 1), to_y(total(down_more, down2), -1)
    up, down, up_more, down_more = lax.optimization_barrier((up, down, up_more, down_more))
    over = to_far_z(jnp.stack([total(keep_a[1], up_more[1], down[1]), total(keep_b[1], up[1], down_more[1])]))
    done_a = total(keep_a[0], up_more[0], down[0], over[0])
    done_b = total(keep_b[0], up[0], down_more[0], over[1])

    half = Z_TOK // 2
    s2a, s2b = to_y(total(near[0, :half], far[0, :half]), 1), to_y(total(near[0, half:], far[0, half:]), -1)
    s3 = jnp.concatenate([total(near[1, :half], far[1, :half]), total(near[1, half:], far[1, half:], s2b)])
    s1 = jnp.concatenate([total(near[2, :half], far[2, :half], s2a), total(near[2, half:], far[2, half:])])
    s1, s3 = to_y(s1, 1), to_y(s3, -1)
    return jnp.concatenate([done_a, done_b, total(near[3], far[3], s1, s3)])


def solution(mesh):
    placed = (P("ctx", None, "ch"), P(None, None, "ch"), P(None, "ch"), P(None, "ch"), P("ch", None))
    return jax.shard_map(per_device, mesh=mesh, in_specs=placed, out_specs=P("ctx", "ch"), check_vma=False)
```

```python
import functools

import jax
import jax.numpy as jnp
from jax import lax
from jax.experimental import pallas as pl
from jax.experimental.pallas import tpu as pltpu
from jax.sharding import PartitionSpec as P

f32, bf16 = jnp.float32, jnp.bfloat16
LANES = 128
SUBS = 8
PAD = 8


def row_scan(values, factor, rows):
    step = 1
    while step < SUBS:
        back = jnp.where(rows >= step, pltpu.roll(values, step, axis=0), 0.0)
        values = values + factor * back
        factor = factor * factor
        step *= 2
    return values


def fill(rows_ref, x_ref, halo, steps):
    for s in range(SUBS):
        at = s * (steps + PAD) + PAD
        rows_ref[pl.ds(at, steps), :] = x_ref[pl.ds(s * steps, steps), :].astype(f32)
        before = x_ref[pl.ds(s * steps - 16, 16), :].astype(f32)[14:] if s else halo.astype(f32)
        rows_ref[pl.ds(at - 2, 2), :] = before


def state_kernel(key_ref, val_ref, halo_ref, sf_ref, rate_ref, p_ref, own_ref, start_ref, xs):
    n_modes = rate_ref.shape[0]
    steps = p_ref.shape[0]
    rows = lax.broadcasted_iota(jnp.int32, (SUBS, LANES), 0)
    for j in range(2):
        fill(xs.at[j], (key_ref, val_ref)[j].at[0], halo_ref[j + 1], steps)
    w = [[jnp.broadcast_to(sf_ref[k, j + 1][None], (SUBS, LANES)) for k in range(3)] for j in range(2)]
    decay = [jnp.exp(-jnp.broadcast_to(rate_ref[pl.ds(r, 1), :], (SUBS, LANES))) for r in range(n_modes)]

    def tap(j, at):
        return xs[j, pl.ds(8 + at, SUBS, stride=steps + PAD), :]

    def body(t, carry):
        k1, k2, v1, v2, state = carry
        k0, v0 = tap(0, t), tap(1, t)
        key = w[0][0] * k0 + w[0][1] * k1 + w[0][2] * k2
        val = w[1][0] * v0 + w[1][1] * v1 + w[1][2] * v2
        p = (key * val).astype(bf16).astype(f32)
        p_ref[t] = p
        state = tuple(a * s + p for a, s in zip(decay, state))
        return (k0, k1, v0, v1, state)

    zero = jnp.zeros((SUBS, LANES), f32)
    init = (tap(0, -1), tap(0, -2), tap(1, -1), tap(1, -2), (zero,) * n_modes)
    state = lax.fori_loop(0, steps, body, init, unroll=8)[4]
    for r in range(n_modes):
        rate = jnp.broadcast_to(rate_ref[pl.ds(r, 1), :], (SUBS, LANES))
        scanned = row_scan(state[r], jnp.exp(-rate * steps), rows)
        own_ref[pl.ds(r, 1), :] = scanned[SUBS - 1 :]
        start_ref[r] = jnp.where(rows >= 1, pltpu.roll(scanned, 1, axis=0), 0.0)


def gate_kernel(x_ref, halo_ref, sf_ref, rate_ref, res_ref, p_ref, start_ref, enter_ref, out_ref, xs, ys):
    n_modes = rate_ref.shape[0]
    steps = p_ref.shape[0]
    rows = lax.broadcasted_iota(jnp.int32, (SUBS, LANES), 0).astype(f32)
    fill(xs, x_ref.at[0], halo_ref[0], steps)
    w = [jnp.broadcast_to(sf_ref[k, 0][None], (SUBS, LANES)) for k in range(3)]
    decay, gain, state0 = [], [], []
    for r in range(n_modes):
        rate = jnp.broadcast_to(rate_ref[pl.ds(r, 1), :], (SUBS, LANES))
        enter = jnp.broadcast_to(enter_ref[pl.ds(r, 1), :], (SUBS, LANES))
        decay.append(jnp.exp(-rate))
        gain.append(jnp.broadcast_to(res_ref[pl.ds(r, 1), :], (SUBS, LANES)))
        state0.append(start_ref[r] + jnp.exp(-rate * steps * rows) * enter)

    def tap(at):
        return xs[pl.ds(8 + at, SUBS, stride=steps + PAD), :]

    def body(t, carry):
        x1, x2, state = carry
        x0 = tap(t)
        gate = w[0] * x0 + w[1] * x1 + w[2] * x2
        p = p_ref[t]
        state = tuple(a * s + p for a, s in zip(decay, state))
        parts = [c * s for c, s in zip(gain, state)]
        while len(parts) > 1:
            parts = [a + b for a, b in zip(parts[::2], parts[1::2])]
        ys[pl.ds(t, SUBS, stride=steps + PAD), :] = gate * parts[0]
        return (x0, x1, state)

    lax.fori_loop(0, steps, body, (tap(-1), tap(-2), tuple(state0)), unroll=4)
    for s in range(SUBS):
        out_ref[pl.ds(s * steps, steps), :] = ys[pl.ds(s * (steps + PAD), steps), :].astype(bf16)


def states(x, halo, sf, rate):
    _, n_tok, width = x.shape
    modes = rate.shape[0]
    steps = n_tok // SUBS
    col = lambda g: (0, g)
    return pl.pallas_call(
        state_kernel,
        grid=(width // LANES,),
        in_specs=[
            pl.BlockSpec((1, n_tok, LANES), lambda g: (1, 0, g)),
            pl.BlockSpec((1, n_tok, LANES), lambda g: (2, 0, g)),
            pl.BlockSpec((3, 2, LANES), lambda g: (0, 0, g)),
            pl.BlockSpec((3, 3, LANES), lambda g: (0, 0, g)),
            pl.BlockSpec((modes, LANES), col),
        ],
        out_specs=[
            pl.BlockSpec((steps, SUBS, LANES), lambda g: (0, 0, g)),
            pl.BlockSpec((modes, LANES), col),
            pl.BlockSpec((modes, SUBS, LANES), lambda g: (0, 0, g)),
        ],
        out_shape=[
            jax.ShapeDtypeStruct((steps, SUBS, width), f32),
            jax.ShapeDtypeStruct((modes, width), f32),
            jax.ShapeDtypeStruct((modes, SUBS, width), f32),
        ],
        scratch_shapes=[pltpu.VMEM((2, n_tok + SUBS * PAD, LANES), f32)],
        compiler_params=pltpu.CompilerParams(vmem_limit_bytes=59 << 20),
        name="states",
    )(x, x, halo, sf, rate)


def gated(x, halo, sf, rate, res, p, start, enter):
    _, n_tok, width = x.shape
    modes = rate.shape[0]
    steps = n_tok // SUBS
    col = lambda g: (0, g)
    three = lambda g: (0, 0, g)
    return pl.pallas_call(
        gate_kernel,
        grid=(width // LANES,),
        in_specs=[
            pl.BlockSpec((1, n_tok, LANES), three),
            pl.BlockSpec((1, 2, LANES), three),
            pl.BlockSpec((3, 3, LANES), three),
            pl.BlockSpec((modes, LANES), col),
            pl.BlockSpec((modes, LANES), col),
            pl.BlockSpec((steps, SUBS, LANES), three),
            pl.BlockSpec((modes, SUBS, LANES), three),
            pl.BlockSpec((modes, LANES), col),
        ],
        out_specs=pl.BlockSpec((n_tok, LANES), col),
        out_shape=jax.ShapeDtypeStruct((n_tok, width), bf16),
        scratch_shapes=[pltpu.VMEM((n_tok + SUBS * PAD, LANES), f32), pltpu.VMEM((n_tok + SUBS * PAD, LANES), f32)],
        compiler_params=pltpu.CompilerParams(vmem_limit_bytes=59 << 20),
        name="gated",
    )(x, halo, sf, rate, res, p, start, enter)


def spread(x, axis, target):
    pairs = [(i, target(i)) for i in range(lax.axis_size(axis))]
    return lax.ppermute(x, axis, [(i, j) for i, j in pairs if j is not None])


def to_core(x):
    return spread(x, "ch", lambda i: i ^ 1)


def to_far_z(x):
    return spread(x, "ch", lambda i: i ^ 2)


def to_y(x, by):
    return spread(x, "ch", lambda i: (i + 4 * by) % 16)


def to_x(x, by):
    return spread(x, "ctx", lambda i: i // 4 * 4 + (i + by) % 4)


def entering_state(own, rate, n_tok):
    at = lax.axis_index("ctx") % 4
    behind = [own] + [to_x(own, k) for k in (1, 2, 3)]
    near = jnp.zeros_like(own)
    whole = jnp.zeros_like(own)
    for k, state in enumerate(behind):
        if k:
            near = near + jnp.where(at >= k, jnp.exp(-rate * (n_tok * (k - 1))) * state, 0.0)
        ahead = ((3 - (at - k)) % 4).astype(f32)
        whole = whole + jnp.exp(-rate * (n_tok * ahead)) * state
    before = spread(whole, "ctx", lambda i: i + 4 if i < 4 else None)
    return near + jnp.exp(-rate * (n_tok * at.astype(f32))) * before


def project_kernel(plan, n_added, cols_ref, g_ref, gp_ref, w_ref, wp_ref, *refs):
    added, refs = refs[:n_added], refs[n_added:]
    out_refs, (acts, weights, act_sems, weight_sems) = refs[:-4], refs[-4:]
    depth = g_ref.shape[1]
    act_copies = [pltpu.make_async_copy(r, acts.at[j], act_sems.at[j]) for j, r in enumerate((g_ref, gp_ref))]
    copies = []
    for k, (col, _) in enumerate(plan):
        at = pl.ds(pl.multiple_of(cols_ref[col] * depth, depth), depth)
        pair = [
            pltpu.make_async_copy(source.at[:, at], weights.at[k, j], weight_sems.at[k, j])
            for j, source in enumerate((w_ref, wp_ref))
        ]
        for copy in act_copies + pair if k == 0 else pair:
            copy.start()
        copies.append(pair)
    for k, (_, pieces) in enumerate(plan):
        for copy in act_copies + copies[k] if k == 0 else copies[k]:
            copy.wait()
        for first, count, out, slot, extra in pieces:
            rows = pl.ds(first, count)
            acc = jnp.dot(acts[0, rows, :], weights[k, 0], preferred_element_type=f32)
            acc = acc + jnp.dot(acts[1, rows, :], weights[k, 1], preferred_element_type=f32)
            if extra is not None:
                acc = acc + added[extra[0]][extra[1]].astype(f32)
            out_refs[out][slot] = acc.astype(bf16)


def project(operands, plan, counts, added=()):
    cols, g, gp, w, wp = operands
    n_tok, depth = g.shape
    slots = [0] * len(counts)
    laid = []
    for (dy, dz), pieces in plan:
        mine = []
        for first, out, *extra in pieces:
            mine.append((first, counts[out], out, slots[out], extra[0] if extra else None))
            slots[out] += 1
        laid.append((2 * dy + dz, mine))
    vmem = pl.BlockSpec(memory_space=pltpu.VMEM)
    anywhere = pl.BlockSpec(memory_space=pl.ANY)
    return pl.pallas_call(
        functools.partial(project_kernel, laid, len(added)),
        in_specs=[pl.BlockSpec(memory_space=pltpu.SMEM)] + [anywhere] * 4 + [vmem] * len(added),
        out_specs=[vmem] * len(counts),
        out_shape=[jax.ShapeDtypeStruct((n, count, depth), bf16) for n, count in zip(slots, counts)],
        scratch_shapes=[
            pltpu.VMEM((2, n_tok, depth), bf16),
            pltpu.VMEM((len(plan), 2, depth, depth), bf16),
            pltpu.SemaphoreType.DMA((2,)),
            pltpu.SemaphoreType.DMA((len(plan), 2)),
        ],
        compiler_params=pltpu.CompilerParams(vmem_limit_bytes=50 << 20),
        name="project",
    )(cols, g, gp, w, wp, *added)


def total(*parts):
    return sum(p.astype(f32) for p in parts).astype(bf16)


Z_TOK = 320


def per_device(features, short_filter, decay_rate, residues, out_weight):
    n_tok = features.shape[0]
    halo = spread(features[n_tok - 2 :], "ctx", lambda i: i + 1 if i < 7 else None).transpose(1, 0, 2)
    x = features.transpose(1, 0, 2)
    weight_pair = to_core(out_weight)
    me = lax.axis_index("ch")
    steps = jnp.arange(8, dtype=jnp.int32)
    cols = (me // 4 + steps // 2) % 4 * 4 + (me // 2 + steps) % 2 * 2 + me % 2
    product, own, start = states(x, halo, short_filter, decay_rate)
    enter = entering_state(own, decay_rate, float(n_tok))
    mine = gated(x, halo, short_filter, decay_rate, residues, product, start, enter)
    operands = (cols, mine, to_core(mine), out_weight, weight_pair)
    n_y = n_tok - Z_TOK
    a, b, z = 0, n_y // 2, n_y

    up2, down2 = project(operands, [((2, dz), [(a, 0), (b, 1)]) for dz in (1, 0)], [b, b])
    up2, down2 = to_y(up2, 1), to_y(down2, -1)
    (far,) = project(operands, [((dy, 1), [(z, 0)]) for dy in range(4)], [Z_TOK])
    far = to_far_z(far)

    up, down, up_more, down_more, keep_a, keep_b = project(
        operands,
        [((1, 1), [(b, 0), (a, 2)]), ((3, 1), [(a, 1), (b, 3)]), ((0, 1), [(a, 4), (b, 5)])],
        [b] * 6,
    )
    up, down = to_y(up[0], 1), to_y(down[0], -1)
    up_more, down_more = to_y(total(up_more[0], up2[0]), 1), to_y(total(down_more[0], down2[0]), -1)
    rise, fall, stay_a, stay_b = project(
        operands,
        [((1, 0), [(b, 0), (a, 0, (0, 1))]), ((3, 0), [(a, 1), (b, 1, (1, 1))]), ((0, 0), [(a, 2), (b, 3)])],
        [b] * 4,
        [up2, down2],
    )
    rise, fall = to_y(rise, 1), to_y(fall, -1)
    (near,) = project(operands, [((dy, 0), [(z, 0)]) for dy in range(4)], [Z_TOK])
    up, down, up_more, down_more = lax.optimization_barrier((up, down, up_more, down_more))
    over = to_far_z(jnp.stack([total(keep_a[0], up_more, down), total(keep_b[0], up, down_more)]))
    rise, fall = lax.optimization_barrier((rise, fall))
    done_a = total(stay_a[0], rise[1], fall[0], over[0])
    done_b = total(stay_b[0], rise[0], fall[1], over[1])

    half = Z_TOK // 2
    s2a, s2b = to_y(total(near[2, :half], far[2, :half]), 1), to_y(total(near[2, half:], far[2, half:]), -1)
    s3 = jnp.concatenate([total(near[3, :half], far[3, :half]), total(near[3, half:], far[3, half:], s2b)])
    s1 = jnp.concatenate([total(near[1, :half], far[1, :half], s2a), total(near[1, half:], far[1, half:])])
    s1, s3 = to_y(s1, 1), to_y(s3, -1)
    return jnp.concatenate([done_a, done_b, total(near[0], far[0], s1, s3)])


def solution(mesh):
    placed = (P("ctx", None, "ch"), P(None, None, "ch"), P(None, "ch"), P(None, "ch"), P("ch", None))
    return jax.shard_map(per_device, mesh=mesh, in_specs=placed, out_specs=P("ctx", "ch"), check_vma=False)
```

```python
import functools

import jax
import jax.numpy as jnp
from jax import lax
from jax.experimental import pallas as pl
from jax.experimental.pallas import tpu as pltpu
from jax.sharding import PartitionSpec as P

f32, bf16 = jnp.float32, jnp.bfloat16
LANES = 128
SUBS = 8
PAD = 8
STATE_ROWS, FIRST, LAST, PAYLOAD = 16, 16, 20, 32


def row_scan(values, factor, rows):
    step = 1
    while step < SUBS:
        back = jnp.where(rows >= step, pltpu.roll(values, step, axis=0), 0.0)
        values = values + factor * back
        factor = factor * factor
        step *= 2
    return values


def fill(rows_ref, x_ref, halo, steps):
    for s in range(SUBS):
        at = s * (steps + PAD) + PAD
        rows_ref[pl.ds(at, steps), :] = x_ref[pl.ds(s * steps, steps), :].astype(f32)
        before = x_ref[pl.ds(s * steps - 16, 16), :].astype(f32)[14:] if s else halo
        rows_ref[pl.ds(at - 2, 2), :] = before


def state_kernel(key_ref, val_ref, query_ref, sf_ref, rate_ref, p_ref, told_ref, start_ref, xs, told):
    n_modes = rate_ref.shape[0]
    steps = p_ref.shape[0]
    rows = lax.broadcasted_iota(jnp.int32, (SUBS, LANES), 0)
    none = jnp.zeros((2, LANES), f32)
    for j in range(2):
        fill(xs.at[j], (key_ref, val_ref)[j].at[0], none, steps)
    w = [[jnp.broadcast_to(sf_ref[k, j + 1][None], (SUBS, LANES)) for k in range(3)] for j in range(2)]
    decay = [jnp.exp(-jnp.broadcast_to(rate_ref[pl.ds(r, 1), :], (SUBS, LANES))) for r in range(n_modes)]

    def tap(j, at):
        return xs[j, pl.ds(PAD + at, SUBS, stride=steps + PAD), :]

    def body(t, carry, first=False):
        k1, k2, v1, v2, state = carry
        k0, v0 = tap(0, t), tap(1, t)
        key = w[0][0] * k0 + w[0][1] * k1 + w[0][2] * k2
        val = w[1][0] * v0 + w[1][1] * v1 + w[1][2] * v2
        p = (key * val).astype(bf16).astype(f32)
        if first:
            p = jnp.where(rows >= 1, p, 0.0)
        p_ref[t] = p
        state = tuple(a * s + p for a, s in zip(decay, state))
        return (k0, k1, v0, v1, state)

    zero = jnp.zeros((SUBS, LANES), f32)
    carry = (tap(0, -1), tap(0, -2), tap(1, -1), tap(1, -2), (zero,) * n_modes)
    carry = body(1, body(0, carry, True), True)
    state = lax.fori_loop(2, steps, body, carry, unroll=7)[4]
    for r in range(n_modes):
        rate = jnp.broadcast_to(rate_ref[pl.ds(r, 1), :], (SUBS, LANES))
        scanned = row_scan(state[r], jnp.exp(-rate * steps), rows)
        told[pl.ds(r, 1), :] = scanned[SUBS - 1 :]
        start_ref[r] = jnp.where(rows >= 1, pltpu.roll(scanned, 1, axis=0), 0.0)
    end = (SUBS - 1) * (steps + PAD) + PAD + steps
    told[pl.ds(LAST, PAYLOAD - LAST), :] = jnp.zeros((PAYLOAD - LAST, LANES), f32)
    told[pl.ds(LAST, 2), :] = query_ref[0].astype(f32)[14:]
    for j in range(2):
        told[pl.ds(FIRST + 2 * j, 2), :] = xs[j, pl.ds(PAD, 2), :]
        told[pl.ds(LAST + 2 + 2 * j, 2), :] = xs[j, pl.ds(end - 2, 2), :]
    told_ref[...] = told[...].astype(bf16)


def gate_kernel(at_ref, x_ref, sf_ref, rate_ref, res_ref, p_ref, start_ref, *refs):
    told_refs, (out_ref, xs, ys, told) = refs[:-4], refs[-4:]
    n_modes = rate_ref.shape[0]
    steps = p_ref.shape[0]
    n_tok = SUBS * steps
    me = at_ref[0]
    rows = lax.broadcasted_iota(jnp.int32, (SUBS, LANES), 0)

    told[0] = jnp.zeros((PAYLOAD, LANES), f32)
    for n, ref in enumerate(told_refs):
        told[1 + neighbour(me, n)] = ref[...].astype(f32)

    def first_products(j):
        taps = []
        for i in range(2):
            row = lambda slot, at: told[slot, pl.ds(at, 1), :]
            x = [row(j, LAST + 2 + 2 * i), row(j, LAST + 3 + 2 * i), row(1 + j, FIRST + 2 * i), row(1 + j, FIRST + 1 + 2 * i)]
            w = [sf_ref[k, i + 1][None] for k in range(3)]
            taps.append([w[0] * x[t + 2] + w[1] * x[t + 1] + w[2] * x[t] for t in range(2)])
        return [(taps[0][t] * taps[1][t]).astype(bf16).astype(f32) for t in range(2)]

    rates = rate_ref[...]
    late = [jnp.exp(-rates * (n_tok - 1 - t)) for t in range(2)]
    enter_all = jnp.zeros_like(rates)
    for j in range(len(told_refs) - 1):
        p0, p1 = first_products(j)
        ended = told[1 + j, :n_modes, :] + late[0] * p0 + late[1] * p1
        gap = (jnp.maximum(me - 1 - j, 0) * n_tok).astype(f32)
        enter_all = enter_all + jnp.where(j < me, jnp.exp(-rates * gap), 0.0) * ended
    told[0, pl.ds(0, n_modes), :] = enter_all
    p_first = [jnp.broadcast_to(p, (SUBS, LANES)) for p in first_products(me)]

    fill(xs, x_ref.at[0], told[me, pl.ds(LAST, 2), :], steps)
    w = [jnp.broadcast_to(sf_ref[k, 0][None], (SUBS, LANES)) for k in range(3)]
    decay, gain, state0 = [], [], []
    for r in range(n_modes):
        rate = jnp.broadcast_to(rate_ref[pl.ds(r, 1), :], (SUBS, LANES))
        enter = jnp.broadcast_to(told[0, pl.ds(r, 1), :], (SUBS, LANES))
        decay.append(jnp.exp(-rate))
        gain.append(jnp.broadcast_to(res_ref[pl.ds(r, 1), :], (SUBS, LANES)))
        passed = (rows * steps).astype(f32)
        mine = jnp.exp(-rate * (passed - 1.0)) * p_first[0] + jnp.exp(-rate * (passed - 2.0)) * p_first[1]
        state0.append(start_ref[r] + jnp.exp(-rate * passed) * enter + jnp.where(rows >= 1, mine, 0.0))

    def tap(at):
        return xs[pl.ds(PAD + at, SUBS, stride=steps + PAD), :]

    def body(t, carry, first=None):
        x1, x2, state = carry
        x0 = tap(t)
        gate = w[0] * x0 + w[1] * x1 + w[2] * x2
        p = p_ref[t]
        if first is not None:
            p = jnp.where(rows >= 1, p, first)
        state = tuple(a * s + p for a, s in zip(decay, state))
        parts = [c * s for c, s in zip(gain, state)]
        while len(parts) > 1:
            parts = [a + b for a, b in zip(parts[::2], parts[1::2])]
        ys[pl.ds(t, SUBS, stride=steps + PAD), :] = gate * parts[0]
        return (x0, x1, state)

    carry = (tap(-1), tap(-2), tuple(state0))
    carry = body(1, body(0, carry, p_first[0]), p_first[1])
    lax.fori_loop(2, steps, body, carry, unroll=6)
    for s in range(SUBS):
        out_ref[pl.ds(s * steps, steps), :] = ys[pl.ds(s * (steps + PAD), steps), :].astype(bf16)


def neighbour(me, n):
    return (me // 4 + n // 4) % 2 * 4 + (me + 8 - n) % 4


def states(x, sf, rate):
    _, n_tok, width = x.shape
    modes = rate.shape[0]
    steps = n_tok // SUBS
    col = lambda g: (0, g)
    three = lambda g: (0, 0, g)
    return pl.pallas_call(
        state_kernel,
        grid=(width // LANES,),
        in_specs=[
            pl.BlockSpec((1, n_tok, LANES), lambda g: (1, 0, g)),
            pl.BlockSpec((1, n_tok, LANES), lambda g: (2, 0, g)),
            pl.BlockSpec((1, 16, LANES), lambda g: (0, n_tok // 16 - 1, g)),
            pl.BlockSpec((3, 3, LANES), three),
            pl.BlockSpec((modes, LANES), col),
        ],
        out_specs=[
            pl.BlockSpec((steps, SUBS, LANES), three),
            pl.BlockSpec((PAYLOAD, LANES), col),
            pl.BlockSpec((modes, SUBS, LANES), three),
        ],
        out_shape=[
            jax.ShapeDtypeStruct((steps, SUBS, width), f32),
            jax.ShapeDtypeStruct((PAYLOAD, width), bf16),
            jax.ShapeDtypeStruct((modes, SUBS, width), f32),
        ],
        scratch_shapes=[pltpu.VMEM((2, n_tok + SUBS * PAD, LANES), f32), pltpu.VMEM((PAYLOAD, LANES), f32)],
        compiler_params=pltpu.CompilerParams(vmem_limit_bytes=60 << 20),
        name="states",
    )(x, x, x, sf, rate)


def gated(at, x, sf, rate, res, p, start, told):
    _, n_tok, width = x.shape
    modes = rate.shape[0]
    steps = n_tok // SUBS
    col = lambda g: (0, g)
    three = lambda g: (0, 0, g)
    return pl.pallas_call(
        gate_kernel,
        grid=(width // LANES,),
        in_specs=[
            pl.BlockSpec(memory_space=pltpu.SMEM),
            pl.BlockSpec((1, n_tok, LANES), three),
            pl.BlockSpec((3, 3, LANES), three),
            pl.BlockSpec((modes, LANES), col),
            pl.BlockSpec((modes, LANES), col),
            pl.BlockSpec((steps, SUBS, LANES), three),
            pl.BlockSpec((modes, SUBS, LANES), three),
        ]
        + [pl.BlockSpec((PAYLOAD, LANES), col)] * len(told),
        out_specs=pl.BlockSpec((n_tok, LANES), col),
        out_shape=jax.ShapeDtypeStruct((n_tok, width), bf16),
        scratch_shapes=[
            pltpu.VMEM((n_tok + SUBS * PAD, LANES), f32),
            pltpu.VMEM((n_tok + SUBS * PAD, LANES), f32),
            pltpu.VMEM((len(told) + 1, PAYLOAD, LANES), f32),
        ],
        compiler_params=pltpu.CompilerParams(vmem_limit_bytes=60 << 20),
        name="gated",
    )(at, x, sf, rate, res, p, start, *told)


def spread(x, axis, target):
    pairs = [(i, target(i)) for i in range(lax.axis_size(axis))]
    return lax.ppermute(x, axis, [(i, j) for i, j in pairs if j is not None])


def to_core(x):
    return spread(x, "ch", lambda i: i ^ 1)


def to_far_z(x):
    return spread(x, "ch", lambda i: i ^ 2)


def to_y(x, by):
    return spread(x, "ch", lambda i: (i + 4 * by) % 16)


def to_block(x, n):
    return spread(x, "ctx", lambda i: (i // 4 + n // 4) % 2 * 4 + (i + n) % 4)


def project_kernel(plan, n_added, cols_ref, g_ref, gp_ref, w_ref, wp_ref, *refs):
    added, refs = refs[:n_added], refs[n_added:]
    out_refs, (acts, weights, act_sems, weight_sems) = refs[:-4], refs[-4:]
    depth = g_ref.shape[1]
    act_copies = [pltpu.make_async_copy(r, acts.at[j], act_sems.at[j]) for j, r in enumerate((g_ref, gp_ref))]
    copies = []
    for k, (col, _) in enumerate(plan):
        at = pl.ds(pl.multiple_of(cols_ref[col] * depth, depth), depth)
        pair = [
            pltpu.make_async_copy(source.at[:, at], weights.at[k, j], weight_sems.at[k, j])
            for j, source in enumerate((w_ref, wp_ref))
        ]
        for copy in act_copies + pair if k == 0 else pair:
            copy.start()
        copies.append(pair)
    for k, (_, pieces) in enumerate(plan):
        for copy in act_copies + copies[k] if k == 0 else copies[k]:
            copy.wait()
        for first, count, out, slot, extra in pieces:
            rows = pl.ds(first, count)
            acc = jnp.dot(acts[0, rows, :], weights[k, 0], preferred_element_type=f32)
            acc = acc + jnp.dot(acts[1, rows, :], weights[k, 1], preferred_element_type=f32)
            if extra is not None:
                acc = acc + added[extra[0]][extra[1]].astype(f32)
            out_refs[out][slot] = acc.astype(bf16)


def project(operands, plan, counts, added=(), limit=50):
    cols, g, gp, w, wp = operands
    n_tok, depth = g.shape
    slots = [0] * len(counts)
    laid = []
    for (dy, dz), pieces in plan:
        mine = []
        for first, out, *extra in pieces:
            mine.append((first, counts[out], out, slots[out], extra[0] if extra else None))
            slots[out] += 1
        laid.append((2 * dy + dz, mine))
    vmem = pl.BlockSpec(memory_space=pltpu.VMEM)
    anywhere = pl.BlockSpec(memory_space=pl.ANY)
    return pl.pallas_call(
        functools.partial(project_kernel, laid, len(added)),
        in_specs=[pl.BlockSpec(memory_space=pltpu.SMEM)] + [anywhere] * 4 + [vmem] * len(added),
        out_specs=[vmem] * len(counts),
        out_shape=[jax.ShapeDtypeStruct((n, count, depth), bf16) for n, count in zip(slots, counts)],
        scratch_shapes=[
            pltpu.VMEM((2, n_tok, depth), bf16),
            pltpu.VMEM((len(plan), 2, depth, depth), bf16),
            pltpu.SemaphoreType.DMA((2,)),
            pltpu.SemaphoreType.DMA((len(plan), 2)),
        ],
        compiler_params=pltpu.CompilerParams(vmem_limit_bytes=limit << 20),
        name="project",
    )(cols, g, gp, w, wp, *added)


def total(*parts):
    return sum(p.astype(f32) for p in parts).astype(bf16)


Z_TOK = 320


def per_device(features, short_filter, decay_rate, residues, out_weight):
    n_tok = features.shape[0]
    x = features.transpose(1, 0, 2)
    weight_pair = to_core(out_weight)
    me = lax.axis_index("ch")
    steps = jnp.arange(8, dtype=jnp.int32)
    cols = (me // 4 + steps // 2) % 4 * 4 + (me // 2 + steps) % 2 * 2 + me % 2
    product, told, start = states(x, short_filter, decay_rate)
    heard = [told] + [to_block(told, n) for n in range(1, 8)]
    at = lax.axis_index("ctx").astype(jnp.int32)[None]
    mine = gated(at, x, short_filter, decay_rate, residues, product, start, heard)
    operands = (cols, mine, to_core(mine), out_weight, weight_pair)
    n_y = n_tok - Z_TOK
    a, b, z = 0, n_y // 2, n_y

    up2, down2 = project(operands, [((2, dz), [(a, 0), (b, 1)]) for dz in (1, 0)], [b, b], limit=59)
    up2, down2 = to_y(up2, 1), to_y(down2, -1)
    (far,) = project(operands, [((dy, 1), [(z, 0)]) for dy in range(4)], [Z_TOK])
    far = to_far_z(far)

    up, down, up_more, down_more, keep_a, keep_b = project(
        operands,
        [((1, 1), [(b, 0), (a, 2)]), ((3, 1), [(a, 1), (b, 3)]), ((0, 1), [(a, 4), (b, 5)])],
        [b] * 6,
    )
    up, down = to_y(up[0], 1), to_y(down[0], -1)
    up_more, down_more = to_y(total(up_more[0], up2[0]), 1), to_y(total(down_more[0], down2[0]), -1)
    rise, fall, stay_a, stay_b = project(
        operands,
        [((1, 0), [(b, 0), (a, 0, (0, 1))]), ((3, 0), [(a, 1), (b, 1, (1, 1))]), ((0, 0), [(a, 2), (b, 3)])],
        [b] * 4,
        [up2, down2],
    )
    rise, fall = to_y(rise, 1), to_y(fall, -1)
    last = (cols, lax.optimization_barrier((mine, stay_a))[0]) + operands[2:]
    (near,) = project(last, [((dy, 0), [(z, 0)]) for dy in range(4)], [Z_TOK])
    up, down, up_more, down_more = lax.optimization_barrier((up, down, up_more, down_more))
    over = to_far_z(jnp.stack([total(keep_a[0], up_more, down), total(keep_b[0], up, down_more)]))
    rise, fall = lax.optimization_barrier((rise, fall))
    done_a = total(stay_a[0], rise[1], fall[0], over[0])
    done_b = total(stay_b[0], rise[0], fall[1], over[1])

    half = Z_TOK // 2
    s2a, s2b = to_y(total(near[2, :half], far[2, :half]), 1), to_y(total(near[2, half:], far[2, half:]), -1)
    s3 = jnp.concatenate([total(near[3, :half], far[3, :half]), total(near[3, half:], far[3, half:], s2b)])
    s1 = jnp.concatenate([total(near[1, :half], far[1, :half], s2a), total(near[1, half:], far[1, half:])])
    s1, s3 = to_y(s1, 1), to_y(s3, -1)
    return jnp.concatenate([done_a, done_b, total(near[0], far[0], s1, s3)])


def solution(mesh):
    placed = (P("ctx", None, "ch"), P(None, None, "ch"), P(None, "ch"), P(None, "ch"), P("ch", None))
    return jax.shard_map(per_device, mesh=mesh, in_specs=placed, out_specs=P("ctx", "ch"), check_vma=False)
```

```python
import functools

import jax
import jax.numpy as jnp
from jax import lax
from jax.experimental import pallas as pl
from jax.experimental.pallas import tpu as pltpu
from jax.sharding import PartitionSpec as P

f32, bf16 = jnp.float32, jnp.bfloat16
LANES = 128
SUBS = 8
PAD = 8
STATE_ROWS, FIRST, LAST, PAYLOAD = 16, 16, 20, 32


def row_scan(values, factor, rows):
    step = 1
    while step < SUBS:
        back = jnp.where(rows >= step, pltpu.roll(values, step, axis=0), 0.0)
        values = values + factor * back
        factor = factor * factor
        step *= 2
    return values


def fill(rows_ref, x_ref, halo, steps):
    for s in range(SUBS):
        at = s * (steps + PAD) + PAD
        rows_ref[pl.ds(at, steps), :] = x_ref[pl.ds(s * steps, steps), :].astype(f32)
        before = x_ref[pl.ds(s * steps - 16, 16), :].astype(f32)[14:] if s else halo
        rows_ref[pl.ds(at - 2, 2), :] = before


def state_kernel(key_ref, val_ref, query_ref, sf_ref, rate_ref, p_ref, told_ref, start_ref, xs, told):
    n_modes = rate_ref.shape[0]
    steps = p_ref.shape[0]
    rows = lax.broadcasted_iota(jnp.int32, (SUBS, LANES), 0)
    none = jnp.zeros((2, LANES), f32)
    for j in range(2):
        fill(xs.at[j], (key_ref, val_ref)[j].at[0], none, steps)
    w = [[jnp.broadcast_to(sf_ref[k, j + 1][None], (SUBS, LANES)) for k in range(3)] for j in range(2)]
    decay = [jnp.exp(-jnp.broadcast_to(rate_ref[pl.ds(r, 1), :], (SUBS, LANES))) for r in range(n_modes)]

    def tap(j, at):
        return xs[j, pl.ds(PAD + at, SUBS, stride=steps + PAD), :]

    def body(t, carry, first=False):
        k1, k2, v1, v2, state = carry
        k0, v0 = tap(0, t), tap(1, t)
        key = w[0][0] * k0 + w[0][1] * k1 + w[0][2] * k2
        val = w[1][0] * v0 + w[1][1] * v1 + w[1][2] * v2
        p = (key * val).astype(bf16).astype(f32)
        if first:
            p = jnp.where(rows >= 1, p, 0.0)
        p_ref[t] = p
        state = tuple(a * s + p for a, s in zip(decay, state))
        return (k0, k1, v0, v1, state)

    zero = jnp.zeros((SUBS, LANES), f32)
    carry = (tap(0, -1), tap(0, -2), tap(1, -1), tap(1, -2), (zero,) * n_modes)
    carry = body(1, body(0, carry, True), True)
    state = lax.fori_loop(2, steps, body, carry, unroll=7)[4]
    for r in range(n_modes):
        rate = jnp.broadcast_to(rate_ref[pl.ds(r, 1), :], (SUBS, LANES))
        scanned = row_scan(state[r], jnp.exp(-rate * steps), rows)
        told[pl.ds(r, 1), :] = scanned[SUBS - 1 :]
        start_ref[r] = jnp.where(rows >= 1, pltpu.roll(scanned, 1, axis=0), 0.0)
    end = (SUBS - 1) * (steps + PAD) + PAD + steps
    told[pl.ds(LAST, PAYLOAD - LAST), :] = jnp.zeros((PAYLOAD - LAST, LANES), f32)
    told[pl.ds(LAST, 2), :] = query_ref[0].astype(f32)[14:]
    for j in range(2):
        told[pl.ds(FIRST + 2 * j, 2), :] = xs[j, pl.ds(PAD, 2), :]
        told[pl.ds(LAST + 2 + 2 * j, 2), :] = xs[j, pl.ds(end - 2, 2), :]
    told_ref[...] = told[...].astype(bf16)


def gate_kernel(at_ref, x_ref, sf_ref, rate_ref, res_ref, p_ref, start_ref, *refs):
    told_refs, (out_ref, xs, ys, told) = refs[:-4], refs[-4:]
    n_modes = rate_ref.shape[0]
    steps = p_ref.shape[0]
    n_tok = SUBS * steps
    me = at_ref[0]
    rows = lax.broadcasted_iota(jnp.int32, (SUBS, LANES), 0)

    told[0] = jnp.zeros((PAYLOAD, LANES), f32)
    for n, ref in enumerate(told_refs):
        for k in range(2):
            told[1 + neighbour(me, n, k)] = ref[k].astype(f32)

    def first_products(j):
        taps = []
        for i in range(2):
            row = lambda slot, at: told[slot, pl.ds(at, 1), :]
            x = [row(j, LAST + 2 + 2 * i), row(j, LAST + 3 + 2 * i), row(1 + j, FIRST + 2 * i), row(1 + j, FIRST + 1 + 2 * i)]
            w = [sf_ref[k, i + 1][None] for k in range(3)]
            taps.append([w[0] * x[t + 2] + w[1] * x[t + 1] + w[2] * x[t] for t in range(2)])
        return [(taps[0][t] * taps[1][t]).astype(bf16).astype(f32) for t in range(2)]

    rates = rate_ref[...]
    late = [jnp.exp(-rates * (n_tok - 1 - t)) for t in range(2)]
    enter_all = jnp.zeros_like(rates)
    for j in range(2 * len(told_refs) - 1):
        p0, p1 = first_products(j)
        ended = told[1 + j, :n_modes, :] + late[0] * p0 + late[1] * p1
        gap = (jnp.maximum(me - 1 - j, 0) * n_tok).astype(f32)
        enter_all = enter_all + jnp.where(j < me, jnp.exp(-rates * gap), 0.0) * ended
    told[0, pl.ds(0, n_modes), :] = enter_all
    p_first = [jnp.broadcast_to(p, (SUBS, LANES)) for p in first_products(me)]

    fill(xs, x_ref.at[0], told[me, pl.ds(LAST, 2), :], steps)
    w = [jnp.broadcast_to(sf_ref[k, 0][None], (SUBS, LANES)) for k in range(3)]
    decay, gain, state0 = [], [], []
    for r in range(n_modes):
        rate = jnp.broadcast_to(rate_ref[pl.ds(r, 1), :], (SUBS, LANES))
        enter = jnp.broadcast_to(told[0, pl.ds(r, 1), :], (SUBS, LANES))
        decay.append(jnp.exp(-rate))
        gain.append(jnp.broadcast_to(res_ref[pl.ds(r, 1), :], (SUBS, LANES)))
        passed = (rows * steps).astype(f32)
        mine = jnp.exp(-rate * (passed - 1.0)) * p_first[0] + jnp.exp(-rate * (passed - 2.0)) * p_first[1]
        state0.append(start_ref[r] + jnp.exp(-rate * passed) * enter + jnp.where(rows >= 1, mine, 0.0))

    def tap(at):
        return xs[pl.ds(PAD + at, SUBS, stride=steps + PAD), :]

    def body(t, carry, first=None):
        x1, x2, state = carry
        x0 = tap(t)
        gate = w[0] * x0 + w[1] * x1 + w[2] * x2
        p = p_ref[t]
        if first is not None:
            p = jnp.where(rows >= 1, p, first)
        state = tuple(a * s + p for a, s in zip(decay, state))
        parts = [c * s for c, s in zip(gain, state)]
        while len(parts) > 1:
            parts = [a + b for a, b in zip(parts[::2], parts[1::2])]
        ys[pl.ds(t, SUBS, stride=steps + PAD), :] = gate * parts[0]
        return (x0, x1, state)

    carry = (tap(-1), tap(-2), tuple(state0))
    carry = body(1, body(0, carry, p_first[0]), p_first[1])
    lax.fori_loop(2, steps, body, carry, unroll=6)
    for s in range(SUBS):
        out_ref[pl.ds(s * steps, steps), :] = ys[pl.ds(s * (steps + PAD), steps), :].astype(bf16)


def neighbour(me, n, k):
    return (me // 4 + k) % 2 * 4 + (me + 4 - n) % 4


def states(x, sf, rate):
    _, n_tok, width = x.shape
    modes = rate.shape[0]
    steps = n_tok // SUBS
    col = lambda g: (0, g)
    three = lambda g: (0, 0, g)
    return pl.pallas_call(
        state_kernel,
        grid=(width // LANES,),
        in_specs=[
            pl.BlockSpec((1, n_tok, LANES), lambda g: (1, 0, g)),
            pl.BlockSpec((1, n_tok, LANES), lambda g: (2, 0, g)),
            pl.BlockSpec((1, 16, LANES), lambda g: (0, n_tok // 16 - 1, g)),
            pl.BlockSpec((3, 3, LANES), three),
            pl.BlockSpec((modes, LANES), col),
        ],
        out_specs=[
            pl.BlockSpec((steps, SUBS, LANES), three),
            pl.BlockSpec((PAYLOAD, LANES), col),
            pl.BlockSpec((modes, SUBS, LANES), three),
        ],
        out_shape=[
            jax.ShapeDtypeStruct((steps, SUBS, width), f32),
            jax.ShapeDtypeStruct((PAYLOAD, width), bf16),
            jax.ShapeDtypeStruct((modes, SUBS, width), f32),
        ],
        scratch_shapes=[pltpu.VMEM((2, n_tok + SUBS * PAD, LANES), f32), pltpu.VMEM((PAYLOAD, LANES), f32)],
        compiler_params=pltpu.CompilerParams(vmem_limit_bytes=60 << 20),
        name="states",
    )(x, x, x, sf, rate)


def gated(at, x, sf, rate, res, p, start, told):
    _, n_tok, width = x.shape
    modes = rate.shape[0]
    steps = n_tok // SUBS
    col = lambda g: (0, g)
    three = lambda g: (0, 0, g)
    return pl.pallas_call(
        gate_kernel,
        grid=(width // LANES,),
        in_specs=[
            pl.BlockSpec(memory_space=pltpu.SMEM),
            pl.BlockSpec((1, n_tok, LANES), three),
            pl.BlockSpec((3, 3, LANES), three),
            pl.BlockSpec((modes, LANES), col),
            pl.BlockSpec((modes, LANES), col),
            pl.BlockSpec((steps, SUBS, LANES), three),
            pl.BlockSpec((modes, SUBS, LANES), three),
        ]
        + [pl.BlockSpec((2, PAYLOAD, LANES), three)] * len(told),
        out_specs=pl.BlockSpec((n_tok, LANES), col),
        out_shape=jax.ShapeDtypeStruct((n_tok, width), bf16),
        scratch_shapes=[
            pltpu.VMEM((n_tok + SUBS * PAD, LANES), f32),
            pltpu.VMEM((n_tok + SUBS * PAD, LANES), f32),
            pltpu.VMEM((2 * len(told) + 1, PAYLOAD, LANES), f32),
        ],
        compiler_params=pltpu.CompilerParams(vmem_limit_bytes=60 << 20),
        name="gated",
    )(at, x, sf, rate, res, p, start, *told)


def spread(x, axis, target):
    pairs = [(i, target(i)) for i in range(lax.axis_size(axis))]
    return lax.ppermute(x, axis, [(i, j) for i, j in pairs if j is not None])


def to_core(x):
    return spread(x, "ch", lambda i: i ^ 1)


def to_far_z(x):
    return spread(x, "ch", lambda i: i ^ 2)


def to_y(x, by):
    return spread(x, "ch", lambda i: (i + 4 * by) % 16)


def to_x(x, by):
    return spread(x, "ctx", lambda i: i // 4 * 4 + (i + by) % 4)


def to_near_z(x):
    return spread(x, "ctx", lambda i: (i + 4) % 8)


def project_kernel(plan, n_added, cols_ref, g_ref, gp_ref, w_ref, wp_ref, *refs):
    added, refs = refs[:n_added], refs[n_added:]
    out_refs, (acts, weights, act_sems, weight_sems) = refs[:-4], refs[-4:]
    depth = g_ref.shape[1]
    act_copies = [pltpu.make_async_copy(r, acts.at[j], act_sems.at[j]) for j, r in enumerate((g_ref, gp_ref))]
    copies = []
    for k, (col, _) in enumerate(plan):
        at = pl.ds(pl.multiple_of(cols_ref[col] * depth, depth), depth)
        pair = [
            pltpu.make_async_copy(source.at[:, at], weights.at[k, j], weight_sems.at[k, j])
            for j, source in enumerate((w_ref, wp_ref))
        ]
        for copy in act_copies + pair if k == 0 else pair:
            copy.start()
        copies.append(pair)
    for k, (_, pieces) in enumerate(plan):
        for copy in act_copies + copies[k] if k == 0 else copies[k]:
            copy.wait()
        for first, count, out, slot, extra in pieces:
            rows = pl.ds(first, count)
            acc = jnp.dot(acts[0, rows, :], weights[k, 0], preferred_element_type=f32)
            acc = acc + jnp.dot(acts[1, rows, :], weights[k, 1], preferred_element_type=f32)
            if extra is not None:
                acc = acc + added[extra[0]][extra[1]].astype(f32)
            out_refs[out][slot] = acc.astype(bf16)


def project(operands, plan, counts, added=()):
    cols, g, gp, w, wp = operands
    n_tok, depth = g.shape
    slots = [0] * len(counts)
    laid = []
    for (dy, dz), pieces in plan:
        mine = []
        for first, out, *extra in pieces:
            mine.append((first, counts[out], out, slots[out], extra[0] if extra else None))
            slots[out] += 1
        laid.append((2 * dy + dz, mine))
    vmem = pl.BlockSpec(memory_space=pltpu.VMEM)
    anywhere = pl.BlockSpec(memory_space=pl.ANY)
    return pl.pallas_call(
        functools.partial(project_kernel, laid, len(added)),
        in_specs=[pl.BlockSpec(memory_space=pltpu.SMEM)] + [anywhere] * 4 + [vmem] * len(added),
        out_specs=[vmem] * len(counts),
        out_shape=[jax.ShapeDtypeStruct((n, count, depth), bf16) for n, count in zip(slots, counts)],
        scratch_shapes=[
            pltpu.VMEM((2, n_tok, depth), bf16),
            pltpu.VMEM((len(plan), 2, depth, depth), bf16),
            pltpu.SemaphoreType.DMA((2,)),
            pltpu.SemaphoreType.DMA((len(plan), 2)),
        ],
        compiler_params=pltpu.CompilerParams(vmem_limit_bytes=50 << 20),
        name="project",
    )(cols, g, gp, w, wp, *added)


def total(*parts):
    return sum(p.astype(f32) for p in parts).astype(bf16)


Z_TOK = 320


def per_device(features, short_filter, decay_rate, residues, out_weight):
    n_tok = features.shape[0]
    x = features.transpose(1, 0, 2)
    weight_pair = to_core(out_weight)
    me = lax.axis_index("ch")
    steps = jnp.arange(8, dtype=jnp.int32)
    cols = (me // 4 + steps // 2) % 4 * 4 + (me // 2 + steps) % 2 * 2 + me % 2
    product, told, start = states(x, short_filter, decay_rate)
    told = jnp.stack([told, to_near_z(told)])
    heard = [told] + [to_x(told, n) for n in (1, 2, 3)]
    at = lax.axis_index("ctx").astype(jnp.int32)[None]
    mine = gated(at, x, short_filter, decay_rate, residues, product, start, heard)
    operands = (cols, mine, to_core(mine), out_weight, weight_pair)
    n_y = n_tok - Z_TOK
    a, b, z = 0, n_y // 2, n_y

    up2, down2, far = project(
        operands,
        [((2, 1), [(a, 0), (b, 1), (z, 2)]), ((2, 0), [(a, 0), (b, 1)])] + [((dy, 1), [(z, 2)]) for dy in (3, 1, 0)],
        [b, b, Z_TOK],
    )
    up2, down2, far = to_y(up2, 1), to_y(down2, -1), to_far_z(far)
    up, down, up_more, down_more, keep_a, keep_b = project(
        operands,
        [((1, 1), [(b, 0), (a, 2)]), ((3, 1), [(a, 1), (b, 3)]), ((0, 1), [(a, 4), (b, 5)])],
        [b] * 6,
    )
    up, down = to_y(up[0], 1), to_y(down[0], -1)
    up_more, down_more = to_y(total(up_more[0], up2[0]), 1), to_y(total(down_more[0], down2[0]), -1)
    rise, fall, rise_more, fall_more, stay_a, stay_b = project(
        operands,
        [((1, 0), [(b, 0), (a, 2, (0, 1))]), ((3, 0), [(a, 1), (b, 3, (1, 1))]), ((0, 0), [(a, 4), (b, 5)])],
        [b] * 6,
        [up2, down2],
    )
    last = (cols, lax.optimization_barrier((mine, stay_a))[0]) + operands[2:]
    (near,) = project(last, [((dy, 0), [(z, 0)]) for dy in (2, 3, 1, 0)], [Z_TOK])
    half = Z_TOK // 2
    s2a, s2b = total(near[0, :half], far[0, :half]), total(near[0, half:], far[0, half:])
    rise, fall = to_y(rise[0], 1), to_y(fall[0], -1)
    rise_more, fall_more, _, _ = lax.optimization_barrier((rise_more[0], fall_more[0], s2a, s2b))
    s2a, s2b = to_y(s2a, 1), to_y(s2b, -1)
    rise_more, fall_more = to_y(rise_more, 1), to_y(fall_more, -1)
    up, down, up_more, down_more = lax.optimization_barrier((up, down, up_more, down_more))
    over = to_far_z(jnp.stack([total(keep_a[0], up_more, down), total(keep_b[0], up, down_more)]))
    rise, fall, rise_more, fall_more = lax.optimization_barrier((rise, fall, rise_more, fall_more))
    done_a = total(stay_a[0], rise_more, fall, over[0])
    done_b = total(stay_b[0], rise, fall_more, over[1])

    s3 = jnp.concatenate([total(near[1, :half], far[1, :half]), total(near[1, half:], far[1, half:], s2b)])
    s1 = jnp.concatenate([total(near[2, :half], far[2, :half], s2a), total(near[2, half:], far[2, half:])])
    s1, s3 = to_y(s1, 1), to_y(s3, -1)
    return jnp.concatenate([done_a, done_b, total(near[3], far[3], s1, s3)])


def solution(mesh):
    placed = (P("ctx", None, "ch"), P(None, None, "ch"), P(None, "ch"), P(None, "ch"), P("ch", None))
    return jax.shard_map(per_device, mesh=mesh, in_specs=placed, out_specs=P("ctx", "ch"), check_vma=False)
```

```python
import functools

import jax
import jax.numpy as jnp
from jax import lax
from jax.experimental import pallas as pl
from jax.experimental.pallas import tpu as pltpu
from jax.sharding import PartitionSpec as P

f32, bf16 = jnp.float32, jnp.bfloat16
LANES = 128
SUBS = 8
PAD = 8
STATE_ROWS, FIRST, LAST, PAYLOAD = 16, 16, 20, 32


def row_scan(values, factor, rows):
    step = 1
    while step < SUBS:
        back = jnp.where(rows >= step, pltpu.roll(values, step, axis=0), 0.0)
        values = values + factor * back
        factor = factor * factor
        step *= 2
    return values


def fill(rows_ref, x_ref, halo, steps):
    for s in range(SUBS):
        at = s * (steps + PAD) + PAD
        rows_ref[pl.ds(at, steps), :] = x_ref[pl.ds(s * steps, steps), :].astype(f32)
        before = x_ref[pl.ds(s * steps - 16, 16), :].astype(f32)[14:] if s else halo
        rows_ref[pl.ds(at - 2, 2), :] = before


def state_kernel(key_ref, val_ref, query_ref, sf_ref, rate_ref, p_ref, told_ref, start_ref, xs, told):
    n_modes = rate_ref.shape[0]
    steps = p_ref.shape[0]
    rows = lax.broadcasted_iota(jnp.int32, (SUBS, LANES), 0)
    none = jnp.zeros((2, LANES), f32)
    for j in range(2):
        fill(xs.at[j], (key_ref, val_ref)[j].at[0], none, steps)
    w = [[jnp.broadcast_to(sf_ref[k, j + 1][None], (SUBS, LANES)) for k in range(3)] for j in range(2)]
    decay = [jnp.exp(-jnp.broadcast_to(rate_ref[pl.ds(r, 1), :], (SUBS, LANES))) for r in range(n_modes)]

    def tap(j, at):
        return xs[j, pl.ds(PAD + at, SUBS, stride=steps + PAD), :]

    def body(t, carry, first=False):
        k1, k2, v1, v2, state = carry
        k0, v0 = tap(0, t), tap(1, t)
        key = w[0][0] * k0 + w[0][1] * k1 + w[0][2] * k2
        val = w[1][0] * v0 + w[1][1] * v1 + w[1][2] * v2
        p = (key * val).astype(bf16).astype(f32)
        if first:
            p = jnp.where(rows >= 1, p, 0.0)
        p_ref[t] = p
        state = tuple(a * s + p for a, s in zip(decay, state))
        return (k0, k1, v0, v1, state)

    zero = jnp.zeros((SUBS, LANES), f32)
    carry = (tap(0, -1), tap(0, -2), tap(1, -1), tap(1, -2), (zero,) * n_modes)
    carry = body(1, body(0, carry, True), True)
    state = lax.fori_loop(2, steps, body, carry, unroll=7)[4]
    for r in range(n_modes):
        rate = jnp.broadcast_to(rate_ref[pl.ds(r, 1), :], (SUBS, LANES))
        scanned = row_scan(state[r], jnp.exp(-rate * steps), rows)
        told[pl.ds(r, 1), :] = scanned[SUBS - 1 :]
        start_ref[r] = jnp.where(rows >= 1, pltpu.roll(scanned, 1, axis=0), 0.0)
    end = (SUBS - 1) * (steps + PAD) + PAD + steps
    told[pl.ds(LAST, PAYLOAD - LAST), :] = jnp.zeros((PAYLOAD - LAST, LANES), f32)
    told[pl.ds(LAST, 2), :] = query_ref[0].astype(f32)[14:]
    for j in range(2):
        told[pl.ds(FIRST + 2 * j, 2), :] = xs[j, pl.ds(PAD, 2), :]
        told[pl.ds(LAST + 2 + 2 * j, 2), :] = xs[j, pl.ds(end - 2, 2), :]
    told_ref[...] = told[...].astype(bf16)


def gate_kernel(at_ref, x_ref, sf_ref, rate_ref, res_ref, p_ref, start_ref, *refs):
    told_refs, (out_ref, xs, ys, told) = refs[:-4], refs[-4:]
    n_modes = rate_ref.shape[0]
    steps = p_ref.shape[0]
    n_tok = SUBS * steps
    me = at_ref[0]
    rows = lax.broadcasted_iota(jnp.int32, (SUBS, LANES), 0)

    told[0] = jnp.zeros((PAYLOAD, LANES), f32)
    for n, ref in enumerate(told_refs):
        for k in range(2):
            told[1 + neighbour(me, n, k)] = ref[k].astype(f32)

    def first_products(j):
        taps = []
        for i in range(2):
            row = lambda slot, at: told[slot, pl.ds(at, 1), :]
            x = [row(j, LAST + 2 + 2 * i), row(j, LAST + 3 + 2 * i), row(1 + j, FIRST + 2 * i), row(1 + j, FIRST + 1 + 2 * i)]
            w = [sf_ref[k, i + 1][None] for k in range(3)]
            taps.append([w[0] * x[t + 2] + w[1] * x[t + 1] + w[2] * x[t] for t in range(2)])
        return [(taps[0][t] * taps[1][t]).astype(bf16).astype(f32) for t in range(2)]

    rates = rate_ref[...]
    late = [jnp.exp(-rates * (n_tok - 1 - t)) for t in range(2)]
    enter_all = jnp.zeros_like(rates)
    for j in range(2 * len(told_refs) - 1):
        p0, p1 = first_products(j)
        ended = told[1 + j, :n_modes, :] + late[0] * p0 + late[1] * p1
        gap = (jnp.maximum(me - 1 - j, 0) * n_tok).astype(f32)
        enter_all = enter_all + jnp.where(j < me, jnp.exp(-rates * gap), 0.0) * ended
    told[0, pl.ds(0, n_modes), :] = enter_all
    p_first = [jnp.broadcast_to(p, (SUBS, LANES)) for p in first_products(me)]

    fill(xs, x_ref.at[0], told[me, pl.ds(LAST, 2), :], steps)
    w = [jnp.broadcast_to(sf_ref[k, 0][None], (SUBS, LANES)) for k in range(3)]
    decay, gain, state0 = [], [], []
    for r in range(n_modes):
        rate = jnp.broadcast_to(rate_ref[pl.ds(r, 1), :], (SUBS, LANES))
        enter = jnp.broadcast_to(told[0, pl.ds(r, 1), :], (SUBS, LANES))
        decay.append(jnp.exp(-rate))
        gain.append(jnp.broadcast_to(res_ref[pl.ds(r, 1), :], (SUBS, LANES)))
        passed = (rows * steps).astype(f32)
        mine = jnp.exp(-rate * (passed - 1.0)) * p_first[0] + jnp.exp(-rate * (passed - 2.0)) * p_first[1]
        state0.append(start_ref[r] + jnp.exp(-rate * passed) * enter + jnp.where(rows >= 1, mine, 0.0))

    def tap(at):
        return xs[pl.ds(PAD + at, SUBS, stride=steps + PAD), :]

    def body(t, carry, first=None):
        x1, x2, state = carry
        x0 = tap(t)
        gate = w[0] * x0 + w[1] * x1 + w[2] * x2
        p = p_ref[t]
        if first is not None:
            p = jnp.where(rows >= 1, p, first)
        state = tuple(a * s + p for a, s in zip(decay, state))
        parts = [c * s for c, s in zip(gain, state)]
        while len(parts) > 1:
            parts = [a + b for a, b in zip(parts[::2], parts[1::2])]
        ys[pl.ds(t, SUBS, stride=steps + PAD), :] = gate * parts[0]
        return (x0, x1, state)

    carry = (tap(-1), tap(-2), tuple(state0))
    carry = body(1, body(0, carry, p_first[0]), p_first[1])
    lax.fori_loop(2, steps, body, carry, unroll=6)
    for s in range(SUBS):
        out_ref[pl.ds(s * steps, steps), :] = ys[pl.ds(s * (steps + PAD), steps), :].astype(bf16)


def neighbour(me, n, k):
    return (me // 4 + k) % 2 * 4 + (me + 4 - n) % 4


def states(x, sf, rate):
    _, n_tok, width = x.shape
    modes = rate.shape[0]
    steps = n_tok // SUBS
    col = lambda g: (0, g)
    three = lambda g: (0, 0, g)
    return pl.pallas_call(
        state_kernel,
        grid=(width // LANES,),
        in_specs=[
            pl.BlockSpec((1, n_tok, LANES), lambda g: (1, 0, g)),
            pl.BlockSpec((1, n_tok, LANES), lambda g: (2, 0, g)),
            pl.BlockSpec((1, 16, LANES), lambda g: (0, n_tok // 16 - 1, g)),
            pl.BlockSpec((3, 3, LANES), three),
            pl.BlockSpec((modes, LANES), col),
        ],
        out_specs=[
            pl.BlockSpec((steps, SUBS, LANES), three),
            pl.BlockSpec((PAYLOAD, LANES), col),
            pl.BlockSpec((modes, SUBS, LANES), three),
        ],
        out_shape=[
            jax.ShapeDtypeStruct((steps, SUBS, width), f32),
            jax.ShapeDtypeStruct((PAYLOAD, width), bf16),
            jax.ShapeDtypeStruct((modes, SUBS, width), f32),
        ],
        scratch_shapes=[pltpu.VMEM((2, n_tok + SUBS * PAD, LANES), f32), pltpu.VMEM((PAYLOAD, LANES), f32)],
        compiler_params=pltpu.CompilerParams(vmem_limit_bytes=60 << 20),
        name="states",
    )(x, x, x, sf, rate)


def gated(at, x, sf, rate, res, p, start, told):
    _, n_tok, width = x.shape
    modes = rate.shape[0]
    steps = n_tok // SUBS
    col = lambda g: (0, g)
    three = lambda g: (0, 0, g)
    return pl.pallas_call(
        gate_kernel,
        grid=(width // LANES,),
        in_specs=[
            pl.BlockSpec(memory_space=pltpu.SMEM),
            pl.BlockSpec((1, n_tok, LANES), three),
            pl.BlockSpec((3, 3, LANES), three),
            pl.BlockSpec((modes, LANES), col),
            pl.BlockSpec((modes, LANES), col),
            pl.BlockSpec((steps, SUBS, LANES), three),
            pl.BlockSpec((modes, SUBS, LANES), three),
        ]
        + [pl.BlockSpec((2, PAYLOAD, LANES), three)] * len(told),
        out_specs=pl.BlockSpec((n_tok, LANES), col),
        out_shape=jax.ShapeDtypeStruct((n_tok, width), bf16),
        scratch_shapes=[
            pltpu.VMEM((n_tok + SUBS * PAD, LANES), f32),
            pltpu.VMEM((n_tok + SUBS * PAD, LANES), f32),
            pltpu.VMEM((2 * len(told) + 1, PAYLOAD, LANES), f32),
        ],
        compiler_params=pltpu.CompilerParams(vmem_limit_bytes=48 << 20),
        name="gated",
    )(at, x, sf, rate, res, p, start, *told)


def spread(x, axis, target):
    pairs = [(i, target(i)) for i in range(lax.axis_size(axis))]
    return lax.ppermute(x, axis, [(i, j) for i, j in pairs if j is not None])


def to_core(x):
    return spread(x, "ch", lambda i: i ^ 1)


def to_far_z(x):
    return spread(x, "ch", lambda i: i ^ 2)


def to_y(x, by):
    return spread(x, "ch", lambda i: (i + 4 * by) % 16)


def to_x(x, by):
    return spread(x, "ctx", lambda i: i // 4 * 4 + (i + by) % 4)


def to_near_z(x):
    return spread(x, "ctx", lambda i: (i + 4) % 8)


def project_kernel(plan, n_added, cols_ref, g_ref, gp_ref, w_ref, wp_ref, *refs):
    added, refs = refs[:n_added], refs[n_added:]
    out_refs, (acts, weights, act_sems, weight_sems) = refs[:-4], refs[-4:]
    depth = g_ref.shape[1]
    act_copies = [pltpu.make_async_copy(r, acts.at[j], act_sems.at[j]) for j, r in enumerate((g_ref, gp_ref))]
    copies = []
    for k, (col, _) in enumerate(plan):
        at = pl.ds(pl.multiple_of(cols_ref[col] * depth, depth), depth)
        pair = [
            pltpu.make_async_copy(source.at[:, at], weights.at[k, j], weight_sems.at[k, j])
            for j, source in enumerate((w_ref, wp_ref))
        ]
        for copy in act_copies + pair if k == 0 else pair:
            copy.start()
        copies.append(pair)
    for k, (_, pieces) in enumerate(plan):
        for copy in act_copies + copies[k] if k == 0 else copies[k]:
            copy.wait()
        for first, count, out, slot, extra in pieces:
            rows = pl.ds(first, count)
            acc = jnp.dot(acts[0, rows, :], weights[k, 0], preferred_element_type=f32)
            acc = acc + jnp.dot(acts[1, rows, :], weights[k, 1], preferred_element_type=f32)
            if extra is not None:
                acc = acc + added[extra[0]][extra[1]].astype(f32)
            out_refs[out][slot] = acc.astype(bf16)


def project(operands, plan, counts, added=()):
    cols, g, gp, w, wp = operands
    n_tok, depth = g.shape
    slots = [0] * len(counts)
    laid = []
    for (dy, dz), pieces in plan:
        mine = []
        for first, out, *extra in pieces:
            mine.append((first, counts[out], out, slots[out], extra[0] if extra else None))
            slots[out] += 1
        laid.append((2 * dy + dz, mine))
    vmem = pl.BlockSpec(memory_space=pltpu.VMEM)
    anywhere = pl.BlockSpec(memory_space=pl.ANY)
    return pl.pallas_call(
        functools.partial(project_kernel, laid, len(added)),
        in_specs=[pl.BlockSpec(memory_space=pltpu.SMEM)] + [anywhere] * 4 + [vmem] * len(added),
        out_specs=[vmem] * len(counts),
        out_shape=[jax.ShapeDtypeStruct((n, count, depth), bf16) for n, count in zip(slots, counts)],
        scratch_shapes=[
            pltpu.VMEM((2, n_tok, depth), bf16),
            pltpu.VMEM((len(plan), 2, depth, depth), bf16),
            pltpu.SemaphoreType.DMA((2,)),
            pltpu.SemaphoreType.DMA((len(plan), 2)),
        ],
        compiler_params=pltpu.CompilerParams(vmem_limit_bytes=50 << 20),
        name="project",
    )(cols, g, gp, w, wp, *added)


def total(*parts):
    return sum(p.astype(f32) for p in parts).astype(bf16)


Z_TOK = 320


def per_device(features, short_filter, decay_rate, residues, out_weight):
    n_tok = features.shape[0]
    x = features.transpose(1, 0, 2)
    weight_pair = to_core(out_weight)
    me = lax.axis_index("ch")
    steps = jnp.arange(8, dtype=jnp.int32)
    cols = (me // 4 + steps // 2) % 4 * 4 + (me // 2 + steps) % 2 * 2 + me % 2
    product, told, start = states(x, short_filter, decay_rate)
    told = jnp.stack([told, to_near_z(told)])
    heard = [told] + [to_x(told, n) for n in (1, 2, 3)]
    at = lax.axis_index("ctx").astype(jnp.int32)[None]
    mine = gated(at, x, short_filter, decay_rate, residues, product, start, heard)
    operands = (cols, mine, to_core(mine), out_weight, weight_pair)
    n_y = n_tok - Z_TOK
    a, b, z = 0, n_y // 2, n_y

    up2, down2 = project(operands, [((2, dz), [(a, 0), (b, 1)]) for dz in (1, 0)], [b, b])
    up2, down2 = to_y(up2, 1), to_y(down2, -1)
    (far,) = project(operands, [((dy, 1), [(z, 0)]) for dy in (0, 1, 2, 3)], [Z_TOK])
    far = to_far_z(far)
    up, down, up_more, down_more, keep_a, keep_b = project(
        operands,
        [((1, 1), [(b, 0), (a, 2)]), ((3, 1), [(a, 1), (b, 3)]), ((0, 1), [(a, 4), (b, 5)])],
        [b] * 6,
    )
    up, down = to_y(up[0], 1), to_y(down[0], -1)
    up_more, down_more = to_y(total(up_more[0], up2[0]), 1), to_y(total(down_more[0], down2[0]), -1)
    rise, fall, rise_more, fall_more, stay_a, stay_b = project(
        operands,
        [((1, 0), [(b, 0), (a, 2, (0, 1))]), ((3, 0), [(a, 1), (b, 3, (1, 1))]), ((0, 0), [(a, 4), (b, 5)])],
        [b] * 6,
        [up2, down2],
    )
    last = (cols, lax.optimization_barrier((mine, stay_a))[0]) + operands[2:]
    (near,) = project(last, [((dy, 0), [(z, 0)]) for dy in (2, 3, 1, 0)], [Z_TOK])
    half = Z_TOK // 2
    s2a, s2b = total(near[0, :half], far[2, :half]), total(near[0, half:], far[2, half:])
    rise, fall = to_y(rise[0], 1), to_y(fall[0], -1)
    rise_more, fall_more, _, _ = lax.optimization_barrier((rise_more[0], fall_more[0], s2a, s2b))
    s2a, s2b = to_y(s2a, 1), to_y(s2b, -1)
    rise_more, fall_more = to_y(rise_more, 1), to_y(fall_more, -1)
    up, down, up_more, down_more = lax.optimization_barrier((up, down, up_more, down_more))
    over = to_far_z(jnp.stack([total(keep_a[0], up_more, down), total(keep_b[0], up, down_more)]))
    rise, fall, rise_more, fall_more = lax.optimization_barrier((rise, fall, rise_more, fall_more))
    done_a = total(stay_a[0], rise_more, fall, over[0])
    done_b = total(stay_b[0], rise, fall_more, over[1])

    s3 = jnp.concatenate([total(near[1, :half], far[3, :half]), total(near[1, half:], far[3, half:], s2b)])
    s1 = jnp.concatenate([total(near[2, :half], far[1, :half], s2a), total(near[2, half:], far[1, half:])])
    s1, s3 = to_y(s1, 1), to_y(s3, -1)
    return jnp.concatenate([done_a, done_b, total(near[3], far[0], s1, s3)])


def solution(mesh):
    placed = (P("ctx", None, "ch"), P(None, None, "ch"), P(None, "ch"), P(None, "ch"), P("ch", None))
    return jax.shard_map(per_device, mesh=mesh, in_specs=placed, out_specs=P("ctx", "ch"), check_vma=False)
```

```python
import functools

import jax
import jax.numpy as jnp
from jax import lax
from jax.experimental import pallas as pl
from jax.experimental.pallas import tpu as pltpu
from jax.sharding import PartitionSpec as P

f32, bf16 = jnp.float32, jnp.bfloat16
LANES = 128
SUBS = 8
PAD = 8
STATE_ROWS, FIRST, LAST, PAYLOAD = 16, 16, 20, 32


def row_scan(values, factor, rows):
    step = 1
    while step < SUBS:
        back = jnp.where(rows >= step, pltpu.roll(values, step, axis=0), 0.0)
        values = values + factor * back
        factor = factor * factor
        step *= 2
    return values


def fill(rows_ref, x_ref, halo, steps):
    for s in range(SUBS):
        at = s * (steps + PAD) + PAD
        rows_ref[pl.ds(at, steps), :] = x_ref[pl.ds(s * steps, steps), :].astype(f32)
        before = x_ref[pl.ds(s * steps - 16, 16), :].astype(f32)[14:] if s else halo
        rows_ref[pl.ds(at - 2, 2), :] = before


def state_kernel(key_ref, val_ref, query_ref, sf_ref, rate_ref, p_ref, told_ref, start_ref, xs, told):
    n_modes = rate_ref.shape[0]
    steps = p_ref.shape[0]
    rows = lax.broadcasted_iota(jnp.int32, (SUBS, LANES), 0)
    none = jnp.zeros((2, LANES), f32)
    for j in range(2):
        fill(xs.at[j], (key_ref, val_ref)[j].at[0], none, steps)
    w = [[jnp.broadcast_to(sf_ref[k, j + 1][None], (SUBS, LANES)) for k in range(3)] for j in range(2)]
    decay = [jnp.exp(-jnp.broadcast_to(rate_ref[pl.ds(r, 1), :], (SUBS, LANES))) for r in range(n_modes)]

    def tap(j, at):
        return xs[j, pl.ds(PAD + at, SUBS, stride=steps + PAD), :]

    def body(t, carry, first=False):
        k1, k2, v1, v2, state = carry
        k0, v0 = tap(0, t), tap(1, t)
        key = w[0][0] * k0 + w[0][1] * k1 + w[0][2] * k2
        val = w[1][0] * v0 + w[1][1] * v1 + w[1][2] * v2
        p = (key * val).astype(bf16).astype(f32)
        if first:
            p = jnp.where(rows >= 1, p, 0.0)
        p_ref[t] = p
        state = tuple(a * s + p for a, s in zip(decay, state))
        return (k0, k1, v0, v1, state)

    zero = jnp.zeros((SUBS, LANES), f32)
    carry = (tap(0, -1), tap(0, -2), tap(1, -1), tap(1, -2), (zero,) * n_modes)
    carry = body(1, body(0, carry, True), True)
    state = lax.fori_loop(2, steps, body, carry, unroll=7)[4]
    for r in range(n_modes):
        rate = jnp.broadcast_to(rate_ref[pl.ds(r, 1), :], (SUBS, LANES))
        scanned = row_scan(state[r], jnp.exp(-rate * steps), rows)
        told[pl.ds(r, 1), :] = scanned[SUBS - 1 :]
        start_ref[r] = jnp.where(rows >= 1, pltpu.roll(scanned, 1, axis=0), 0.0)
    end = (SUBS - 1) * (steps + PAD) + PAD + steps
    told[pl.ds(LAST, PAYLOAD - LAST), :] = jnp.zeros((PAYLOAD - LAST, LANES), f32)
    told[pl.ds(LAST, 2), :] = query_ref[0].astype(f32)[14:]
    for j in range(2):
        told[pl.ds(FIRST + 2 * j, 2), :] = xs[j, pl.ds(PAD, 2), :]
        told[pl.ds(LAST + 2 + 2 * j, 2), :] = xs[j, pl.ds(end - 2, 2), :]
    told_ref[...] = told[...].astype(bf16)


def gate_kernel(at_ref, x_ref, sf_ref, rate_ref, res_ref, p_ref, start_ref, *refs):
    told_refs, (out_ref, xs, ys, told) = refs[:-4], refs[-4:]
    n_modes = rate_ref.shape[0]
    steps = p_ref.shape[0]
    n_tok = SUBS * steps
    me = at_ref[0]
    rows = lax.broadcasted_iota(jnp.int32, (SUBS, LANES), 0)

    told[0] = jnp.zeros((PAYLOAD, LANES), f32)
    for n, ref in enumerate(told_refs):
        for k in range(2):
            told[1 + neighbour(me, n, k)] = ref[k].astype(f32)

    def first_products(j):
        taps = []
        for i in range(2):
            row = lambda slot, at: told[slot, pl.ds(at, 1), :]
            x = [row(j, LAST + 2 + 2 * i), row(j, LAST + 3 + 2 * i), row(1 + j, FIRST + 2 * i), row(1 + j, FIRST + 1 + 2 * i)]
            w = [sf_ref[k, i + 1][None] for k in range(3)]
            taps.append([w[0] * x[t + 2] + w[1] * x[t + 1] + w[2] * x[t] for t in range(2)])
        return [(taps[0][t] * taps[1][t]).astype(bf16).astype(f32) for t in range(2)]

    rates = rate_ref[...]
    late = [jnp.exp(-rates * (n_tok - 1 - t)) for t in range(2)]
    enter_all = jnp.zeros_like(rates)
    for j in range(2 * len(told_refs) - 1):
        p0, p1 = first_products(j)
        ended = told[1 + j, :n_modes, :] + late[0] * p0 + late[1] * p1
        gap = (jnp.maximum(me - 1 - j, 0) * n_tok).astype(f32)
        enter_all = enter_all + jnp.where(j < me, jnp.exp(-rates * gap), 0.0) * ended
    told[0, pl.ds(0, n_modes), :] = enter_all
    p_first = [jnp.broadcast_to(p, (SUBS, LANES)) for p in first_products(me)]

    fill(xs, x_ref.at[0], told[me, pl.ds(LAST, 2), :], steps)
    w = [jnp.broadcast_to(sf_ref[k, 0][None], (SUBS, LANES)) for k in range(3)]
    decay, gain, state0 = [], [], []
    for r in range(n_modes):
        rate = jnp.broadcast_to(rate_ref[pl.ds(r, 1), :], (SUBS, LANES))
        enter = jnp.broadcast_to(told[0, pl.ds(r, 1), :], (SUBS, LANES))
        decay.append(jnp.exp(-rate))
        gain.append(jnp.broadcast_to(res_ref[pl.ds(r, 1), :], (SUBS, LANES)))
        passed = (rows * steps).astype(f32)
        mine = jnp.exp(-rate * (passed - 1.0)) * p_first[0] + jnp.exp(-rate * (passed - 2.0)) * p_first[1]
        state0.append(start_ref[r] + jnp.exp(-rate * passed) * enter + jnp.where(rows >= 1, mine, 0.0))

    def tap(at):
        return xs[pl.ds(PAD + at, SUBS, stride=steps + PAD), :]

    def body(t, carry, first=None):
        x1, x2, state = carry
        x0 = tap(t)
        gate = w[0] * x0 + w[1] * x1 + w[2] * x2
        p = p_ref[t]
        if first is not None:
            p = jnp.where(rows >= 1, p, first)
        state = tuple(a * s + p for a, s in zip(decay, state))
        parts = [c * s for c, s in zip(gain, state)]
        while len(parts) > 1:
            parts = [a + b for a, b in zip(parts[::2], parts[1::2])]
        ys[pl.ds(t, SUBS, stride=steps + PAD), :] = gate * parts[0]
        return (x0, x1, state)

    carry = (tap(-1), tap(-2), tuple(state0))
    carry = body(1, body(0, carry, p_first[0]), p_first[1])
    lax.fori_loop(2, steps, body, carry, unroll=6)
    for s in range(SUBS):
        out_ref[pl.ds(s * steps, steps), :] = ys[pl.ds(s * (steps + PAD), steps), :].astype(bf16)


def neighbour(me, n, k):
    return (me // 4 + k) % 2 * 4 + (me + 4 - n) % 4


def states(x, sf, rate):
    _, n_tok, width = x.shape
    modes = rate.shape[0]
    steps = n_tok // SUBS
    col = lambda g: (0, g)
    three = lambda g: (0, 0, g)
    return pl.pallas_call(
        state_kernel,
        grid=(width // LANES,),
        in_specs=[
            pl.BlockSpec((1, n_tok, LANES), lambda g: (1, 0, g)),
            pl.BlockSpec((1, n_tok, LANES), lambda g: (2, 0, g)),
            pl.BlockSpec((1, 16, LANES), lambda g: (0, n_tok // 16 - 1, g)),
            pl.BlockSpec((3, 3, LANES), three),
            pl.BlockSpec((modes, LANES), col),
        ],
        out_specs=[
            pl.BlockSpec((steps, SUBS, LANES), three),
            pl.BlockSpec((PAYLOAD, LANES), col),
            pl.BlockSpec((modes, SUBS, LANES), three),
        ],
        out_shape=[
            jax.ShapeDtypeStruct((steps, SUBS, width), f32),
            jax.ShapeDtypeStruct((PAYLOAD, width), bf16),
            jax.ShapeDtypeStruct((modes, SUBS, width), f32),
        ],
        scratch_shapes=[pltpu.VMEM((2, n_tok + SUBS * PAD, LANES), f32), pltpu.VMEM((PAYLOAD, LANES), f32)],
        compiler_params=pltpu.CompilerParams(vmem_limit_bytes=60 << 20),
        name="states",
    )(x, x, x, sf, rate)


def gated(at, x, sf, rate, res, p, start, told):
    _, n_tok, width = x.shape
    modes = rate.shape[0]
    steps = n_tok // SUBS
    col = lambda g: (0, g)
    three = lambda g: (0, 0, g)
    return pl.pallas_call(
        gate_kernel,
        grid=(width // LANES,),
        in_specs=[
            pl.BlockSpec(memory_space=pltpu.SMEM),
            pl.BlockSpec((1, n_tok, LANES), three),
            pl.BlockSpec((3, 3, LANES), three),
            pl.BlockSpec((modes, LANES), col),
            pl.BlockSpec((modes, LANES), col),
            pl.BlockSpec((steps, SUBS, LANES), three),
            pl.BlockSpec((modes, SUBS, LANES), three),
        ]
        + [pl.BlockSpec((2, PAYLOAD, LANES), three)] * len(told),
        out_specs=pl.BlockSpec((n_tok, LANES), col),
        out_shape=jax.ShapeDtypeStruct((n_tok, width), bf16),
        scratch_shapes=[
            pltpu.VMEM((n_tok + SUBS * PAD, LANES), f32),
            pltpu.VMEM((n_tok + SUBS * PAD, LANES), f32),
            pltpu.VMEM((2 * len(told) + 1, PAYLOAD, LANES), f32),
        ],
        compiler_params=pltpu.CompilerParams(vmem_limit_bytes=48 << 20),
        name="gated",
    )(at, x, sf, rate, res, p, start, *told)


def spread(x, axis, target):
    pairs = [(i, target(i)) for i in range(lax.axis_size(axis))]
    return lax.ppermute(x, axis, [(i, j) for i, j in pairs if j is not None])


def to_core(x):
    return spread(x, "ch", lambda i: i ^ 1)


def to_far_z(x):
    return spread(x, "ch", lambda i: i ^ 2)


def to_y(x, by):
    return spread(x, "ch", lambda i: (i + 4 * by) % 16)


def to_x(x, by):
    return spread(x, "ctx", lambda i: i // 4 * 4 + (i + by) % 4)


def to_near_z(x):
    return spread(x, "ctx", lambda i: (i + 4) % 8)


def project_kernel(plan, n_added, cols_ref, g_ref, gp_ref, w_ref, wp_ref, *refs):
    added, refs = refs[:n_added], refs[n_added:]
    out_refs, (acts, weights, act_sems, weight_sems) = refs[:-4], refs[-4:]
    depth = g_ref.shape[1]
    act_copies = [pltpu.make_async_copy(r, acts.at[j], act_sems.at[j]) for j, r in enumerate((g_ref, gp_ref))]
    copies = []
    for k, (col, _) in enumerate(plan):
        at = pl.ds(pl.multiple_of(cols_ref[col] * depth, depth), depth)
        pair = [
            pltpu.make_async_copy(source.at[:, at], weights.at[k, j], weight_sems.at[k, j])
            for j, source in enumerate((w_ref, wp_ref))
        ]
        for copy in act_copies + pair if k == 0 else pair:
            copy.start()
        copies.append(pair)
    for k, (_, pieces) in enumerate(plan):
        for copy in act_copies + copies[k] if k == 0 else copies[k]:
            copy.wait()
        for first, count, out, slot, extra in pieces:
            rows = pl.ds(first, count)
            acc = jnp.dot(acts[0, rows, :], weights[k, 0], preferred_element_type=f32)
            acc = acc + jnp.dot(acts[1, rows, :], weights[k, 1], preferred_element_type=f32)
            if extra is not None:
                acc = acc + added[extra[0]][extra[1]].astype(f32)
            out_refs[out][slot] = acc.astype(bf16)


def project(operands, plan, counts, added=(), limit=50):
    cols, g, gp, w, wp = operands
    n_tok, depth = g.shape
    slots = [0] * len(counts)
    laid = []
    for (dy, dz), pieces in plan:
        mine = []
        for first, out, *extra in pieces:
            mine.append((first, counts[out], out, slots[out], extra[0] if extra else None))
            slots[out] += 1
        laid.append((2 * dy + dz, mine))
    vmem = pl.BlockSpec(memory_space=pltpu.VMEM)
    anywhere = pl.BlockSpec(memory_space=pl.ANY)
    return pl.pallas_call(
        functools.partial(project_kernel, laid, len(added)),
        in_specs=[pl.BlockSpec(memory_space=pltpu.SMEM)] + [anywhere] * 4 + [vmem] * len(added),
        out_specs=[vmem] * len(counts),
        out_shape=[jax.ShapeDtypeStruct((n, count, depth), bf16) for n, count in zip(slots, counts)],
        scratch_shapes=[
            pltpu.VMEM((2, n_tok, depth), bf16),
            pltpu.VMEM((len(plan), 2, depth, depth), bf16),
            pltpu.SemaphoreType.DMA((2,)),
            pltpu.SemaphoreType.DMA((len(plan), 2)),
        ],
        compiler_params=pltpu.CompilerParams(vmem_limit_bytes=limit << 20),
        name="project",
    )(cols, g, gp, w, wp, *added)


def total(*parts):
    return sum(p.astype(f32) for p in parts).astype(bf16)


Z_TOK = 352


def per_device(features, short_filter, decay_rate, residues, out_weight):
    n_tok = features.shape[0]
    x = features.transpose(1, 0, 2)
    weight_pair = to_core(out_weight)
    me = lax.axis_index("ch")
    steps = jnp.arange(8, dtype=jnp.int32)
    cols = (me // 4 + steps // 2) % 4 * 4 + (me // 2 + steps) % 2 * 2 + me % 2
    product, told, start = states(x, short_filter, decay_rate)
    told = jnp.stack([told, to_near_z(told)])
    heard = [told] + [to_x(told, n) for n in (1, 2, 3)]
    at = lax.axis_index("ctx").astype(jnp.int32)[None]
    mine = gated(at, x, short_filter, decay_rate, residues, product, start, heard)
    operands = (cols, mine, to_core(mine), out_weight, weight_pair)
    n_y = n_tok - Z_TOK
    a, b, z = 0, n_y // 2, n_y

    up2, down2 = project(operands, [((2, dz), [(a, 0), (b, 1)]) for dz in (1, 0)], [b, b], limit=50)
    up2, down2 = to_y(up2, 1), to_y(down2, -1)
    (far,) = project(operands, [((dy, 1), [(z, 0)]) for dy in (0, 1, 2, 3)], [Z_TOK])
    far = to_far_z(far)
    up, down, up_more, down_more, keep_a, keep_b = project(
        operands,
        [((1, 1), [(b, 0), (a, 2)]), ((3, 1), [(a, 1), (b, 3)]), ((0, 1), [(a, 4), (b, 5)])],
        [b] * 6,
    )
    up, down = to_y(up[0], 1), to_y(down[0], -1)
    up_more, down_more = to_y(total(up_more[0], up2[0]), 1), to_y(total(down_more[0], down2[0]), -1)
    rise, fall, stay_a, stay_b = project(
        operands,
        [((1, 0), [(b, 0), (a, 0, (0, 1))]), ((3, 0), [(a, 1), (b, 1, (1, 1))]), ((0, 0), [(a, 2), (b, 3)])],
        [b] * 4,
        [up2, down2],
    )
    last = (cols, lax.optimization_barrier((mine, stay_a))[0]) + operands[2:]
    (near,) = project(last, [((dy, 0), [(z, 0)]) for dy in (2, 3, 1, 0)], [Z_TOK])
    one, two, three = (total(near[i], far[dy]) for i, dy in ((2, 1), (0, 2), (1, 3)))
    rise, fall = to_y(rise, 1), to_y(fall, -1)
    one, two, three = to_y(one, 1), to_y(two, 2), to_y(three, -1)
    up, down, up_more, down_more = lax.optimization_barrier((up, down, up_more, down_more))
    over = to_far_z(jnp.stack([total(keep_a[0], up_more, down), total(keep_b[0], up, down_more)]))
    rise, fall = lax.optimization_barrier((rise, fall))
    done_a = total(stay_a[0], rise[1], fall[0], over[0])
    done_b = total(stay_b[0], rise[0], fall[1], over[1])

    return jnp.concatenate([done_a, done_b, total(near[3], far[0], one, two, three)])


def solution(mesh):
    placed = (P("ctx", None, "ch"), P(None, None, "ch"), P(None, "ch"), P(None, "ch"), P("ch", None))
    return jax.shard_map(per_device, mesh=mesh, in_specs=placed, out_specs=P("ctx", "ch"), check_vma=False)
```

```python
import functools

import jax
import jax.numpy as jnp
from jax import lax
from jax.experimental import pallas as pl
from jax.experimental.pallas import tpu as pltpu
from jax.sharding import PartitionSpec as P

f32, bf16 = jnp.float32, jnp.bfloat16
LANES = 128
SUBS = 8
PAD = 8
STATE_ROWS, FIRST, LAST, PAYLOAD = 16, 16, 20, 32


def row_scan(values, factor, rows):
    step = 1
    while step < SUBS:
        back = jnp.where(rows >= step, pltpu.roll(values, step, axis=0), 0.0)
        values = values + factor * back
        factor = factor * factor
        step *= 2
    return values


def fill(rows_ref, x_ref, halo, steps):
    for s in range(SUBS):
        at = s * (steps + PAD) + PAD
        rows_ref[pl.ds(at, steps), :] = x_ref[pl.ds(s * steps, steps), :].astype(f32)
        before = x_ref[pl.ds(s * steps - 16, 16), :].astype(f32)[14:] if s else halo
        rows_ref[pl.ds(at - 2, 2), :] = before


def state_kernel(key_ref, val_ref, query_ref, sf_ref, rate_ref, p_ref, told_ref, start_ref, xs, told):
    n_modes = rate_ref.shape[0]
    steps = p_ref.shape[0]
    rows = lax.broadcasted_iota(jnp.int32, (SUBS, LANES), 0)
    none = jnp.zeros((2, LANES), f32)
    for j in range(2):
        fill(xs.at[j], (key_ref, val_ref)[j].at[0], none, steps)
    w = [[jnp.broadcast_to(sf_ref[k, j + 1][None], (SUBS, LANES)) for k in range(3)] for j in range(2)]
    decay = [jnp.exp(-jnp.broadcast_to(rate_ref[pl.ds(r, 1), :], (SUBS, LANES))) for r in range(n_modes)]

    def tap(j, at):
        return xs[j, pl.ds(PAD + at, SUBS, stride=steps + PAD), :]

    def body(t, carry, first=False):
        k1, k2, v1, v2, state = carry
        k0, v0 = tap(0, t), tap(1, t)
        key = w[0][0] * k0 + w[0][1] * k1 + w[0][2] * k2
        val = w[1][0] * v0 + w[1][1] * v1 + w[1][2] * v2
        p = (key * val).astype(bf16).astype(f32)
        if first:
            p = jnp.where(rows >= 1, p, 0.0)
        p_ref[t] = p
        state = tuple(a * s + p for a, s in zip(decay, state))
        return (k0, k1, v0, v1, state)

    zero = jnp.zeros((SUBS, LANES), f32)
    carry = (tap(0, -1), tap(0, -2), tap(1, -1), tap(1, -2), (zero,) * n_modes)
    carry = body(1, body(0, carry, True), True)
    state = lax.fori_loop(2, steps, body, carry, unroll=7)[4]
    for r in range(n_modes):
        rate = jnp.broadcast_to(rate_ref[pl.ds(r, 1), :], (SUBS, LANES))
        scanned = row_scan(state[r], jnp.exp(-rate * steps), rows)
        told[pl.ds(r, 1), :] = scanned[SUBS - 1 :]
        start_ref[r] = jnp.where(rows >= 1, pltpu.roll(scanned, 1, axis=0), 0.0)
    end = (SUBS - 1) * (steps + PAD) + PAD + steps
    told[pl.ds(LAST, PAYLOAD - LAST), :] = jnp.zeros((PAYLOAD - LAST, LANES), f32)
    told[pl.ds(LAST, 2), :] = query_ref[0].astype(f32)[14:]
    for j in range(2):
        told[pl.ds(FIRST + 2 * j, 2), :] = xs[j, pl.ds(PAD, 2), :]
        told[pl.ds(LAST + 2 + 2 * j, 2), :] = xs[j, pl.ds(end - 2, 2), :]
    told_ref[...] = told[...].astype(bf16)


def gate_kernel(at_ref, x_ref, sf_ref, rate_ref, res_ref, p_ref, start_ref, *refs):
    told_refs, (out_ref, xs, ys, told) = refs[:-4], refs[-4:]
    n_modes = rate_ref.shape[0]
    steps = p_ref.shape[0]
    n_tok = SUBS * steps
    me = at_ref[0]
    rows = lax.broadcasted_iota(jnp.int32, (SUBS, LANES), 0)

    told[0] = jnp.zeros((PAYLOAD, LANES), f32)
    for n, ref in enumerate(told_refs):
        for k in range(2):
            told[1 + neighbour(me, n, k)] = ref[k].astype(f32)

    def first_products(j):
        taps = []
        for i in range(2):
            row = lambda slot, at: told[slot, pl.ds(at, 1), :]
            x = [row(j, LAST + 2 + 2 * i), row(j, LAST + 3 + 2 * i), row(1 + j, FIRST + 2 * i), row(1 + j, FIRST + 1 + 2 * i)]
            w = [sf_ref[k, i + 1][None] for k in range(3)]
            taps.append([w[0] * x[t + 2] + w[1] * x[t + 1] + w[2] * x[t] for t in range(2)])
        return [(taps[0][t] * taps[1][t]).astype(bf16).astype(f32) for t in range(2)]

    rates = rate_ref[...]
    late = [jnp.exp(-rates * (n_tok - 1 - t)) for t in range(2)]
    enter_all = jnp.zeros_like(rates)
    for j in range(2 * len(told_refs) - 1):
        p0, p1 = first_products(j)
        ended = told[1 + j, :n_modes, :] + late[0] * p0 + late[1] * p1
        gap = (jnp.maximum(me - 1 - j, 0) * n_tok).astype(f32)
        enter_all = enter_all + jnp.where(j < me, jnp.exp(-rates * gap), 0.0) * ended
    told[0, pl.ds(0, n_modes), :] = enter_all
    p_first = [jnp.broadcast_to(p, (SUBS, LANES)) for p in first_products(me)]

    fill(xs, x_ref.at[0], told[me, pl.ds(LAST, 2), :], steps)
    w = [jnp.broadcast_to(sf_ref[k, 0][None], (SUBS, LANES)) for k in range(3)]
    decay, gain, state0 = [], [], []
    for r in range(n_modes):
        rate = jnp.broadcast_to(rate_ref[pl.ds(r, 1), :], (SUBS, LANES))
        enter = jnp.broadcast_to(told[0, pl.ds(r, 1), :], (SUBS, LANES))
        decay.append(jnp.exp(-rate))
        gain.append(jnp.broadcast_to(res_ref[pl.ds(r, 1), :], (SUBS, LANES)))
        passed = (rows * steps).astype(f32)
        mine = jnp.exp(-rate * (passed - 1.0)) * p_first[0] + jnp.exp(-rate * (passed - 2.0)) * p_first[1]
        state0.append(start_ref[r] + jnp.exp(-rate * passed) * enter + jnp.where(rows >= 1, mine, 0.0))

    def tap(at):
        return xs[pl.ds(PAD + at, SUBS, stride=steps + PAD), :]

    def body(t, carry, first=None):
        x1, x2, state = carry
        x0 = tap(t)
        gate = w[0] * x0 + w[1] * x1 + w[2] * x2
        p = p_ref[t]
        if first is not None:
            p = jnp.where(rows >= 1, p, first)
        state = tuple(a * s + p for a, s in zip(decay, state))
        parts = [c * s for c, s in zip(gain, state)]
        while len(parts) > 1:
            parts = [a + b for a, b in zip(parts[::2], parts[1::2])]
        ys[pl.ds(t, SUBS, stride=steps + PAD), :] = gate * parts[0]
        return (x0, x1, state)

    carry = (tap(-1), tap(-2), tuple(state0))
    carry = body(1, body(0, carry, p_first[0]), p_first[1])
    lax.fori_loop(2, steps, body, carry, unroll=6)
    for s in range(SUBS):
        out_ref[pl.ds(s * steps, steps), :] = ys[pl.ds(s * (steps + PAD), steps), :].astype(bf16)


def neighbour(me, n, k):
    return (me // 4 + k) % 2 * 4 + (me + 4 - n) % 4


def states(x, sf, rate):
    _, n_tok, width = x.shape
    modes = rate.shape[0]
    steps = n_tok // SUBS
    col = lambda g: (0, g)
    three = lambda g: (0, 0, g)
    return pl.pallas_call(
        state_kernel,
        grid=(width // LANES,),
        in_specs=[
            pl.BlockSpec((1, n_tok, LANES), lambda g: (1, 0, g)),
            pl.BlockSpec((1, n_tok, LANES), lambda g: (2, 0, g)),
            pl.BlockSpec((1, 16, LANES), lambda g: (0, n_tok // 16 - 1, g)),
            pl.BlockSpec((3, 3, LANES), three),
            pl.BlockSpec((modes, LANES), col),
        ],
        out_specs=[
            pl.BlockSpec((steps, SUBS, LANES), three),
            pl.BlockSpec((PAYLOAD, LANES), col),
            pl.BlockSpec((modes, SUBS, LANES), three),
        ],
        out_shape=[
            jax.ShapeDtypeStruct((steps, SUBS, width), f32),
            jax.ShapeDtypeStruct((PAYLOAD, width), bf16),
            jax.ShapeDtypeStruct((modes, SUBS, width), f32),
        ],
        scratch_shapes=[pltpu.VMEM((2, n_tok + SUBS * PAD, LANES), f32), pltpu.VMEM((PAYLOAD, LANES), f32)],
        compiler_params=pltpu.CompilerParams(vmem_limit_bytes=60 << 20),
        name="states",
    )(x, x, x, sf, rate)


def gated(at, x, sf, rate, res, p, start, told):
    _, n_tok, width = x.shape
    modes = rate.shape[0]
    steps = n_tok // SUBS
    col = lambda g: (0, g)
    three = lambda g: (0, 0, g)
    return pl.pallas_call(
        gate_kernel,
        grid=(width // LANES,),
        in_specs=[
            pl.BlockSpec(memory_space=pltpu.SMEM),
            pl.BlockSpec((1, n_tok, LANES), three),
            pl.BlockSpec((3, 3, LANES), three),
            pl.BlockSpec((modes, LANES), col),
            pl.BlockSpec((modes, LANES), col),
            pl.BlockSpec((steps, SUBS, LANES), three),
            pl.BlockSpec((modes, SUBS, LANES), three),
        ]
        + [pl.BlockSpec((2, PAYLOAD, LANES), three)] * len(told),
        out_specs=pl.BlockSpec((n_tok, LANES), col),
        out_shape=jax.ShapeDtypeStruct((n_tok, width), bf16),
        scratch_shapes=[
            pltpu.VMEM((n_tok + SUBS * PAD, LANES), f32),
            pltpu.VMEM((n_tok + SUBS * PAD, LANES), f32),
            pltpu.VMEM((2 * len(told) + 1, PAYLOAD, LANES), f32),
        ],
        compiler_params=pltpu.CompilerParams(vmem_limit_bytes=48 << 20),
        name="gated",
    )(at, x, sf, rate, res, p, start, *told)


def spread(x, axis, target):
    pairs = [(i, target(i)) for i in range(lax.axis_size(axis))]
    return lax.ppermute(x, axis, [(i, j) for i, j in pairs if j is not None])


def to_core(x):
    return spread(x, "ch", lambda i: i ^ 1)


def to_far_z(x):
    return spread(x, "ch", lambda i: i ^ 2)


def to_y(x, by):
    return spread(x, "ch", lambda i: (i + 4 * by) % 16)


def to_x(x, by):
    return spread(x, "ctx", lambda i: i // 4 * 4 + (i + by) % 4)


def to_near_z(x):
    return spread(x, "ctx", lambda i: (i + 4) % 8)


def project_kernel(plan, n_added, cols_ref, g_ref, gp_ref, w_ref, wp_ref, *refs):
    added, refs = refs[:n_added], refs[n_added:]
    out_refs, (acts, weights, act_sems, weight_sems) = refs[:-4], refs[-4:]
    depth = g_ref.shape[1]
    act_copies = [pltpu.make_async_copy(r, acts.at[j], act_sems.at[j]) for j, r in enumerate((g_ref, gp_ref))]
    copies = []
    for k, (col, _) in enumerate(plan):
        at = pl.ds(pl.multiple_of(cols_ref[col] * depth, depth), depth)
        pair = [
            pltpu.make_async_copy(source.at[:, at], weights.at[k, j], weight_sems.at[k, j])
            for j, source in enumerate((w_ref, wp_ref))
        ]
        for copy in act_copies + pair if k == 0 else pair:
            copy.start()
        copies.append(pair)
    for k, (_, pieces) in enumerate(plan):
        for copy in act_copies + copies[k] if k == 0 else copies[k]:
            copy.wait()
        for first, count, out, slot, extra in pieces:
            rows = pl.ds(first, count)
            acc = jnp.dot(acts[0, rows, :], weights[k, 0], preferred_element_type=f32)
            acc = acc + jnp.dot(acts[1, rows, :], weights[k, 1], preferred_element_type=f32)
            if extra is not None:
                acc = acc + added[extra[0]][extra[1]].astype(f32)
            out_refs[out][slot] = acc.astype(bf16)


def project(operands, plan, counts, added=(), limit=50):
    cols, g, gp, w, wp = operands
    n_tok, depth = g.shape
    slots = [0] * len(counts)
    laid = []
    for (dy, dz), pieces in plan:
        mine = []
        for first, out, *extra in pieces:
            mine.append((first, counts[out], out, slots[out], extra[0] if extra else None))
            slots[out] += 1
        laid.append((2 * dy + dz, mine))
    vmem = pl.BlockSpec(memory_space=pltpu.VMEM)
    anywhere = pl.BlockSpec(memory_space=pl.ANY)
    return pl.pallas_call(
        functools.partial(project_kernel, laid, len(added)),
        in_specs=[pl.BlockSpec(memory_space=pltpu.SMEM)] + [anywhere] * 4 + [vmem] * len(added),
        out_specs=[vmem] * len(counts),
        out_shape=[jax.ShapeDtypeStruct((n, count, depth), bf16) for n, count in zip(slots, counts)],
        scratch_shapes=[
            pltpu.VMEM((2, n_tok, depth), bf16),
            pltpu.VMEM((len(plan), 2, depth, depth), bf16),
            pltpu.SemaphoreType.DMA((2,)),
            pltpu.SemaphoreType.DMA((len(plan), 2)),
        ],
        compiler_params=pltpu.CompilerParams(vmem_limit_bytes=limit << 20),
        name="project",
    )(cols, g, gp, w, wp, *added)


def total(*parts):
    return sum(p.astype(f32) for p in parts).astype(bf16)


Z_TOK = 320


def per_device(features, short_filter, decay_rate, residues, out_weight):
    n_tok = features.shape[0]
    x = features.transpose(1, 0, 2)
    weight_pair = to_core(out_weight)
    me = lax.axis_index("ch")
    steps = jnp.arange(8, dtype=jnp.int32)
    cols = (me // 4 + steps // 2) % 4 * 4 + (me // 2 + steps) % 2 * 2 + me % 2
    product, told, start = states(x, short_filter, decay_rate)
    told = jnp.stack([told, to_near_z(told)])
    heard = [told] + [to_x(told, n) for n in (1, 2, 3)]
    at = lax.axis_index("ctx").astype(jnp.int32)[None]
    mine = gated(at, x, short_filter, decay_rate, residues, product, start, heard)
    operands = (cols, mine, to_core(mine), out_weight, weight_pair)
    n_y = n_tok - Z_TOK
    a, b, z = 0, n_y // 2, n_y

    up2, down2 = project(operands, [((2, dz), [(a, 0), (b, 1)]) for dz in (1, 0)], [b, b], limit=50)
    up2, down2 = to_y(up2, 1), to_y(down2, -1)
    (far,) = project(operands, [((dy, 1), [(z, 0)]) for dy in (0, 1, 2, 3)], [Z_TOK])
    far = to_far_z(far)
    up, down, up_more, down_more, keep_a, keep_b = project(
        operands,
        [((1, 1), [(b, 0), (a, 2)]), ((3, 1), [(a, 1), (b, 3)]), ((0, 1), [(a, 4), (b, 5)])],
        [b] * 6,
    )
    up, down = to_y(up[0], 1), to_y(down[0], -1)
    up_more, down_more = to_y(total(up_more[0], up2[0]), 1), to_y(total(down_more[0], down2[0]), -1)
    rise, fall, stay_a, stay_b = project(
        operands,
        [((1, 0), [(b, 0), (a, 0, (0, 1))]), ((3, 0), [(a, 1), (b, 1, (1, 1))]), ((0, 0), [(a, 2), (b, 3)])],
        [b] * 4,
        [up2, down2],
    )
    last = (cols, lax.optimization_barrier((mine, stay_a))[0]) + operands[2:]
    (near,) = project(last, [((dy, 0), [(z, 0)]) for dy in (2, 3, 1, 0)], [Z_TOK])
    half = Z_TOK // 2
    s2a, s2b = total(near[0, :half], far[2, :half]), total(near[0, half:], far[2, half:])
    rise, fall = to_y(rise, 1), to_y(fall, -1)
    s2a, s2b = to_y(s2a, 1), to_y(s2b, -1)
    up, down, up_more, down_more = lax.optimization_barrier((up, down, up_more, down_more))
    over = to_far_z(jnp.stack([total(keep_a[0], up_more, down), total(keep_b[0], up, down_more)]))
    rise, fall = lax.optimization_barrier((rise, fall))
    done_a = total(stay_a[0], rise[1], fall[0], over[0])
    done_b = total(stay_b[0], rise[0], fall[1], over[1])

    s1 = total(near[2], far[1], jnp.pad(s2a, ((0, half), (0, 0))))
    s3 = total(near[1], far[3], jnp.pad(s2b, ((half, 0), (0, 0))))
    s1, s3 = to_y(s1, 1), to_y(s3, -1)
    return jnp.concatenate([done_a, done_b, total(near[3], far[0], s1, s3)])


def solution(mesh):
    placed = (P("ctx", None, "ch"), P(None, None, "ch"), P(None, "ch"), P(None, "ch"), P("ch", None))
    return jax.shard_map(per_device, mesh=mesh, in_specs=placed, out_specs=P("ctx", "ch"), check_vma=False)
```

```python
import functools

import jax
import jax.numpy as jnp
from jax import lax
from jax.experimental import pallas as pl
from jax.experimental.pallas import tpu as pltpu
from jax.sharding import PartitionSpec as P

f32, bf16 = jnp.float32, jnp.bfloat16
LANES = 128
SUBS = 8
PAD = 8
STATE_ROWS, FIRST, LAST, PAYLOAD = 16, 16, 20, 32


def row_scan(values, factor, rows):
    step = 1
    while step < SUBS:
        back = jnp.where(rows >= step, pltpu.roll(values, step, axis=0), 0.0)
        values = values + factor * back
        factor = factor * factor
        step *= 2
    return values


def fill(rows_ref, x_ref, halo, steps):
    for s in range(SUBS):
        at = s * (steps + PAD) + PAD
        rows_ref[pl.ds(at, steps), :] = x_ref[pl.ds(s * steps, steps), :].astype(f32)
        before = x_ref[pl.ds(s * steps - 16, 16), :].astype(f32)[14:] if s else halo
        rows_ref[pl.ds(at - 2, 2), :] = before


def state_kernel(key_ref, val_ref, query_ref, sf_ref, rate_ref, p_ref, told_ref, start_ref, xs, told):
    n_modes = rate_ref.shape[0]
    steps = p_ref.shape[0]
    rows = lax.broadcasted_iota(jnp.int32, (SUBS, LANES), 0)
    none = jnp.zeros((2, LANES), f32)
    for j in range(2):
        fill(xs.at[j], (key_ref, val_ref)[j].at[0], none, steps)
    w = [[jnp.broadcast_to(sf_ref[k, j + 1][None], (SUBS, LANES)) for k in range(3)] for j in range(2)]
    decay = [jnp.exp(-jnp.broadcast_to(rate_ref[pl.ds(r, 1), :], (SUBS, LANES))) for r in range(n_modes)]

    def tap(j, at):
        return xs[j, pl.ds(PAD + at, SUBS, stride=steps + PAD), :]

    def body(t, carry, first=False):
        k1, k2, v1, v2, state = carry
        k0, v0 = tap(0, t), tap(1, t)
        key = w[0][0] * k0 + w[0][1] * k1 + w[0][2] * k2
        val = w[1][0] * v0 + w[1][1] * v1 + w[1][2] * v2
        p = (key * val).astype(bf16).astype(f32)
        if first:
            p = jnp.where(rows >= 1, p, 0.0)
        p_ref[t] = p
        state = tuple(a * s + p for a, s in zip(decay, state))
        return (k0, k1, v0, v1, state)

    zero = jnp.zeros((SUBS, LANES), f32)
    carry = (tap(0, -1), tap(0, -2), tap(1, -1), tap(1, -2), (zero,) * n_modes)
    carry = body(1, body(0, carry, True), True)
    state = lax.fori_loop(2, steps, body, carry, unroll=7)[4]
    for r in range(n_modes):
        rate = jnp.broadcast_to(rate_ref[pl.ds(r, 1), :], (SUBS, LANES))
        scanned = row_scan(state[r], jnp.exp(-rate * steps), rows)
        told[pl.ds(r, 1), :] = scanned[SUBS - 1 :]
        start_ref[r] = jnp.where(rows >= 1, pltpu.roll(scanned, 1, axis=0), 0.0)
    end = (SUBS - 1) * (steps + PAD) + PAD + steps
    told[pl.ds(LAST, PAYLOAD - LAST), :] = jnp.zeros((PAYLOAD - LAST, LANES), f32)
    told[pl.ds(LAST, 2), :] = query_ref[0].astype(f32)[14:]
    for j in range(2):
        told[pl.ds(FIRST + 2 * j, 2), :] = xs[j, pl.ds(PAD, 2), :]
        told[pl.ds(LAST + 2 + 2 * j, 2), :] = xs[j, pl.ds(end - 2, 2), :]
    told_ref[...] = told[...].astype(bf16)


def gate_kernel(at_ref, x_ref, sf_ref, rate_ref, res_ref, p_ref, start_ref, *refs):
    told_refs, (out_ref, xs, ys, told) = refs[:-4], refs[-4:]
    n_modes = rate_ref.shape[0]
    steps = p_ref.shape[0]
    n_tok = SUBS * steps
    me = at_ref[0]
    rows = lax.broadcasted_iota(jnp.int32, (SUBS, LANES), 0)

    told[0] = jnp.zeros((PAYLOAD, LANES), f32)
    for n, ref in enumerate(told_refs):
        for k in range(2):
            told[1 + neighbour(me, n, k)] = ref[k].astype(f32)

    def first_products(j):
        taps = []
        for i in range(2):
            row = lambda slot, at: told[slot, pl.ds(at, 1), :]
            x = [row(j, LAST + 2 + 2 * i), row(j, LAST + 3 + 2 * i), row(1 + j, FIRST + 2 * i), row(1 + j, FIRST + 1 + 2 * i)]
            w = [sf_ref[k, i + 1][None] for k in range(3)]
            taps.append([w[0] * x[t + 2] + w[1] * x[t + 1] + w[2] * x[t] for t in range(2)])
        return [(taps[0][t] * taps[1][t]).astype(bf16).astype(f32) for t in range(2)]

    rates = rate_ref[...]
    late = [jnp.exp(-rates * (n_tok - 1 - t)) for t in range(2)]
    enter_all = jnp.zeros_like(rates)
    for j in range(2 * len(told_refs) - 1):
        p0, p1 = first_products(j)
        ended = told[1 + j, :n_modes, :] + late[0] * p0 + late[1] * p1
        gap = (jnp.maximum(me - 1 - j, 0) * n_tok).astype(f32)
        enter_all = enter_all + jnp.where(j < me, jnp.exp(-rates * gap), 0.0) * ended
    told[0, pl.ds(0, n_modes), :] = enter_all
    p_first = [jnp.broadcast_to(p, (SUBS, LANES)) for p in first_products(me)]

    fill(xs, x_ref.at[0], told[me, pl.ds(LAST, 2), :], steps)
    w = [jnp.broadcast_to(sf_ref[k, 0][None], (SUBS, LANES)) for k in range(3)]
    decay, gain, state0 = [], [], []
    for r in range(n_modes):
        rate = jnp.broadcast_to(rate_ref[pl.ds(r, 1), :], (SUBS, LANES))
        enter = jnp.broadcast_to(told[0, pl.ds(r, 1), :], (SUBS, LANES))
        decay.append(jnp.exp(-rate))
        gain.append(jnp.broadcast_to(res_ref[pl.ds(r, 1), :], (SUBS, LANES)))
        passed = (rows * steps).astype(f32)
        mine = jnp.exp(-rate * (passed - 1.0)) * p_first[0] + jnp.exp(-rate * (passed - 2.0)) * p_first[1]
        state0.append(start_ref[r] + jnp.exp(-rate * passed) * enter + jnp.where(rows >= 1, mine, 0.0))

    def tap(at):
        return xs[pl.ds(PAD + at, SUBS, stride=steps + PAD), :]

    def body(t, carry, first=None):
        x1, x2, state = carry
        x0 = tap(t)
        gate = w[0] * x0 + w[1] * x1 + w[2] * x2
        p = p_ref[t]
        if first is not None:
            p = jnp.where(rows >= 1, p, first)
        state = tuple(a * s + p for a, s in zip(decay, state))
        parts = [c * s for c, s in zip(gain, state)]
        while len(parts) > 1:
            parts = [a + b for a, b in zip(parts[::2], parts[1::2])]
        ys[pl.ds(t, SUBS, stride=steps + PAD), :] = gate * parts[0]
        return (x0, x1, state)

    carry = (tap(-1), tap(-2), tuple(state0))
    carry = body(1, body(0, carry, p_first[0]), p_first[1])
    lax.fori_loop(2, steps, body, carry, unroll=6)
    for s in range(SUBS):
        out_ref[pl.ds(s * steps, steps), :] = ys[pl.ds(s * (steps + PAD), steps), :].astype(bf16)


def neighbour(me, n, k):
    return (me // 4 + k) % 2 * 4 + (me + 4 - n) % 4


def states(x, sf, rate):
    _, n_tok, width = x.shape
    modes = rate.shape[0]
    steps = n_tok // SUBS
    col = lambda g: (0, g)
    three = lambda g: (0, 0, g)
    return pl.pallas_call(
        state_kernel,
        grid=(width // LANES,),
        in_specs=[
            pl.BlockSpec((1, n_tok, LANES), lambda g: (1, 0, g)),
            pl.BlockSpec((1, n_tok, LANES), lambda g: (2, 0, g)),
            pl.BlockSpec((1, 16, LANES), lambda g: (0, n_tok // 16 - 1, g)),
            pl.BlockSpec((3, 3, LANES), three),
            pl.BlockSpec((modes, LANES), col),
        ],
        out_specs=[
            pl.BlockSpec((steps, SUBS, LANES), three),
            pl.BlockSpec((PAYLOAD, LANES), col),
            pl.BlockSpec((modes, SUBS, LANES), three),
        ],
        out_shape=[
            jax.ShapeDtypeStruct((steps, SUBS, width), f32),
            jax.ShapeDtypeStruct((PAYLOAD, width), bf16),
            jax.ShapeDtypeStruct((modes, SUBS, width), f32),
        ],
        scratch_shapes=[pltpu.VMEM((2, n_tok + SUBS * PAD, LANES), f32), pltpu.VMEM((PAYLOAD, LANES), f32)],
        compiler_params=pltpu.CompilerParams(vmem_limit_bytes=60 << 20),
        name="states",
    )(x, x, x, sf, rate)


def gated(at, x, sf, rate, res, p, start, told):
    _, n_tok, width = x.shape
    modes = rate.shape[0]
    steps = n_tok // SUBS
    col = lambda g: (0, g)
    three = lambda g: (0, 0, g)
    return pl.pallas_call(
        gate_kernel,
        grid=(width // LANES,),
        in_specs=[
            pl.BlockSpec(memory_space=pltpu.SMEM),
            pl.BlockSpec((1, n_tok, LANES), three),
            pl.BlockSpec((3, 3, LANES), three),
            pl.BlockSpec((modes, LANES), col),
            pl.BlockSpec((modes, LANES), col),
            pl.BlockSpec((steps, SUBS, LANES), three),
            pl.BlockSpec((modes, SUBS, LANES), three),
        ]
        + [pl.BlockSpec((2, PAYLOAD, LANES), three)] * len(told),
        out_specs=pl.BlockSpec((n_tok, LANES), col),
        out_shape=jax.ShapeDtypeStruct((n_tok, width), bf16),
        scratch_shapes=[
            pltpu.VMEM((n_tok + SUBS * PAD, LANES), f32),
            pltpu.VMEM((n_tok + SUBS * PAD, LANES), f32),
            pltpu.VMEM((2 * len(told) + 1, PAYLOAD, LANES), f32),
        ],
        compiler_params=pltpu.CompilerParams(vmem_limit_bytes=48 << 20),
        name="gated",
    )(at, x, sf, rate, res, p, start, *told)


def spread(x, axis, target):
    pairs = [(i, target(i)) for i in range(lax.axis_size(axis))]
    return lax.ppermute(x, axis, [(i, j) for i, j in pairs if j is not None])


def to_core(x):
    return spread(x, "ch", lambda i: i ^ 1)


def to_far_z(x):
    return spread(x, "ch", lambda i: i ^ 2)


def to_y(x, by):
    return spread(x, "ch", lambda i: (i + 4 * by) % 16)


def to_x(x, by):
    return spread(x, "ctx", lambda i: i // 4 * 4 + (i + by) % 4)


def to_near_z(x):
    return spread(x, "ctx", lambda i: (i + 4) % 8)


def project_kernel(plan, n_added, cols_ref, g_ref, gp_ref, w_ref, wp_ref, *refs):
    added, refs = refs[:n_added], refs[n_added:]
    out_refs, (acts, weights, act_sems, weight_sems) = refs[:-4], refs[-4:]
    depth = g_ref.shape[1]
    act_copies = [pltpu.make_async_copy(r, acts.at[j], act_sems.at[j]) for j, r in enumerate((g_ref, gp_ref))]
    copies = []
    for k, (col, _) in enumerate(plan):
        at = pl.ds(pl.multiple_of(cols_ref[col] * depth, depth), depth)
        pair = [
            pltpu.make_async_copy(source.at[:, at], weights.at[k, j], weight_sems.at[k, j])
            for j, source in enumerate((w_ref, wp_ref))
        ]
        for copy in act_copies + pair if k == 0 else pair:
            copy.start()
        copies.append(pair)
    for k, (_, pieces) in enumerate(plan):
        for copy in act_copies + copies[k] if k == 0 else copies[k]:
            copy.wait()
        for first, count, out, slot, extra in pieces:
            rows = pl.ds(first, count)
            acc = jnp.dot(acts[0, rows, :], weights[k, 0], preferred_element_type=f32)
            acc = acc + jnp.dot(acts[1, rows, :], weights[k, 1], preferred_element_type=f32)
            if extra is not None:
                acc = acc + added[extra[0]][extra[1]].astype(f32)
            out_refs[out][slot] = acc.astype(bf16)


def project(operands, plan, counts, added=(), limit=50):
    cols, g, gp, w, wp = operands
    n_tok, depth = g.shape
    slots = [0] * len(counts)
    laid = []
    for (dy, dz), pieces in plan:
        mine = []
        for first, out, *extra in pieces:
            mine.append((first, counts[out], out, slots[out], extra[0] if extra else None))
            slots[out] += 1
        laid.append((2 * dy + dz, mine))
    vmem = pl.BlockSpec(memory_space=pltpu.VMEM)
    anywhere = pl.BlockSpec(memory_space=pl.ANY)
    return pl.pallas_call(
        functools.partial(project_kernel, laid, len(added)),
        in_specs=[pl.BlockSpec(memory_space=pltpu.SMEM)] + [anywhere] * 4 + [vmem] * len(added),
        out_specs=[vmem] * len(counts),
        out_shape=[jax.ShapeDtypeStruct((n, count, depth), bf16) for n, count in zip(slots, counts)],
        scratch_shapes=[
            pltpu.VMEM((2, n_tok, depth), bf16),
            pltpu.VMEM((len(plan), 2, depth, depth), bf16),
            pltpu.SemaphoreType.DMA((2,)),
            pltpu.SemaphoreType.DMA((len(plan), 2)),
        ],
        compiler_params=pltpu.CompilerParams(vmem_limit_bytes=limit << 20),
        name="project",
    )(cols, g, gp, w, wp, *added)


def total(*parts):
    return sum(p.astype(f32) for p in parts).astype(bf16)


Z_TOK = 320


def per_device(features, short_filter, decay_rate, residues, out_weight):
    n_tok = features.shape[0]
    x = features.transpose(1, 0, 2)
    weight_pair = to_core(out_weight)
    me = lax.axis_index("ch")
    steps = jnp.arange(8, dtype=jnp.int32)
    cols = (me // 4 + steps // 2) % 4 * 4 + (me // 2 + steps) % 2 * 2 + me % 2
    product, told, start = states(x, short_filter, decay_rate)
    told = jnp.stack([told, to_near_z(told)])
    heard = [told] + [to_x(told, n) for n in (1, 2, 3)]
    at = lax.axis_index("ctx").astype(jnp.int32)[None]
    mine = gated(at, x, short_filter, decay_rate, residues, product, start, heard)
    operands = (cols, mine, to_core(mine), out_weight, weight_pair)
    n_y = n_tok - Z_TOK
    a, b, z = 0, n_y // 2, n_y

    up2, down2 = project(operands, [((2, dz), [(a, 0), (b, 1)]) for dz in (1, 0)], [b, b], limit=50)
    up2, down2 = to_y(up2, 1), to_y(down2, -1)
    (far,) = project(operands, [((dy, 1), [(z, 0)]) for dy in (0, 1, 2, 3)], [Z_TOK])
    far = to_far_z(far)
    up, down, up_more, down_more, keep_a, keep_b = project(
        operands,
        [((1, 1), [(b, 0), (a, 2)]), ((3, 1), [(a, 1), (b, 3)]), ((0, 1), [(a, 4), (b, 5)])],
        [b] * 6,
    )
    up, down = to_y(up[0], 1), to_y(down[0], -1)
    up_more, down_more = to_y(total(up_more[0], up2[0]), 1), to_y(total(down_more[0], down2[0]), -1)
    rise, fall, stay_a, stay_b = project(
        operands,
        [((1, 0), [(b, 0), (a, 0, (0, 1))]), ((3, 0), [(a, 1), (b, 1, (1, 1))]), ((0, 0), [(a, 2), (b, 3)])],
        [b] * 4,
        [up2, down2],
    )
    last = (cols, lax.optimization_barrier((mine, stay_a, up, down))[0]) + operands[2:]
    (near,) = project(last, [((dy, 0), [(z, 0)]) for dy in (2, 3, 1, 0)], [Z_TOK])
    half = Z_TOK // 2
    s2a, s2b = total(near[0, :half], far[2, :half]), total(near[0, half:], far[2, half:])
    rise, fall = to_y(rise, 1), to_y(fall, -1)
    s2a, s2b = to_y(s2a, 1), to_y(s2b, -1)
    up, down, up_more, down_more = lax.optimization_barrier((up, down, up_more, down_more))
    over = to_far_z(jnp.stack([total(keep_a[0], up_more, down), total(keep_b[0], up, down_more)]))
    rise, fall = lax.optimization_barrier((rise, fall))
    done_a = total(stay_a[0], rise[1], fall[0], over[0])
    done_b = total(stay_b[0], rise[0], fall[1], over[1])

    s1 = total(near[2], far[1], jnp.pad(s2a, ((0, half), (0, 0))))
    s3 = total(near[1], far[3], jnp.pad(s2b, ((half, 0), (0, 0))))
    s1, s3 = to_y(s1, 1), to_y(s3, -1)
    return jnp.concatenate([done_a, done_b, total(near[3], far[0], s1, s3)])


def solution(mesh):
    placed = (P("ctx", None, "ch"), P(None, None, "ch"), P(None, "ch"), P(None, "ch"), P("ch", None))
    return jax.shard_map(per_device, mesh=mesh, in_specs=placed, out_specs=P("ctx", "ch"), check_vma=False)
```

```python
import functools

import jax
import jax.numpy as jnp
from jax import lax
from jax.experimental import pallas as pl
from jax.experimental.pallas import tpu as pltpu
from jax.sharding import PartitionSpec as P

f32, bf16 = jnp.float32, jnp.bfloat16
LANES = 128
SUBS = 8
PAD = 8
STATE_ROWS, FIRST, LAST, PAYLOAD = 16, 16, 20, 32


def row_scan(values, factor, rows):
    step = 1
    while step < SUBS:
        back = jnp.where(rows >= step, pltpu.roll(values, step, axis=0), 0.0)
        values = values + factor * back
        factor = factor * factor
        step *= 2
    return values


def fill(rows_ref, x_ref, halo, steps):
    for s in range(SUBS):
        at = s * (steps + PAD) + PAD
        rows_ref[pl.ds(at, steps), :] = x_ref[pl.ds(s * steps, steps), :].astype(f32)
        before = x_ref[pl.ds(s * steps - 16, 16), :].astype(f32)[14:] if s else halo
        rows_ref[pl.ds(at - 2, 2), :] = before


def state_kernel(key_ref, val_ref, query_ref, sf_ref, rate_ref, p_ref, told_ref, xs, told):
    n_modes = rate_ref.shape[0]
    steps = p_ref.shape[0] - n_modes
    rows = lax.broadcasted_iota(jnp.int32, (SUBS, LANES), 0)
    none = jnp.zeros((2, LANES), f32)
    for j in range(2):
        fill(xs.at[j], (key_ref, val_ref)[j].at[0], none, steps)
    w = [[jnp.broadcast_to(sf_ref[k, j + 1][None], (SUBS, LANES)) for k in range(3)] for j in range(2)]
    decay = [jnp.exp(-jnp.broadcast_to(rate_ref[pl.ds(r, 1), :], (SUBS, LANES))) for r in range(n_modes)]

    def tap(j, at):
        return xs[j, pl.ds(PAD + at, SUBS, stride=steps + PAD), :]

    def body(t, carry, first=False):
        k1, k2, v1, v2, state = carry
        k0, v0 = tap(0, t), tap(1, t)
        key = w[0][0] * k0 + w[0][1] * k1 + w[0][2] * k2
        val = w[1][0] * v0 + w[1][1] * v1 + w[1][2] * v2
        p = (key * val).astype(bf16).astype(f32)
        if first:
            p = jnp.where(rows >= 1, p, 0.0)
        p_ref[t] = p
        state = tuple(a * s + p for a, s in zip(decay, state))
        return (k0, k1, v0, v1, state)

    zero = jnp.zeros((SUBS, LANES), f32)
    carry = (tap(0, -1), tap(0, -2), tap(1, -1), tap(1, -2), (zero,) * n_modes)
    carry = body(1, body(0, carry, True), True)
    state = lax.fori_loop(2, steps, body, carry, unroll=7)[4]
    for r in range(n_modes):
        rate = jnp.broadcast_to(rate_ref[pl.ds(r, 1), :], (SUBS, LANES))
        scanned = row_scan(state[r], jnp.exp(-rate * steps), rows)
        told[pl.ds(r, 1), :] = scanned[SUBS - 1 :]
        p_ref[steps + r] = jnp.where(rows >= 1, pltpu.roll(scanned, 1, axis=0), 0.0)
    end = (SUBS - 1) * (steps + PAD) + PAD + steps
    told[pl.ds(LAST, PAYLOAD - LAST), :] = jnp.zeros((PAYLOAD - LAST, LANES), f32)
    told[pl.ds(LAST, 2), :] = query_ref[0].astype(f32)[14:]
    for j in range(2):
        told[pl.ds(FIRST + 2 * j, 2), :] = xs[j, pl.ds(PAD, 2), :]
        told[pl.ds(LAST + 2 + 2 * j, 2), :] = xs[j, pl.ds(end - 2, 2), :]
    told_ref[...] = told[...].astype(bf16)


def gate_kernel(at_ref, x_ref, sf_ref, rate_ref, res_ref, p_ref, *refs):
    told_refs, (out_ref, xs, ys, told) = refs[:-4], refs[-4:]
    n_modes = rate_ref.shape[0]
    steps = p_ref.shape[0] - n_modes
    n_tok = SUBS * steps
    me = at_ref[0]
    rows = lax.broadcasted_iota(jnp.int32, (SUBS, LANES), 0)

    told[0] = jnp.zeros((PAYLOAD, LANES), f32)
    for n, ref in enumerate(told_refs):
        for k in range(2):
            told[1 + neighbour(me, n, k)] = ref[k].astype(f32)

    def first_products(j):
        taps = []
        for i in range(2):
            row = lambda slot, at: told[slot, pl.ds(at, 1), :]
            x = [row(j, LAST + 2 + 2 * i), row(j, LAST + 3 + 2 * i), row(1 + j, FIRST + 2 * i), row(1 + j, FIRST + 1 + 2 * i)]
            w = [sf_ref[k, i + 1][None] for k in range(3)]
            taps.append([w[0] * x[t + 2] + w[1] * x[t + 1] + w[2] * x[t] for t in range(2)])
        return [(taps[0][t] * taps[1][t]).astype(bf16).astype(f32) for t in range(2)]

    rates = rate_ref[...]
    late = [jnp.exp(-rates * (n_tok - 1 - t)) for t in range(2)]
    enter_all = jnp.zeros_like(rates)
    for j in range(2 * len(told_refs) - 1):
        p0, p1 = first_products(j)
        ended = told[1 + j, :n_modes, :] + late[0] * p0 + late[1] * p1
        gap = (jnp.maximum(me - 1 - j, 0) * n_tok).astype(f32)
        enter_all = enter_all + jnp.where(j < me, jnp.exp(-rates * gap), 0.0) * ended
    told[0, pl.ds(0, n_modes), :] = enter_all
    p_first = [jnp.broadcast_to(p, (SUBS, LANES)) for p in first_products(me)]

    fill(xs, x_ref.at[0], told[me, pl.ds(LAST, 2), :], steps)
    w = [jnp.broadcast_to(sf_ref[k, 0][None], (SUBS, LANES)) for k in range(3)]
    decay, gain, state0 = [], [], []
    for r in range(n_modes):
        rate = jnp.broadcast_to(rate_ref[pl.ds(r, 1), :], (SUBS, LANES))
        enter = jnp.broadcast_to(told[0, pl.ds(r, 1), :], (SUBS, LANES))
        decay.append(jnp.exp(-rate))
        gain.append(jnp.broadcast_to(res_ref[pl.ds(r, 1), :], (SUBS, LANES)))
        passed = (rows * steps).astype(f32)
        mine = jnp.exp(-rate * (passed - 1.0)) * p_first[0] + jnp.exp(-rate * (passed - 2.0)) * p_first[1]
        state0.append(p_ref[steps + r] + jnp.exp(-rate * passed) * enter + jnp.where(rows >= 1, mine, 0.0))

    def tap(at):
        return xs[pl.ds(PAD + at, SUBS, stride=steps + PAD), :]

    def body(t, carry, first=None):
        x1, x2, state = carry
        x0 = tap(t)
        gate = w[0] * x0 + w[1] * x1 + w[2] * x2
        p = p_ref[t]
        if first is not None:
            p = jnp.where(rows >= 1, p, first)
        state = tuple(a * s + p for a, s in zip(decay, state))
        parts = [c * s for c, s in zip(gain, state)]
        while len(parts) > 1:
            parts = [a + b for a, b in zip(parts[::2], parts[1::2])]
        ys[pl.ds(t, SUBS, stride=steps + PAD), :] = gate * parts[0]
        return (x0, x1, state)

    carry = (tap(-1), tap(-2), tuple(state0))
    carry = body(1, body(0, carry, p_first[0]), p_first[1])
    lax.fori_loop(2, steps, body, carry, unroll=6)
    for s in range(SUBS):
        out_ref[pl.ds(s * steps, steps), :] = ys[pl.ds(s * (steps + PAD), steps), :].astype(bf16)


def neighbour(me, n, k):
    return (me // 4 + k) % 2 * 4 + (me + 4 - n) % 4


def states(x, sf, rate):
    _, n_tok, width = x.shape
    modes = rate.shape[0]
    steps = n_tok // SUBS
    col = lambda g: (0, g)
    three = lambda g: (0, 0, g)
    return pl.pallas_call(
        state_kernel,
        grid=(width // LANES,),
        in_specs=[
            pl.BlockSpec((1, n_tok, LANES), lambda g: (1, 0, g)),
            pl.BlockSpec((1, n_tok, LANES), lambda g: (2, 0, g)),
            pl.BlockSpec((1, 16, LANES), lambda g: (0, n_tok // 16 - 1, g)),
            pl.BlockSpec((3, 3, LANES), three),
            pl.BlockSpec((modes, LANES), col),
        ],
        out_specs=[
            pl.BlockSpec((steps + modes, SUBS, LANES), three),
            pl.BlockSpec((PAYLOAD, LANES), col),
        ],
        out_shape=[
            jax.ShapeDtypeStruct((steps + modes, SUBS, width), f32),
            jax.ShapeDtypeStruct((PAYLOAD, width), bf16),
        ],
        scratch_shapes=[pltpu.VMEM((2, n_tok + SUBS * PAD, LANES), f32), pltpu.VMEM((PAYLOAD, LANES), f32)],
        compiler_params=pltpu.CompilerParams(vmem_limit_bytes=60 << 20),
        name="states",
    )(x, x, x, sf, rate)


def gated(at, x, sf, rate, res, p, told):
    _, n_tok, width = x.shape
    modes = rate.shape[0]
    steps = n_tok // SUBS
    col = lambda g: (0, g)
    three = lambda g: (0, 0, g)
    return pl.pallas_call(
        gate_kernel,
        grid=(width // LANES,),
        in_specs=[
            pl.BlockSpec(memory_space=pltpu.SMEM),
            pl.BlockSpec((1, n_tok, LANES), three),
            pl.BlockSpec((3, 3, LANES), three),
            pl.BlockSpec((modes, LANES), col),
            pl.BlockSpec((modes, LANES), col),
            pl.BlockSpec((steps + modes, SUBS, LANES), three),
        ]
        + [pl.BlockSpec((2, PAYLOAD, LANES), three)] * len(told),
        out_specs=pl.BlockSpec((n_tok, LANES), col),
        out_shape=jax.ShapeDtypeStruct((n_tok, width), bf16),
        scratch_shapes=[
            pltpu.VMEM((n_tok + SUBS * PAD, LANES), f32),
            pltpu.VMEM((n_tok + SUBS * PAD, LANES), f32),
            pltpu.VMEM((2 * len(told) + 1, PAYLOAD, LANES), f32),
        ],
        compiler_params=pltpu.CompilerParams(vmem_limit_bytes=48 << 20),
        name="gated",
    )(at, x, sf, rate, res, p, *told)


def spread(x, axis, target):
    pairs = [(i, target(i)) for i in range(lax.axis_size(axis))]
    return lax.ppermute(x, axis, [(i, j) for i, j in pairs if j is not None])


def to_core(x):
    return spread(x, "ch", lambda i: i ^ 1)


def to_far_z(x):
    return spread(x, "ch", lambda i: i ^ 2)


def to_y(x, by):
    return spread(x, "ch", lambda i: (i + 4 * by) % 16)


def to_x(x, by):
    return spread(x, "ctx", lambda i: i // 4 * 4 + (i + by) % 4)


def to_near_z(x):
    return spread(x, "ctx", lambda i: (i + 4) % 8)


def project_kernel(plan, n_added, cols_ref, g_ref, gp_ref, w_ref, wp_ref, *refs):
    added, refs = refs[:n_added], refs[n_added:]
    out_refs, (weights, sems) = refs[:-2], refs[-2:]
    depth = g_ref.shape[1]
    copies = []
    for k, (col, _) in enumerate(plan):
        at = pl.ds(pl.multiple_of(cols_ref[col] * depth, depth), depth)
        pair = [
            pltpu.make_async_copy(source.at[:, at], weights.at[k, j], sems.at[k, j])
            for j, source in enumerate((w_ref, wp_ref))
        ]
        for copy in pair:
            copy.start()
        copies.append(pair)
    for k, (_, pieces) in enumerate(plan):
        for copy in copies[k]:
            copy.wait()
        for first, count, out, slot, extra in pieces:
            rows = pl.ds(first, count)
            acc = jnp.dot(g_ref[rows, :], weights[k, 0], preferred_element_type=f32)
            acc = acc + jnp.dot(gp_ref[rows, :], weights[k, 1], preferred_element_type=f32)
            if extra is not None:
                acc = acc + added[extra[0]][extra[1]].astype(f32)
            out_refs[out][slot] = acc.astype(bf16)


def project(operands, plan, counts, added=(), limit=50):
    cols, g, gp, w, wp = operands
    depth = g.shape[1]
    slots = [0] * len(counts)
    laid = []
    for (dy, dz), pieces in plan:
        mine = []
        for first, out, *extra in pieces:
            mine.append((first, counts[out], out, slots[out], extra[0] if extra else None))
            slots[out] += 1
        laid.append((2 * dy + dz, mine))
    vmem = pl.BlockSpec(memory_space=pltpu.VMEM)
    anywhere = pl.BlockSpec(memory_space=pl.ANY)
    return pl.pallas_call(
        functools.partial(project_kernel, laid, len(added)),
        in_specs=[pl.BlockSpec(memory_space=pltpu.SMEM)] + [vmem] * 2 + [anywhere] * 2 + [vmem] * len(added),
        out_specs=[vmem] * len(counts),
        out_shape=[jax.ShapeDtypeStruct((n, count, depth), bf16) for n, count in zip(slots, counts)],
        scratch_shapes=[
            pltpu.VMEM((len(plan), 2, depth, depth), bf16),
            pltpu.SemaphoreType.DMA((len(plan), 2)),
        ],
        compiler_params=pltpu.CompilerParams(vmem_limit_bytes=limit << 20),
        name="project",
    )(cols, g, gp, w, wp, *added)


def total(*parts):
    return sum(p.astype(f32) for p in parts).astype(bf16)


Z_TOK = 384


def per_device(features, short_filter, decay_rate, residues, out_weight):
    n_tok = features.shape[0]
    x = features.transpose(1, 0, 2)
    weight_pair = to_core(out_weight)
    me = lax.axis_index("ch")
    steps = jnp.arange(8, dtype=jnp.int32)
    cols = (me // 4 + steps // 2) % 4 * 4 + (me // 2 + steps) % 2 * 2 + me % 2
    product, told = states(x, short_filter, decay_rate)
    told = jnp.stack([told, to_near_z(told)])
    heard = [told] + [to_x(told, n) for n in (1, 2, 3)]
    at = lax.axis_index("ctx").astype(jnp.int32)[None]
    mine = gated(at, x, short_filter, decay_rate, residues, product, heard)
    operands = (cols, mine, to_core(mine), out_weight, weight_pair)
    n_y = n_tok - Z_TOK
    a, b, z = 0, n_y // 2, n_y

    up2, down2 = project(operands, [((2, dz), [(a, 0), (b, 1)]) for dz in (1, 0)], [b, b], limit=50)
    up2, down2 = to_y(up2, 1), to_y(down2, -1)
    (far,) = project(operands, [((dy, 1), [(z, 0)]) for dy in (0, 1, 2, 3)], [Z_TOK])
    far = to_far_z(far)
    up, down, up_more, down_more, keep_a, keep_b = project(
        operands,
        [((1, 1), [(b, 0), (a, 2)]), ((3, 1), [(a, 1), (b, 3)]), ((0, 1), [(a, 4), (b, 5)])],
        [b] * 6,
    )
    up, down = to_y(up[0], 1), to_y(down[0], -1)
    up_more, down_more = to_y(total(up_more[0], up2[0]), 1), to_y(total(down_more[0], down2[0]), -1)
    rise, fall, stay_a, stay_b = project(
        operands,
        [((1, 0), [(b, 0), (a, 0, (0, 1))]), ((3, 0), [(a, 1), (b, 1, (1, 1))]), ((0, 0), [(a, 2), (b, 3)])],
        [b] * 4,
        [up2, down2],
    )
    last = (cols, lax.optimization_barrier((mine, stay_a, up, down))[0]) + operands[2:]
    (near,) = project(last, [((dy, 0), [(z, 0)]) for dy in (2, 3, 1, 0)], [Z_TOK])
    half = Z_TOK // 2
    s2a, s2b = total(near[0, :half], far[2, :half]), total(near[0, half:], far[2, half:])
    rise, fall = to_y(rise, 1), to_y(fall, -1)
    s2a, s2b = to_y(s2a, 1), to_y(s2b, -1)
    up, down, up_more, down_more = lax.optimization_barrier((up, down, up_more, down_more))
    over = to_far_z(jnp.stack([total(keep_a[0], up_more, down), total(keep_b[0], up, down_more)]))
    rise, fall = lax.optimization_barrier((rise, fall))
    done_a = total(stay_a[0], rise[1], fall[0], over[0])
    done_b = total(stay_b[0], rise[0], fall[1], over[1])

    s1 = total(near[2], far[1], jnp.pad(s2a, ((0, half), (0, 0))))
    s3 = total(near[1], far[3], jnp.pad(s2b, ((half, 0), (0, 0))))
    s1, s3 = to_y(s1, 1), to_y(s3, -1)
    return jnp.concatenate([done_a, done_b, total(near[3], far[0], s1, s3)])


def solution(mesh):
    placed = (P("ctx", None, "ch"), P(None, None, "ch"), P(None, "ch"), P(None, "ch"), P("ch", None))
    return jax.shard_map(per_device, mesh=mesh, in_specs=placed, out_specs=P("ctx", "ch"), check_vma=False)
```

```python
import functools

import jax
import jax.numpy as jnp
from jax import lax
from jax.experimental import pallas as pl
from jax.experimental.pallas import tpu as pltpu
from jax.sharding import PartitionSpec as P

f32, bf16 = jnp.float32, jnp.bfloat16
LANES = 128
SUBS = 8
PAD = 8
STATE_ROWS, FIRST, LAST, PAYLOAD = 16, 16, 20, 32


def row_scan(values, factor, rows):
    step = 1
    while step < SUBS:
        back = jnp.where(rows >= step, pltpu.roll(values, step, axis=0), 0.0)
        values = values + factor * back
        factor = factor * factor
        step *= 2
    return values


def fill(rows_ref, x_ref, halo, steps):
    for s in range(SUBS):
        at = s * (steps + PAD) + PAD
        rows_ref[pl.ds(at, steps), :] = x_ref[pl.ds(s * steps, steps), :].astype(f32)
        before = x_ref[pl.ds(s * steps - 16, 16), :].astype(f32)[14:] if s else halo
        rows_ref[pl.ds(at - 2, 2), :] = before


def state_kernel(key_ref, val_ref, query_ref, sf_ref, rate_ref, p_ref, told_ref, xs, told):
    n_modes = rate_ref.shape[0]
    steps = p_ref.shape[0] - n_modes
    rows = lax.broadcasted_iota(jnp.int32, (SUBS, LANES), 0)
    none = jnp.zeros((2, LANES), f32)
    for j in range(2):
        fill(xs.at[j], (key_ref, val_ref)[j].at[0], none, steps)
    w = [[jnp.broadcast_to(sf_ref[k, j + 1][None], (SUBS, LANES)) for k in range(3)] for j in range(2)]
    decay = [jnp.exp(-jnp.broadcast_to(rate_ref[pl.ds(r, 1), :], (SUBS, LANES))) for r in range(n_modes)]

    def tap(j, at):
        return xs[j, pl.ds(PAD + at, SUBS, stride=steps + PAD), :]

    def body(t, carry, first=False):
        k1, k2, v1, v2, state = carry
        k0, v0 = tap(0, t), tap(1, t)
        key = w[0][0] * k0 + w[0][1] * k1 + w[0][2] * k2
        val = w[1][0] * v0 + w[1][1] * v1 + w[1][2] * v2
        p = (key * val).astype(bf16).astype(f32)
        if first:
            p = jnp.where(rows >= 1, p, 0.0)
        p_ref[t] = p
        state = tuple(a * s + p for a, s in zip(decay, state))
        return (k0, k1, v0, v1, state)

    zero = jnp.zeros((SUBS, LANES), f32)
    carry = (tap(0, -1), tap(0, -2), tap(1, -1), tap(1, -2), (zero,) * n_modes)
    carry = body(1, body(0, carry, True), True)
    state = lax.fori_loop(2, steps, body, carry, unroll=7)[4]
    for r in range(n_modes):
        rate = jnp.broadcast_to(rate_ref[pl.ds(r, 1), :], (SUBS, LANES))
        scanned = row_scan(state[r], jnp.exp(-rate * steps), rows)
        told[pl.ds(r, 1), :] = scanned[SUBS - 1 :]
        p_ref[steps + r] = jnp.where(rows >= 1, pltpu.roll(scanned, 1, axis=0), 0.0)
    end = (SUBS - 1) * (steps + PAD) + PAD + steps
    told[pl.ds(LAST, PAYLOAD - LAST), :] = jnp.zeros((PAYLOAD - LAST, LANES), f32)
    told[pl.ds(LAST, 2), :] = query_ref[0].astype(f32)[14:]
    for j in range(2):
        told[pl.ds(FIRST + 2 * j, 2), :] = xs[j, pl.ds(PAD, 2), :]
        told[pl.ds(LAST + 2 + 2 * j, 2), :] = xs[j, pl.ds(end - 2, 2), :]
    told_ref[...] = told[...].astype(bf16)


def gate_kernel(at_ref, x_ref, sf_ref, rate_ref, res_ref, p_ref, *refs):
    told_refs, (out_ref, xs, ys, told) = refs[:-4], refs[-4:]
    n_modes = rate_ref.shape[0]
    steps = p_ref.shape[0] - n_modes
    n_tok = SUBS * steps
    me = at_ref[0]
    rows = lax.broadcasted_iota(jnp.int32, (SUBS, LANES), 0)

    told[0] = jnp.zeros((PAYLOAD, LANES), f32)
    for n, ref in enumerate(told_refs):
        for k in range(2):
            told[1 + neighbour(me, n, k)] = ref[k].astype(f32)

    def first_products(j):
        taps = []
        for i in range(2):
            row = lambda slot, at: told[slot, pl.ds(at, 1), :]
            x = [row(j, LAST + 2 + 2 * i), row(j, LAST + 3 + 2 * i), row(1 + j, FIRST + 2 * i), row(1 + j, FIRST + 1 + 2 * i)]
            w = [sf_ref[k, i + 1][None] for k in range(3)]
            taps.append([w[0] * x[t + 2] + w[1] * x[t + 1] + w[2] * x[t] for t in range(2)])
        return [(taps[0][t] * taps[1][t]).astype(bf16).astype(f32) for t in range(2)]

    rates = rate_ref[...]
    late = [jnp.exp(-rates * (n_tok - 1 - t)) for t in range(2)]
    enter_all = jnp.zeros_like(rates)
    for j in range(2 * len(told_refs) - 1):
        p0, p1 = first_products(j)
        ended = told[1 + j, :n_modes, :] + late[0] * p0 + late[1] * p1
        gap = (jnp.maximum(me - 1 - j, 0) * n_tok).astype(f32)
        enter_all = enter_all + jnp.where(j < me, jnp.exp(-rates * gap), 0.0) * ended
    told[0, pl.ds(0, n_modes), :] = enter_all
    p_first = [jnp.broadcast_to(p, (SUBS, LANES)) for p in first_products(me)]

    fill(xs, x_ref.at[0], told[me, pl.ds(LAST, 2), :], steps)
    w = [jnp.broadcast_to(sf_ref[k, 0][None], (SUBS, LANES)) for k in range(3)]
    decay, gain, state0 = [], [], []
    for r in range(n_modes):
        rate = jnp.broadcast_to(rate_ref[pl.ds(r, 1), :], (SUBS, LANES))
        enter = jnp.broadcast_to(told[0, pl.ds(r, 1), :], (SUBS, LANES))
        decay.append(jnp.exp(-rate))
        gain.append(jnp.broadcast_to(res_ref[pl.ds(r, 1), :], (SUBS, LANES)))
        passed = (rows * steps).astype(f32)
        mine = jnp.exp(-rate * (passed - 1.0)) * p_first[0] + jnp.exp(-rate * (passed - 2.0)) * p_first[1]
        state0.append(p_ref[steps + r] + jnp.exp(-rate * passed) * enter + jnp.where(rows >= 1, mine, 0.0))

    def tap(at):
        return xs[pl.ds(PAD + at, SUBS, stride=steps + PAD), :]

    def body(t, carry, first=None):
        x1, x2, state = carry
        x0 = tap(t)
        gate = w[0] * x0 + w[1] * x1 + w[2] * x2
        p = p_ref[t]
        if first is not None:
            p = jnp.where(rows >= 1, p, first)
        state = tuple(a * s + p for a, s in zip(decay, state))
        parts = [c * s for c, s in zip(gain, state)]
        while len(parts) > 1:
            parts = [a + b for a, b in zip(parts[::2], parts[1::2])]
        ys[pl.ds(t, SUBS, stride=steps + PAD), :] = gate * parts[0]
        return (x0, x1, state)

    carry = (tap(-1), tap(-2), tuple(state0))
    carry = body(1, body(0, carry, p_first[0]), p_first[1])
    lax.fori_loop(2, steps, body, carry, unroll=6)
    for s in range(SUBS):
        out_ref[pl.ds(s * steps, steps), :] = ys[pl.ds(s * (steps + PAD), steps), :].astype(bf16)


def neighbour(me, n, k):
    return (me // 4 + k) % 2 * 4 + (me + 4 - n) % 4


def states(x, sf, rate):
    _, n_tok, width = x.shape
    modes = rate.shape[0]
    steps = n_tok // SUBS
    col = lambda g: (0, g)
    three = lambda g: (0, 0, g)
    return pl.pallas_call(
        state_kernel,
        grid=(width // LANES,),
        in_specs=[
            pl.BlockSpec((1, n_tok, LANES), lambda g: (1, 0, g)),
            pl.BlockSpec((1, n_tok, LANES), lambda g: (2, 0, g)),
            pl.BlockSpec((1, 16, LANES), lambda g: (0, n_tok // 16 - 1, g)),
            pl.BlockSpec((3, 3, LANES), three),
            pl.BlockSpec((modes, LANES), col),
        ],
        out_specs=[
            pl.BlockSpec((steps + modes, SUBS, LANES), three),
            pl.BlockSpec((PAYLOAD, LANES), col),
        ],
        out_shape=[
            jax.ShapeDtypeStruct((steps + modes, SUBS, width), f32),
            jax.ShapeDtypeStruct((PAYLOAD, width), bf16),
        ],
        scratch_shapes=[pltpu.VMEM((2, n_tok + SUBS * PAD, LANES), f32), pltpu.VMEM((PAYLOAD, LANES), f32)],
        compiler_params=pltpu.CompilerParams(vmem_limit_bytes=60 << 20),
        name="states",
    )(x, x, x, sf, rate)


def gated(at, x, sf, rate, res, p, told):
    _, n_tok, width = x.shape
    modes = rate.shape[0]
    steps = n_tok // SUBS
    col = lambda g: (0, g)
    three = lambda g: (0, 0, g)
    return pl.pallas_call(
        gate_kernel,
        grid=(width // LANES,),
        in_specs=[
            pl.BlockSpec(memory_space=pltpu.SMEM),
            pl.BlockSpec((1, n_tok, LANES), three),
            pl.BlockSpec((3, 3, LANES), three),
            pl.BlockSpec((modes, LANES), col),
            pl.BlockSpec((modes, LANES), col),
            pl.BlockSpec((steps + modes, SUBS, LANES), three),
        ]
        + [pl.BlockSpec((2, PAYLOAD, LANES), three)] * len(told),
        out_specs=pl.BlockSpec((n_tok, LANES), col),
        out_shape=jax.ShapeDtypeStruct((n_tok, width), bf16),
        scratch_shapes=[
            pltpu.VMEM((n_tok + SUBS * PAD, LANES), f32),
            pltpu.VMEM((n_tok + SUBS * PAD, LANES), f32),
            pltpu.VMEM((2 * len(told) + 1, PAYLOAD, LANES), f32),
        ],
        compiler_params=pltpu.CompilerParams(vmem_limit_bytes=48 << 20),
        name="gated",
    )(at, x, sf, rate, res, p, *told)


def spread(x, axis, target):
    pairs = [(i, target(i)) for i in range(lax.axis_size(axis))]
    return lax.ppermute(x, axis, [(i, j) for i, j in pairs if j is not None])


def to_core(x):
    return spread(x, "ch", lambda i: i ^ 1)


def to_far_z(x):
    return spread(x, "ch", lambda i: i ^ 2)


def to_y(x, by):
    return spread(x, "ch", lambda i: (i + 4 * by) % 16)


def to_x(x, by):
    return spread(x, "ctx", lambda i: i // 4 * 4 + (i + by) % 4)


def to_near_z(x):
    return spread(x, "ctx", lambda i: (i + 4) % 8)


def project_kernel(plan, n_added, cols_ref, g_ref, gp_ref, w_ref, wp_ref, *refs):
    added, refs = refs[:n_added], refs[n_added:]
    out_refs, (weights, sems) = refs[:-2], refs[-2:]
    depth = g_ref.shape[1]
    copies = []
    for k, (col, _) in enumerate(plan):
        at = pl.ds(pl.multiple_of(cols_ref[col] * depth, depth), depth)
        pair = [
            pltpu.make_async_copy(source.at[:, at], weights.at[k, j], sems.at[k, j])
            for j, source in enumerate((w_ref, wp_ref))
        ]
        for copy in pair:
            copy.start()
        copies.append(pair)
    for k, (_, pieces) in enumerate(plan):
        for copy in copies[k]:
            copy.wait()
        for first, count, out, slot, extra in pieces:
            rows = pl.ds(first, count)
            acc = jnp.dot(g_ref[rows, :], weights[k, 0], preferred_element_type=f32)
            acc = acc + jnp.dot(gp_ref[rows, :], weights[k, 1], preferred_element_type=f32)
            if extra is not None:
                acc = acc + added[extra[0]][extra[1]].astype(f32)
            out_refs[out][slot] = acc.astype(bf16)


def project(operands, plan, counts, added=(), limit=48):
    cols, g, gp, w, wp = operands
    depth = g.shape[1]
    slots = [0] * len(counts)
    laid = []
    for (dy, dz), pieces in plan:
        mine = []
        for first, out, *extra in pieces:
            mine.append((first, counts[out], out, slots[out], extra[0] if extra else None))
            slots[out] += 1
        laid.append((2 * dy + dz, mine))
    vmem = pl.BlockSpec(memory_space=pltpu.VMEM)
    anywhere = pl.BlockSpec(memory_space=pl.ANY)
    return pl.pallas_call(
        functools.partial(project_kernel, laid, len(added)),
        in_specs=[pl.BlockSpec(memory_space=pltpu.SMEM)] + [vmem] * 2 + [anywhere] * 2 + [vmem] * len(added),
        out_specs=[vmem] * len(counts),
        out_shape=[jax.ShapeDtypeStruct((n, count, depth), bf16) for n, count in zip(slots, counts)],
        scratch_shapes=[
            pltpu.VMEM((len(plan), 2, depth, depth), bf16),
            pltpu.SemaphoreType.DMA((len(plan), 2)),
        ],
        compiler_params=pltpu.CompilerParams(vmem_limit_bytes=limit << 20),
        name="project",
    )(cols, g, gp, w, wp, *added)


def total(*parts):
    return sum(p.astype(f32) for p in parts).astype(bf16)


Z_TOK = 384


def per_device(features, short_filter, decay_rate, residues, out_weight):
    n_tok = features.shape[0]
    x = features.transpose(1, 0, 2)
    weight_pair = to_core(out_weight)
    me = lax.axis_index("ch")
    steps = jnp.arange(8, dtype=jnp.int32)
    cols = (me // 4 + steps // 2) % 4 * 4 + (me // 2 + steps) % 2 * 2 + me % 2
    product, told = states(x, short_filter, decay_rate)
    told = jnp.stack([told, to_near_z(told)])
    heard = [told] + [to_x(told, n) for n in (1, 2, 3)]
    at = lax.axis_index("ctx").astype(jnp.int32)[None]
    mine = gated(at, x, short_filter, decay_rate, residues, product, heard)
    operands = (cols, mine, to_core(mine), out_weight, weight_pair)
    n_y = n_tok - Z_TOK
    a, b, z = 0, n_y // 2, n_y

    up2, down2 = project(operands, [((2, dz), [(a, 0), (b, 1)]) for dz in (1, 0)], [b, b], limit=48)
    up2, down2 = to_y(up2, 1), to_y(down2, -1)
    (far,) = project(operands, [((dy, 1), [(z, 0)]) for dy in (0, 1, 2, 3)], [Z_TOK])
    far = to_far_z(far)
    up, down, up_more, down_more, keep_a, keep_b = project(
        operands,
        [((1, 1), [(b, 0), (a, 2)]), ((3, 1), [(a, 1), (b, 3)]), ((0, 1), [(a, 4), (b, 5)])],
        [b] * 6,
    )
    up, down = to_y(up[0], 1), to_y(down[0], -1)
    up_more, down_more = to_y(total(up_more[0], up2[0]), 1), to_y(total(down_more[0], down2[0]), -1)
    rise, fall, stay_a, stay_b = project(
        operands,
        [((1, 0), [(b, 0), (a, 0, (0, 1))]), ((3, 0), [(a, 1), (b, 1, (1, 1))]), ((0, 0), [(a, 2), (b, 3)])],
        [b] * 4,
        [up2, down2],
    )
    last = (cols, lax.optimization_barrier((mine, stay_a, up, down))[0]) + operands[2:]
    (near,) = project(last, [((dy, 0), [(z, 0)]) for dy in (2, 3, 1, 0)], [Z_TOK])
    half = Z_TOK // 2
    s2a, s2b = total(near[0, :half], far[2, :half]), total(near[0, half:], far[2, half:])
    rise, fall = to_y(rise, 1), to_y(fall, -1)
    s2a, s2b = to_y(s2a, 1), to_y(s2b, -1)
    up, down, up_more, down_more = lax.optimization_barrier((up, down, up_more, down_more))
    over = to_far_z(jnp.stack([total(keep_a[0], up_more, down), total(keep_b[0], up, down_more)]))
    rise, fall = lax.optimization_barrier((rise, fall))
    done_a = total(stay_a[0], rise[1], fall[0], over[0])
    done_b = total(stay_b[0], rise[0], fall[1], over[1])

    s1 = total(near[2], far[1], jnp.pad(s2a, ((0, half), (0, 0))))
    s3 = total(near[1], far[3], jnp.pad(s2b, ((half, 0), (0, 0))))
    s1, s3 = to_y(s1, 1), to_y(s3, -1)
    return jnp.concatenate([done_a, done_b, total(near[3], far[0], s1, s3)])


def solution(mesh):
    placed = (P("ctx", None, "ch"), P(None, None, "ch"), P(None, "ch"), P(None, "ch"), P("ch", None))
    return jax.shard_map(per_device, mesh=mesh, in_specs=placed, out_specs=P("ctx", "ch"), check_vma=False)
```

```python
import functools

import jax
import jax.numpy as jnp
from jax import lax
from jax.experimental import pallas as pl
from jax.experimental.pallas import tpu as pltpu
from jax.sharding import PartitionSpec as P

f32, bf16 = jnp.float32, jnp.bfloat16
LANES = 128
SUBS = 8
PAD = 8
STATE_ROWS, FIRST, LAST, PAYLOAD = 16, 16, 20, 32


def row_scan(values, factor, rows):
    step = 1
    while step < SUBS:
        back = jnp.where(rows >= step, pltpu.roll(values, step, axis=0), 0.0)
        values = values + factor * back
        factor = factor * factor
        step *= 2
    return values


def fill(rows_ref, x_ref, halo, steps):
    for s in range(SUBS):
        at = s * (steps + PAD) + PAD
        rows_ref[pl.ds(at, steps), :] = x_ref[pl.ds(s * steps, steps), :].astype(f32)
        before = x_ref[pl.ds(s * steps - 16, 16), :].astype(f32)[14:] if s else halo
        rows_ref[pl.ds(at - 2, 2), :] = before


def state_kernel(key_ref, val_ref, query_ref, sf_ref, rate_ref, p_ref, told_ref, xs, told):
    n_modes = rate_ref.shape[0]
    steps = p_ref.shape[0] - n_modes
    rows = lax.broadcasted_iota(jnp.int32, (SUBS, LANES), 0)
    none = jnp.zeros((2, LANES), f32)
    for j in range(2):
        fill(xs.at[j], (key_ref, val_ref)[j].at[0], none, steps)
    w = [[jnp.broadcast_to(sf_ref[k, j + 1][None], (SUBS, LANES)) for k in range(3)] for j in range(2)]
    decay = [jnp.exp(-jnp.broadcast_to(rate_ref[pl.ds(r, 1), :], (SUBS, LANES))) for r in range(n_modes)]

    def tap(j, at):
        return xs[j, pl.ds(PAD + at, SUBS, stride=steps + PAD), :]

    def body(t, carry, first=False):
        k1, k2, v1, v2, state = carry
        k0, v0 = tap(0, t), tap(1, t)
        key = w[0][0] * k0 + w[0][1] * k1 + w[0][2] * k2
        val = w[1][0] * v0 + w[1][1] * v1 + w[1][2] * v2
        p = (key * val).astype(bf16).astype(f32)
        if first:
            p = jnp.where(rows >= 1, p, 0.0)
        p_ref[t] = p
        state = tuple(a * s + p for a, s in zip(decay, state))
        return (k0, k1, v0, v1, state)

    zero = jnp.zeros((SUBS, LANES), f32)
    carry = (tap(0, -1), tap(0, -2), tap(1, -1), tap(1, -2), (zero,) * n_modes)
    carry = body(1, body(0, carry, True), True)
    state = lax.fori_loop(2, steps, body, carry, unroll=7)[4]
    for r in range(n_modes):
        rate = jnp.broadcast_to(rate_ref[pl.ds(r, 1), :], (SUBS, LANES))
        scanned = row_scan(state[r], jnp.exp(-rate * steps), rows)
        told[pl.ds(r, 1), :] = scanned[SUBS - 1 :]
        p_ref[steps + r] = jnp.where(rows >= 1, pltpu.roll(scanned, 1, axis=0), 0.0)
    end = (SUBS - 1) * (steps + PAD) + PAD + steps
    told[pl.ds(LAST, PAYLOAD - LAST), :] = jnp.zeros((PAYLOAD - LAST, LANES), f32)
    told[pl.ds(LAST, 2), :] = query_ref[0].astype(f32)[14:]
    for j in range(2):
        told[pl.ds(FIRST + 2 * j, 2), :] = xs[j, pl.ds(PAD, 2), :]
        told[pl.ds(LAST + 2 + 2 * j, 2), :] = xs[j, pl.ds(end - 2, 2), :]
    told_ref[...] = told[...].astype(bf16)


def gate_kernel(at_ref, x_ref, sf_ref, rate_ref, res_ref, p_ref, *refs):
    told_refs, (out_ref, xs, ys, told) = refs[:-4], refs[-4:]
    n_modes = rate_ref.shape[0]
    steps = p_ref.shape[0] - n_modes
    n_tok = SUBS * steps
    me = at_ref[0]
    rows = lax.broadcasted_iota(jnp.int32, (SUBS, LANES), 0)

    told[0] = jnp.zeros((PAYLOAD, LANES), f32)
    for n, ref in enumerate(told_refs):
        for k in range(2):
            told[1 + neighbour(me, n, k)] = ref[k].astype(f32)

    def first_products(j):
        taps = []
        for i in range(2):
            row = lambda slot, at: told[slot, pl.ds(at, 1), :]
            x = [row(j, LAST + 2 + 2 * i), row(j, LAST + 3 + 2 * i), row(1 + j, FIRST + 2 * i), row(1 + j, FIRST + 1 + 2 * i)]
            w = [sf_ref[k, i + 1][None] for k in range(3)]
            taps.append([w[0] * x[t + 2] + w[1] * x[t + 1] + w[2] * x[t] for t in range(2)])
        return [(taps[0][t] * taps[1][t]).astype(bf16).astype(f32) for t in range(2)]

    rates = rate_ref[...]
    late = [jnp.exp(-rates * (n_tok - 1 - t)) for t in range(2)]
    enter_all = jnp.zeros_like(rates)
    for j in range(2 * len(told_refs) - 1):
        p0, p1 = first_products(j)
        ended = told[1 + j, :n_modes, :] + late[0] * p0 + late[1] * p1
        gap = (jnp.maximum(me - 1 - j, 0) * n_tok).astype(f32)
        enter_all = enter_all + jnp.where(j < me, jnp.exp(-rates * gap), 0.0) * ended
    told[0, pl.ds(0, n_modes), :] = enter_all
    p_first = [jnp.broadcast_to(p, (SUBS, LANES)) for p in first_products(me)]

    fill(xs, x_ref.at[0], told[me, pl.ds(LAST, 2), :], steps)
    w = [jnp.broadcast_to(sf_ref[k, 0][None], (SUBS, LANES)) for k in range(3)]
    decay, gain, state0 = [], [], []
    for r in range(n_modes):
        rate = jnp.broadcast_to(rate_ref[pl.ds(r, 1), :], (SUBS, LANES))
        enter = jnp.broadcast_to(told[0, pl.ds(r, 1), :], (SUBS, LANES))
        decay.append(jnp.exp(-rate))
        gain.append(jnp.broadcast_to(res_ref[pl.ds(r, 1), :], (SUBS, LANES)))
        passed = (rows * steps).astype(f32)
        mine = jnp.exp(-rate * (passed - 1.0)) * p_first[0] + jnp.exp(-rate * (passed - 2.0)) * p_first[1]
        state0.append(p_ref[steps + r] + jnp.exp(-rate * passed) * enter + jnp.where(rows >= 1, mine, 0.0))

    def tap(at):
        return xs[pl.ds(PAD + at, SUBS, stride=steps + PAD), :]

    def body(t, carry, first=None):
        x1, x2, state = carry
        x0 = tap(t)
        gate = w[0] * x0 + w[1] * x1 + w[2] * x2
        p = p_ref[t]
        if first is not None:
            p = jnp.where(rows >= 1, p, first)
        state = tuple(a * s + p for a, s in zip(decay, state))
        parts = [c * s for c, s in zip(gain, state)]
        while len(parts) > 1:
            parts = [a + b for a, b in zip(parts[::2], parts[1::2])]
        ys[pl.ds(t, SUBS, stride=steps + PAD), :] = gate * parts[0]
        return (x0, x1, state)

    carry = (tap(-1), tap(-2), tuple(state0))
    carry = body(1, body(0, carry, p_first[0]), p_first[1])
    lax.fori_loop(2, steps, body, carry, unroll=6)
    for s in range(SUBS):
        out_ref[pl.ds(s * steps, steps), :] = ys[pl.ds(s * (steps + PAD), steps), :].astype(bf16)


def neighbour(me, n, k):
    return (me // 4 + k) % 2 * 4 + (me + 4 - n) % 4


def states(x, sf, rate):
    _, n_tok, width = x.shape
    modes = rate.shape[0]
    steps = n_tok // SUBS
    col = lambda g: (0, g)
    three = lambda g: (0, 0, g)
    return pl.pallas_call(
        state_kernel,
        grid=(width // LANES,),
        in_specs=[
            pl.BlockSpec((1, n_tok, LANES), lambda g: (1, 0, g)),
            pl.BlockSpec((1, n_tok, LANES), lambda g: (2, 0, g)),
            pl.BlockSpec((1, 16, LANES), lambda g: (0, n_tok // 16 - 1, g)),
            pl.BlockSpec((3, 3, LANES), three),
            pl.BlockSpec((modes, LANES), col),
        ],
        out_specs=[
            pl.BlockSpec((steps + modes, SUBS, LANES), three),
            pl.BlockSpec((PAYLOAD, LANES), col),
        ],
        out_shape=[
            jax.ShapeDtypeStruct((steps + modes, SUBS, width), f32),
            jax.ShapeDtypeStruct((PAYLOAD, width), bf16),
        ],
        scratch_shapes=[pltpu.VMEM((2, n_tok + SUBS * PAD, LANES), f32), pltpu.VMEM((PAYLOAD, LANES), f32)],
        compiler_params=pltpu.CompilerParams(vmem_limit_bytes=60 << 20),
        name="states",
    )(x, x, x, sf, rate)


def gated(at, x, sf, rate, res, p, told):
    _, n_tok, width = x.shape
    modes = rate.shape[0]
    steps = n_tok // SUBS
    col = lambda g: (0, g)
    three = lambda g: (0, 0, g)
    return pl.pallas_call(
        gate_kernel,
        grid=(width // LANES,),
        in_specs=[
            pl.BlockSpec(memory_space=pltpu.SMEM),
            pl.BlockSpec((1, n_tok, LANES), three),
            pl.BlockSpec((3, 3, LANES), three),
            pl.BlockSpec((modes, LANES), col),
            pl.BlockSpec((modes, LANES), col),
            pl.BlockSpec((steps + modes, SUBS, LANES), three),
        ]
        + [pl.BlockSpec((2, PAYLOAD, LANES), three)] * len(told),
        out_specs=pl.BlockSpec((n_tok, LANES), col),
        out_shape=jax.ShapeDtypeStruct((n_tok, width), bf16),
        scratch_shapes=[
            pltpu.VMEM((n_tok + SUBS * PAD, LANES), f32),
            pltpu.VMEM((n_tok + SUBS * PAD, LANES), f32),
            pltpu.VMEM((2 * len(told) + 1, PAYLOAD, LANES), f32),
        ],
        compiler_params=pltpu.CompilerParams(vmem_limit_bytes=52 << 20),
        name="gated",
    )(at, x, sf, rate, res, p, *told)


def spread(x, axis, target):
    pairs = [(i, target(i)) for i in range(lax.axis_size(axis))]
    return lax.ppermute(x, axis, [(i, j) for i, j in pairs if j is not None])


def to_core(x):
    return spread(x, "ch", lambda i: i ^ 1)


def to_far_z(x):
    return spread(x, "ch", lambda i: i ^ 2)


def to_y(x, by):
    return spread(x, "ch", lambda i: (i + 4 * by) % 16)


def to_x(x, by):
    return spread(x, "ctx", lambda i: i // 4 * 4 + (i + by) % 4)


def to_near_z(x):
    return spread(x, "ctx", lambda i: (i + 4) % 8)


def project_kernel(plan, n_added, cols_ref, g_ref, gp_ref, w_ref, wp_ref, *refs):
    added, refs = refs[:n_added], refs[n_added:]
    out_refs, (weights, sems) = refs[:-2], refs[-2:]
    depth = g_ref.shape[1]
    copies = []
    for k, (col, _) in enumerate(plan):
        at = pl.ds(pl.multiple_of(cols_ref[col] * depth, depth), depth)
        pair = [
            pltpu.make_async_copy(source.at[:, at], weights.at[k, j], sems.at[k, j])
            for j, source in enumerate((w_ref, wp_ref))
        ]
        for copy in pair:
            copy.start()
        copies.append(pair)
    for k, (_, pieces) in enumerate(plan):
        for copy in copies[k]:
            copy.wait()
        for first, count, out, slot, extra in pieces:
            rows = pl.ds(first, count)
            acc = jnp.dot(g_ref[rows, :], weights[k, 0], preferred_element_type=f32)
            acc = acc + jnp.dot(gp_ref[rows, :], weights[k, 1], preferred_element_type=f32)
            if extra is not None:
                acc = acc + added[extra[0]][extra[1]].astype(f32)
            out_refs[out][slot] = acc.astype(bf16)


def project(operands, plan, counts, added=(), limit=48):
    cols, g, gp, w, wp = operands
    depth = g.shape[1]
    slots = [0] * len(counts)
    laid = []
    for (dy, dz), pieces in plan:
        mine = []
        for first, out, *extra in pieces:
            mine.append((first, counts[out], out, slots[out], extra[0] if extra else None))
            slots[out] += 1
        laid.append((2 * dy + dz, mine))
    vmem = pl.BlockSpec(memory_space=pltpu.VMEM)
    anywhere = pl.BlockSpec(memory_space=pl.ANY)
    return pl.pallas_call(
        functools.partial(project_kernel, laid, len(added)),
        in_specs=[pl.BlockSpec(memory_space=pltpu.SMEM)] + [vmem] * 2 + [anywhere] * 2 + [vmem] * len(added),
        out_specs=[vmem] * len(counts),
        out_shape=[jax.ShapeDtypeStruct((n, count, depth), bf16) for n, count in zip(slots, counts)],
        scratch_shapes=[
            pltpu.VMEM((len(plan), 2, depth, depth), bf16),
            pltpu.SemaphoreType.DMA((len(plan), 2)),
        ],
        compiler_params=pltpu.CompilerParams(vmem_limit_bytes=limit << 20),
        name="project",
    )(cols, g, gp, w, wp, *added)


def total(*parts):
    return sum(p.astype(f32) for p in parts).astype(bf16)


Z_TOK = 384


def per_device(features, short_filter, decay_rate, residues, out_weight):
    n_tok = features.shape[0]
    x = features.transpose(1, 0, 2)
    weight_pair = to_core(out_weight)
    me = lax.axis_index("ch")
    steps = jnp.arange(8, dtype=jnp.int32)
    cols = (me // 4 + steps // 2) % 4 * 4 + (me // 2 + steps) % 2 * 2 + me % 2
    product, told = states(x, short_filter, decay_rate)
    told = jnp.stack([told, to_near_z(told)])
    heard = [told] + [to_x(told, n) for n in (1, 2, 3)]
    at = lax.axis_index("ctx").astype(jnp.int32)[None]
    mine = gated(at, x, short_filter, decay_rate, residues, product, heard)
    operands = (cols, mine, to_core(mine), out_weight, weight_pair)
    n_y = n_tok - Z_TOK
    a, b, z = 0, n_y // 2, n_y

    up2, down2 = project(operands, [((2, dz), [(a, 0), (b, 1)]) for dz in (1, 0)], [b, b], limit=48)
    up2, down2 = to_y(up2, 1), to_y(down2, -1)
    (far,) = project(operands, [((dy, 1), [(z, 0)]) for dy in (0, 1, 2, 3)], [Z_TOK])
    far = to_far_z(far)
    up, down, up_more, down_more, keep_a, keep_b = project(
        operands,
        [((1, 1), [(b, 0), (a, 2)]), ((3, 1), [(a, 1), (b, 3)]), ((0, 1), [(a, 4), (b, 5)])],
        [b] * 6,
    )
    up, down = to_y(up[0], 1), to_y(down[0], -1)
    up_more, down_more = to_y(total(up_more[0], up2[0]), 1), to_y(total(down_more[0], down2[0]), -1)
    rise, fall, stay_a, stay_b = project(
        operands,
        [((1, 0), [(b, 0), (a, 0, (0, 1))]), ((3, 0), [(a, 1), (b, 1, (1, 1))]), ((0, 0), [(a, 2), (b, 3)])],
        [b] * 4,
        [up2, down2],
    )
    last = (cols, lax.optimization_barrier((mine, stay_a, up, down))[0]) + operands[2:]
    (near,) = project(last, [((dy, 0), [(z, 0)]) for dy in (2, 3, 1, 0)], [Z_TOK])
    half = Z_TOK // 2
    s2a, s2b = total(near[0, :half], far[2, :half]), total(near[0, half:], far[2, half:])
    rise, fall = to_y(rise, 1), to_y(fall, -1)
    s2a, s2b = to_y(s2a, 1), to_y(s2b, -1)
    up, down, up_more, down_more = lax.optimization_barrier((up, down, up_more, down_more))
    over = to_far_z(jnp.stack([total(keep_a[0], up_more, down), total(keep_b[0], up, down_more)]))
    rise, fall = lax.optimization_barrier((rise, fall))
    done_a = total(stay_a[0], rise[1], fall[0], over[0])
    done_b = total(stay_b[0], rise[0], fall[1], over[1])

    s1 = total(near[2], far[1], jnp.pad(s2a, ((0, half), (0, 0))))
    s3 = total(near[1], far[3], jnp.pad(s2b, ((half, 0), (0, 0))))
    s1, s3 = to_y(s1, 1), to_y(s3, -1)
    return jnp.concatenate([done_a, done_b, total(near[3], far[0], s1, s3)])


def solution(mesh):
    placed = (P("ctx", None, "ch"), P(None, None, "ch"), P(None, "ch"), P(None, "ch"), P("ch", None))
    return jax.shard_map(per_device, mesh=mesh, in_specs=placed, out_specs=P("ctx", "ch"), check_vma=False)
```
